512 devices in a mesh: grp: 16 (over y, x), dev: 32 (over z, core).
Axes of the slice: x: 4, y: 4, z: 16, core: 2. Of those that a mesh axis runs over, the one named last changes fastest.
Arguments:
- points: float32 [3, 524288], P(None, ('grp', 'dev')), may hold values from 0 to 2
- charges: float32 [16, 524288], P(None, ('grp', 'dev')), may hold values from -6 to 6
- morton: int32 [524288], P(('grp', 'dev')), may hold values from 0 to 1023, as said below
- neighbours: int32 [2048, 8], P(('grp', 'dev')), may hold values from 0 to 2047, as said below
- counts: int32 [2048], P(('grp', 'dev')), may hold values from 1 to 8
- skel_leaf: float32 [3, 524288], P(None, ('grp', 'dev')), may hold values from 0 to 2
- skel_block: float32 [3, 131072], P(None, ('grp', 'dev')), may hold values from 0 to 2
- skel_group: float32 [3, 4096], replicated, may hold values from 0 to 2
Outputs:
- potential: float32 [16, 524288], P(None, ('grp', 'dev'))
The draws below stay inside these ranges and needn't reach their ends.
Inputs may be any that keep to these rules, and one draw needn't show every extreme that they name: `morton`: each aligned run of 1024 entries is a permutation of 0 to 1023. `neighbours`: entry [q, k] is a leaf other than q, at most 4 leaves away from q; only slots k < counts[q] are used.
All inputs are finite; a program needn't handle non-finite values.
Results may differ from the reference program's by a relative error of at most 0.0003.
Values sent between devices are 32-bit elements; how exact they have to be, the bound alone decides.
No kernel may reach another device: no remote copies, remote signals or barrier semaphores. Data moves between devices by JAX's collectives and lax.ppermute only.
A program may use at most 64 MiB of HBM per device.

```python
import math
import jax
import jax.numpy as jnp
from jax import lax

P_SIZE = 256
R = 256
NBR = 8
LEAF_DEV = 4
NRHS = 16
GROUPS = 16
BLOCKS_GRP = 32
BLOCKS = 512
LEAVES = 2048
NPTS = 524288


def neighbour_tables(key):
    leaf_total = NPTS // P_SIZE
    subkeys = jax.random.split(jax.random.fold_in(key, 11), 4)
    offsets = jnp.concatenate([jnp.arange(1, LEAF_DEV + 1), -jnp.arange(1, LEAF_DEV + 1)]).astype(jnp.int32)
    orders = jax.vmap(lambda leaf_key: jax.random.permutation(leaf_key, 2 * LEAF_DEV))(jax.random.split(subkeys[0], leaf_total))
    chosen = offsets[orders[:, :NBR]]
    own_leaf = jnp.arange(leaf_total, dtype=jnp.int32)[:, None]
    forward = own_leaf + chosen
    inside = (forward >= 0) & (forward < leaf_total)
    neighbour_ids = jnp.where(inside, forward, own_leaf - chosen).astype(jnp.int32)
    neighbour_ids = neighbour_ids.at[leaf_total - 2, 0].set(leaf_total - 1).at[1, 0].set(0)
    amounts = jax.random.randint(subkeys[1], (leaf_total,), 1, NBR + 1)
    fullest = jax.random.randint(subkeys[2], (), 0, leaf_total)
    emptiest = (fullest + 1 + jax.random.randint(subkeys[3], (), 0, leaf_total - 1)) % leaf_total
    amounts = amounts.at[fullest].set(NBR).at[emptiest].set(1)
    return (neighbour_ids.astype(jnp.int32), amounts.astype(jnp.int32))


def draw_neighbours(key, part):
    return neighbour_tables(key)[0]


def draw_counts(key, part):
    return neighbour_tables(key)[1]


def morton_order(key):
    block_pts = LEAF_DEV * P_SIZE
    subkeys = jax.random.split(jax.random.fold_in(key, 5), NPTS // block_pts)
    orders = jax.vmap(lambda block_key: jax.random.permutation(block_key, block_pts))(subkeys)
    return orders.reshape(-1).astype(jnp.int32)


def draw_morton(key, part):
    return morton_order(key)


def extent_of_cloud():
    return 2.0


def draw_points(key, part):
    leaf_total = NPTS // P_SIZE
    leaf_half = 0.6
    extent = extent_of_cloud()
    subkeys = jax.random.split(jax.random.fold_in(key, 23), 4)
    group_pos = jax.random.uniform(subkeys[0], (3, GROUPS), jnp.float32)
    block_pos = jax.random.uniform(subkeys[1], (3, BLOCKS), jnp.float32)
    leaf_pos = jax.random.uniform(subkeys[2], (3, leaf_total), jnp.float32)
    blended = 0.5 * jnp.repeat(group_pos, BLOCKS_GRP * LEAF_DEV, axis=1) + 0.3 * jnp.repeat(block_pos, LEAF_DEV, axis=1) + 0.2 * leaf_pos
    centres = leaf_half + (extent - 2.0 * leaf_half) * blended
    offsets = jax.random.uniform(subkeys[3], (3, leaf_total, P_SIZE), jnp.float32, -1.0, 1.0)
    sorted_pts = (centres[:, :, None] + leaf_half * offsets).reshape(3, NPTS)
    block_pts = LEAF_DEV * P_SIZE
    block_start = jnp.arange(NPTS, dtype=jnp.int32) // block_pts * block_pts
    source_idx = (block_start + morton_order(key)).astype(jnp.int32)
    return jnp.zeros((3, NPTS), jnp.float32).at[:, source_idx].set(sorted_pts)


def draw_skel_leaf(key, part):
    fraction = jax.random.uniform(jax.random.fold_in(key, 31), (3, LEAVES * R), jnp.float32)
    return extent_of_cloud() * fraction


def draw_skel_block(key, part):
    fraction = jax.random.uniform(jax.random.fold_in(key, 37), (3, BLOCKS * R), jnp.float32)
    return extent_of_cloud() * fraction


def draw_skel_group(key, part):
    fraction = jax.random.uniform(jax.random.fold_in(key, 41), (3, GROUPS * R), jnp.float32)
    return extent_of_cloud() * fraction


def shard_levels(key, shape, shards, smallest, largest):
    level, own = 1.0, jax.random.fold_in(key, 6)
    for dim, parts in shards:
        steps = jnp.exp(jax.random.uniform(jax.random.fold_in(own, dim), (parts,), jnp.float32, smallest / len(shards), largest / len(shards)))
        level = level * jnp.repeat(steps, shape[dim] // parts).reshape([-1 if axis == dim else 1 for axis in range(len(shape))])
    return level


def noise(stream_key, shape, scale, most, cuts=(), held_as=jnp.bfloat16):
    array = scale * jax.random.normal(stream_key, shape, jnp.float32)
    if cuts:
        array = array * shard_levels(stream_key, shape, cuts, -0.22, 0.18)
    return jnp.clip(array, -most, most).astype(held_as)


def setup_inputs(seed: int = 0) -> dict:
    arg_keys = jax.random.split(jax.random.key(seed), 9)
    points = draw_points(jax.random.fold_in(arg_keys[8], 71), 0)
    charges = noise(arg_keys[1], (NRHS, NPTS), 1.0, 6.0, ((1, 512),), jnp.float32)
    morton = draw_morton(jax.random.fold_in(arg_keys[8], 71), 0)
    neighbours = draw_neighbours(jax.random.fold_in(arg_keys[8], 71), 0)
    counts = draw_counts(jax.random.fold_in(arg_keys[8], 71), 0)
    skel_leaf = draw_skel_leaf(jax.random.fold_in(arg_keys[8], 71), 0)
    skel_block = draw_skel_block(jax.random.fold_in(arg_keys[8], 71), 0)
    skel_group = draw_skel_group(jax.random.fold_in(arg_keys[8], 71), 0)
    return {"points": points, "charges": charges, "morton": morton, "neighbours": neighbours, "counts": counts, "skel_leaf": skel_leaf, "skel_block": skel_block, "skel_group": skel_group}


width_sq = 0.1
gain_factor = 5.0

def kernel_tile(source, target):
    distance = (source[0][:, None] - target[0][None, :]) ** 2
    distance = distance + (source[1][:, None] - target[1][None, :]) ** 2
    distance = distance + (source[2][:, None] - target[2][None, :]) ** 2
    return jnp.exp(-distance / width_sq)

def translate(values, source, target, term_count):
    product = jnp.dot(values, kernel_tile(source, target), precision=lax.Precision.HIGHEST, preferred_element_type=jnp.float32)
    return gain_factor / math.sqrt(term_count) * product

def by_leaf(matrix, leading, number, length):
    return matrix.reshape(leading, number, length).transpose(1, 0, 2)

def reference(points, charges, morton, neighbours, counts, skel_leaf, skel_block, skel_group):
    block_pts = LEAF_DEV * P_SIZE
    block_start = jnp.arange(NPTS, dtype=jnp.int32) // block_pts * block_pts
    source_idx = (block_start + morton).astype(jnp.int32)
    sorted_pts = jnp.take(points, source_idx, axis=1)
    sorted_chg = jnp.take(charges, source_idx, axis=1)
    leaf_pts = by_leaf(sorted_pts, 3, LEAVES, P_SIZE)
    leaf_chg = by_leaf(sorted_chg, NRHS, LEAVES, P_SIZE)
    leaf_skel = by_leaf(skel_leaf, 3, LEAVES, R)
    block_skel = by_leaf(skel_block, 3, BLOCKS, R)
    group_skel = by_leaf(skel_group, 3, GROUPS, R)
    leaf_weights = lax.map(lambda inputs: translate(inputs[0], inputs[1], inputs[2], P_SIZE), (leaf_chg, leaf_pts, leaf_skel))
    owner_block = jnp.arange(LEAVES, dtype=jnp.int32) // LEAF_DEV
    lifted = lax.map(lambda inputs: translate(inputs[0], inputs[1], inputs[2], LEAF_DEV * R), (leaf_weights, leaf_skel, block_skel[owner_block]))
    block_weights = lifted.reshape(BLOCKS, LEAF_DEV, NRHS, R).sum(axis=1)
    parent = jnp.arange(BLOCKS, dtype=jnp.int32) // BLOCKS_GRP
    raised = lax.map(lambda inputs: translate(inputs[0], inputs[1], inputs[2], BLOCKS_GRP * R), (block_weights, block_skel, group_skel[parent]))
    group_weights = raised.reshape(GROUPS, BLOCKS_GRP, NRHS, R).sum(axis=1)

    def group_far(target_id):
        keep_mask = (jnp.arange(GROUPS, dtype=jnp.int32) != target_id).astype(jnp.float32)
        masked = (group_weights * keep_mask[:, None, None]).transpose(1, 0, 2).reshape(NRHS, GROUPS * R)
        return translate(masked, skel_group, group_skel[target_id], (GROUPS - 1) * R)
    group_field = lax.map(group_far, jnp.arange(GROUPS, dtype=jnp.int32))

    def block_far(block_id):
        group_id = block_id // BLOCKS_GRP
        first_block = (group_id * BLOCKS_GRP).astype(jnp.int32)
        members = lax.dynamic_slice_in_dim(block_weights, first_block, BLOCKS_GRP, 0)
        keep_mask = (jnp.arange(BLOCKS_GRP, dtype=jnp.int32) + first_block != block_id).astype(jnp.float32)
        masked = (members * keep_mask[:, None, None]).transpose(1, 0, 2).reshape(NRHS, BLOCKS_GRP * R)
        sources = lax.dynamic_slice_in_dim(skel_block, (first_block * R).astype(jnp.int32), BLOCKS_GRP * R, 1)
        target = block_skel[block_id]
        peer_sum = translate(masked, sources, target, (BLOCKS_GRP - 1) * R)
        return peer_sum + translate(group_field[group_id], group_skel[group_id], target, R)
    block_field = lax.map(block_far, jnp.arange(BLOCKS, dtype=jnp.int32))
    leaf_field = lax.map(lambda inputs: translate(inputs[0], inputs[1], inputs[2], R), (block_field[owner_block], block_skel[owner_block], leaf_skel))

    def near_leaf(leaf_id):
        own_pts = leaf_pts[leaf_id]
        direct = translate(leaf_chg[leaf_id], own_pts, own_pts, P_SIZE)

        def one_slot(slot_index, running):
            neighbour = neighbours[leaf_id, slot_index]
            tile_term = translate(leaf_chg[neighbour], leaf_pts[neighbour], own_pts, P_SIZE)
            return running + jnp.where(slot_index < counts[leaf_id], tile_term, jnp.zeros_like(tile_term))
        direct = lax.fori_loop(0, NBR, one_slot, direct)
        return direct + translate(leaf_field[leaf_id], leaf_skel[leaf_id], own_pts, R)
    potential = lax.map(near_leaf, jnp.arange(LEAVES, dtype=jnp.int32))
    return potential.transpose(1, 0, 2).reshape(NRHS, NPTS)
```

```python
import functools
import math

import jax
import jax.numpy as jnp
from jax import lax
from jax.experimental import pallas as pl
from jax.experimental.pallas import tpu as pltpu
from jax.sharding import PartitionSpec as P

f32 = jnp.float32
bf16 = jnp.bfloat16
width_sq = 0.1
gain_factor = 5.0
coord_scale = math.sqrt(math.log2(math.e) / width_sq)
VEC = 16
ROWS = 24
T = 256
LEAVES_DEV = 4


def dg(a, b, ca, cb):
    return lax.dot_general(a, b, (((ca,), (cb,)), ((), ())), preferred_element_type=f32)


def split2(v):
    h = v.astype(bf16)
    return h, (v - h.astype(f32)).astype(bf16)


def split3(v):
    a = v.astype(bf16).astype(f32)
    r = v - a
    b = r.astype(bf16).astype(f32)
    return a, b, r - b


def centred(x3):
    x = (x3 - 1.0) * coord_scale
    n = jnp.sum(x * x, axis=0, keepdims=True)
    return x, n, jnp.ones_like(n), jnp.zeros((3,) + n.shape[1:], f32)


def feat_src(x3):
    x, n, o, z = centred(x3)
    a, b, c = split3(jnp.concatenate([x, n, o, z], axis=0))
    return jnp.concatenate([a, a, a, b, b, c], axis=0).astype(bf16)


def feat_tgt(x3):
    x, n, o, z = centred(x3)
    a, b, c = split3(jnp.concatenate([2.0 * x, -o, -n, z], axis=0))
    return jnp.concatenate([a, b, c, a, b, a], axis=0).astype(bf16)


def tile(fs, ft):
    return split2(jnp.exp2(dg(fs, ft, 0, 0)))


def stack2(v):
    h, l = split2(v)
    return jnp.concatenate([h, l], axis=0)


def times(vv, kt):
    kh, kl = kt
    r = dg(vv, kh, 1, 0)
    return r[:VEC] + r[VEC:] + dg(vv[:VEC], kl, 1, 0)


def gain(count):
    return gain_factor / math.sqrt(count)


def up_kernel(pts_ref, chg_ref, mor_ref, skl_ref, skb_ref, srt_ref, bws_ref):
    n = chg_ref.shape[1]
    rows = jnp.concatenate([chg_ref[...], pts_ref[...], jnp.zeros((5, n), f32)], axis=0)
    a, b, c = split3(rows)
    parts = jnp.concatenate([a, b, c], axis=0).astype(bf16)
    for i in range(n // T):
        col = slice(i * T, (i + 1) * T)
        hot = (lax.broadcasted_iota(jnp.int32, (n, T), 0) == mor_ref[:, col]).astype(f32).astype(bf16)
        s = dg(parts, hot, 1, 0)
        srt_ref[:, col] = s[:ROWS] + s[ROWS : 2 * ROWS] + s[2 * ROWS :]
    ft_block = feat_tgt(skb_ref[...])
    total = jnp.zeros((VEC, T), f32)
    for q in range(LEAVES_DEV):
        col = slice(q * T, (q + 1) * T)
        skel = skl_ref[:, col]
        lw = times(stack2(srt_ref[:VEC, col]), tile(feat_src(srt_ref[VEC : VEC + 3, col]), feat_tgt(skel)))
        total = total + times(stack2(gain(T) * lw), tile(feat_src(skel), ft_block))
    bws_ref[:VEC, :] = gain(LEAVES_DEV * T) * total
    bws_ref[VEC:, :] = jnp.concatenate([skb_ref[...], jnp.zeros((5, T), f32)], axis=0)


def group_kernel(id_ref, all_ref, skg_ref, gw_ref):
    n = all_ref.shape[0]
    own = pl.ds(pl.multiple_of(id_ref[0] * T, T), T)
    ft = feat_tgt(skg_ref[:, own])
    total = jnp.zeros((VEC, T), f32)
    for c in range(n):
        total = total + times(stack2(all_ref[c, :VEC, :]), tile(feat_src(all_ref[c, VEC : VEC + 3, :]), ft))
    total = gain(n * T) * total
    for g in range(gw_ref.shape[0]):
        gw_ref[g] = total


def near_kernel(id_ref, nbr_ref, cnt_ref, left_ref, mid_ref, right_ref, all_ref, skb_ref, near_ref, peer_ref):
    member = id_ref[1]
    n = all_ref.shape[0]
    ft = feat_tgt(skb_ref[...])
    total = jnp.zeros((VEC, T), f32)
    for c in range(n):
        keep = jnp.where(member == c, 0.0, 1.0)
        total = total + times(stack2(keep * all_ref[c, :VEC, :]), tile(feat_src(all_ref[c, VEC : VEC + 3, :]), ft))
    peer_ref[...] = gain((n - 1) * T) * total
    first = id_ref[2]
    fts = [feat_tgt(mid_ref[VEC : VEC + 3, q * T : (q + 1) * T]) for q in range(LEAVES_DEV)]
    acc = [jnp.zeros((VEC, T), f32) for _ in range(LEAVES_DEV)]
    for s in range(-LEAVES_DEV, 2 * LEAVES_DEV):
        ref = (left_ref, mid_ref, right_ref)[s // LEAVES_DEV + 1]
        j = s % LEAVES_DEV
        v = ref[:VEC, j * T : (j + 1) * T]
        fs = feat_src(ref[VEC : VEC + 3, j * T : (j + 1) * T])
        for q in range(LEAVES_DEV):
            if abs(s - q) > LEAVES_DEV:
                continue
            uses = jnp.int32(1 if s == q else 0)
            for k in range(nbr_ref.shape[1]):
                hit = jnp.logical_and(nbr_ref[q, k] == first + s, cnt_ref[q] > k)
                uses = uses + hit.astype(jnp.int32)
            acc[q] = acc[q] + times(stack2(uses.astype(f32) * v), tile(fs, fts[q]))
    for q in range(LEAVES_DEV):
        near_ref[:, q * T : (q + 1) * T] = gain(T) * acc[q]


def down_kernel(id_ref, gws_ref, skg_ref, peer_ref, skb_ref, skl_ref, mid_ref, near_ref, out_ref):
    group = id_ref[0]
    n = gws_ref.shape[0]
    own = skg_ref[:, pl.ds(pl.multiple_of(group * T, T), T)]
    ft_own = feat_tgt(own)
    total = jnp.zeros((VEC, T), f32)
    for g in range(n):
        keep = jnp.where(group == g, 0.0, 1.0)
        total = total + times(stack2(keep * gws_ref[g]), tile(feat_src(skg_ref[:, g * T : (g + 1) * T]), ft_own))
    field = gain((n - 1) * T) * total
    field = peer_ref[...] + gain(T) * times(stack2(field), tile(feat_src(own), feat_tgt(skb_ref[...])))
    vv = stack2(field)
    fs_block = feat_src(skb_ref[...])
    for q in range(LEAVES_DEV):
        col = slice(q * T, (q + 1) * T)
        lf = gain(T) * times(vv, tile(fs_block, feat_tgt(skl_ref[:, col])))
        far = times(stack2(lf), tile(feat_src(skl_ref[:, col]), feat_tgt(mid_ref[VEC : VEC + 3, col])))
        out_ref[:, col] = near_ref[:, col] + gain(T) * far


VM = pl.BlockSpec(memory_space=pltpu.VMEM)
SM = pl.BlockSpec(memory_space=pltpu.SMEM)


def shape(*dims):
    return jax.ShapeDtypeStruct(dims, f32)


def body(points, charges, morton, neighbours, counts, skel_leaf, skel_block, skel_group):
    n_groups = lax.axis_size("grp")
    n_blocks = lax.axis_size("dev")
    n = points.shape[1]
    group_id = lax.axis_index("grp")
    member_id = lax.axis_index("dev")
    block_id = group_id * n_blocks + member_id
    ids = jnp.stack([group_id, member_id, block_id * LEAVES_DEV]).astype(jnp.int32)
    srt, bws = pl.pallas_call(
        up_kernel,
        out_shape=(shape(ROWS, n), shape(ROWS, T)),
        in_specs=[VM] * 5,
        out_specs=(VM, VM),
        name="up",
    )(points, charges, morton.reshape(1, n), skel_leaf, skel_block)
    whole = n_groups * n_blocks
    left = lax.ppermute(srt, ("grp", "dev"), [(i, i + 1) for i in range(whole - 1)])
    right = lax.ppermute(srt, ("grp", "dev"), [(i + 1, i) for i in range(whole - 1)])
    all_bws = lax.all_gather(bws, "dev", axis=0, tiled=False)
    gw = pl.pallas_call(
        group_kernel,
        out_shape=shape(n_groups, VEC, T),
        in_specs=[SM, VM, VM],
        out_specs=VM,
        name="group",
    )(ids, all_bws, skel_group)
    gws = lax.all_to_all(gw, "grp", 0, 0, tiled=False)
    near, peer = pl.pallas_call(
        near_kernel,
        out_shape=(shape(VEC, n), shape(VEC, T)),
        in_specs=[SM, SM, SM, VM, VM, VM, VM, VM],
        out_specs=(VM, VM),
        name="near",
    )(ids, neighbours, counts, left, srt, right, all_bws, skel_block)
    return pl.pallas_call(
        down_kernel,
        out_shape=shape(VEC, n),
        in_specs=[SM] + [VM] * 7,
        out_specs=VM,
        name="down",
    )(ids, gws, skel_group, peer, skel_block, skel_leaf, srt, near)


def solution(mesh):
    return jax.shard_map(
        body,
        mesh=mesh,
        in_specs=(
            P(None, ("grp", "dev")),
            P(None, ("grp", "dev")),
            P(("grp", "dev")),
            P(("grp", "dev"), None),
            P(("grp", "dev")),
            P(None, ("grp", "dev")),
            P(None, ("grp", "dev")),
            P(),
        ),
        out_specs=P(None, ("grp", "dev")),
        check_vma=False,
    )
```

```python
import math

import jax
import jax.numpy as jnp
from jax import lax
from jax.experimental import pallas as pl
from jax.experimental.pallas import tpu as pltpu
from jax.sharding import Mesh, PartitionSpec as P

f32 = jnp.float32
bf16 = jnp.bfloat16
width_sq = 0.1
gain_factor = 5.0
coord_scale = math.sqrt(math.log2(math.e) / width_sq)
VEC = 16
ROWS = 24
T = 256
LEAVES_DEV = 4
PACK = 40
HALF = 128


def dg(a, b, ca, cb):
    return lax.dot_general(a, b, (((ca,), (cb,)), ((), ())), preferred_element_type=f32)


def split2(v):
    h = v.astype(bf16)
    return h, (v - h.astype(f32)).astype(bf16)


def split3(v):
    a = v.astype(bf16).astype(f32)
    r = v - a
    b = r.astype(bf16).astype(f32)
    return a, b, r - b


def centred(x3):
    x = (x3 - 1.0) * coord_scale
    n = jnp.sum(x * x, axis=0, keepdims=True)
    return x, n, jnp.ones_like(n), jnp.zeros((3,) + n.shape[1:], f32)


def feat_src(x3):
    x, n, o, z = centred(x3)
    a, b, c = split3(jnp.concatenate([x, n, o, z], axis=0))
    return jnp.concatenate([a, a, a, b, b, c], axis=0).astype(bf16)


def feat_tgt(x3):
    x, n, o, z = centred(x3)
    a, b, c = split3(jnp.concatenate([2.0 * x, -o, -n, z], axis=0))
    return jnp.concatenate([a, b, c, a, b, a], axis=0).astype(bf16)


def tile(fs, ft):
    return split2(jnp.exp2(dg(fs, ft, 0, 0)))


def stack2(v):
    h, l = split2(v)
    return jnp.concatenate([h, l], axis=0)


def times(vv, kt):
    kh, kl = kt
    r = dg(vv, kh, 1, 0)
    return r[:VEC] + r[VEC:] + dg(vv[:VEC], kl, 1, 0)


def gain(count):
    return gain_factor / math.sqrt(count)


def pack(w, skel):
    z = jnp.zeros((1, HALF), f32)
    return jnp.concatenate([w[:, :HALF], w[:, HALF:], skel[:, :HALF], z, skel[:, HALF:], z], axis=0)


def unpack(p):
    w = jnp.concatenate([p[:VEC], p[VEC : 2 * VEC]], axis=1)
    skel = jnp.concatenate([p[2 * VEC : 2 * VEC + 3], p[2 * VEC + 4 : 2 * VEC + 7]], axis=1)
    return w, skel


def up_kernel(pts_hbm, chg_hbm, mor_hbm, skl_hbm, skb_hbm, srt_ref, pack_ref, *scratch):
    pts_ref, chg_ref, mor_ref, skl_ref, skb_ref, sems = scratch
    copies = [
        pltpu.make_async_copy(src, dst, sems.at[i])
        for i, (src, dst) in enumerate(
            ((pts_hbm, pts_ref), (chg_hbm, chg_ref), (mor_hbm, mor_ref), (skl_hbm, skl_ref), (skb_hbm, skb_ref))
        )
    ]
    for c in copies:
        c.start()
    for c in copies:
        c.wait()
    n = chg_ref.shape[1]
    rows = jnp.concatenate([chg_ref[...], pts_ref[...], jnp.zeros((5, n), f32)], axis=0)
    a, b, c = split3(rows)
    parts = jnp.concatenate([a, b, c], axis=0).astype(bf16)
    for i in range(n // T):
        col = slice(i * T, (i + 1) * T)
        hot = (lax.broadcasted_iota(jnp.int32, (n, T), 0) == mor_ref[:, col]).astype(f32).astype(bf16)
        s = dg(parts, hot, 1, 0)
        srt_ref[:, col] = s[:ROWS] + s[ROWS : 2 * ROWS] + s[2 * ROWS :]
    srt_ref[VEC + 3 : VEC + 6, :T] = skb_ref[...]
    ft_block = feat_tgt(skb_ref[...])
    total = jnp.zeros((VEC, T), f32)
    for q in range(LEAVES_DEV):
        col = slice(q * T, (q + 1) * T)
        skel = skl_ref[:, col]
        lw = times(stack2(srt_ref[:VEC, col]), tile(feat_src(srt_ref[VEC : VEC + 3, col]), feat_tgt(skel)))
        total = total + times(stack2(gain(T) * lw), tile(feat_src(skel), ft_block))
    packed = pack(gain(LEAVES_DEV * T) * total, skb_ref[...])
    for z in range(pack_ref.shape[0]):
        pack_ref[z] = packed


def group_kernel(id_ref, all_ref, skg_ref, gw_ref):
    n = all_ref.shape[0]
    own = pl.ds(pl.multiple_of(id_ref[0] * T, T), T)
    ft = feat_tgt(skg_ref[:, own])
    total = jnp.zeros((VEC, T), f32)
    for c in range(n):
        w, skel = unpack(all_ref[c])
        total = total + times(stack2(w), tile(feat_src(skel), ft))
    total = gain(2 * n * T) * total
    for g in range(gw_ref.shape[0]):
        gw_ref[g] = total


def near_kernel(id_ref, nbr_ref, cnt_ref, left_ref, mid_ref, right_ref, near_ref):
    first = id_ref[3]
    fts = [feat_tgt(mid_ref[VEC : VEC + 3, q * T : (q + 1) * T]) for q in range(LEAVES_DEV)]
    acc = [jnp.zeros((VEC, T), f32) for _ in range(LEAVES_DEV)]
    for s in range(-LEAVES_DEV, 2 * LEAVES_DEV):
        ref = (left_ref, mid_ref, right_ref)[s // LEAVES_DEV + 1]
        j = s % LEAVES_DEV
        v = ref[:VEC, j * T : (j + 1) * T]
        fs = feat_src(ref[VEC : VEC + 3, j * T : (j + 1) * T])
        for q in range(LEAVES_DEV):
            if abs(s - q) > LEAVES_DEV:
                continue
            uses = jnp.int32(1 if s == q else 0)
            for k in range(nbr_ref.shape[1]):
                hit = jnp.logical_and(nbr_ref[q, k] == first + s, cnt_ref[q] > k)
                uses = uses + hit.astype(jnp.int32)
            acc[q] = acc[q] + times(stack2(uses.astype(f32) * v), tile(fs, fts[q]))
    for q in range(LEAVES_DEV):
        near_ref[:, q * T : (q + 1) * T] = gain(T) * acc[q]


def sibling(core, left_ref, right_ref):
    rows = slice(VEC + 3, VEC + 6)
    return jnp.where(core == 0, right_ref[rows, :T], left_ref[rows, :T])


def peer_kernel(id_ref, all_ref, skb_ref, left_ref, right_ref, peer_ref):
    n = all_ref.shape[0]
    ft_own = feat_tgt(skb_ref[...])
    ft_sib = feat_tgt(sibling(id_ref[2], left_ref, right_ref))
    own = jnp.zeros((VEC, T), f32)
    sib = jnp.zeros((VEC, T), f32)
    for c in range(n):
        w, skel = unpack(all_ref[c])
        fs = feat_src(skel)
        keep = jnp.where(id_ref[1] == c, 0.0, 1.0)
        own = own + times(stack2(keep * w), tile(fs, ft_own))
        sib = sib + times(stack2(w), tile(fs, ft_sib))
    peer_ref[0] = gain((2 * n - 1) * T) * own
    peer_ref[1] = gain((2 * n - 1) * T) * sib


def field_kernel(id_ref, gws_ref, skg_ref, peer_ref, skb_ref, left_ref, right_ref, own_ref, sib_ref):
    group = id_ref[0]
    n = gws_ref.shape[0]
    own = skg_ref[:, pl.ds(pl.multiple_of(group * T, T), T)]
    ft_own = feat_tgt(own)
    total = jnp.zeros((VEC, T), f32)
    for g in range(n):
        keep = jnp.where(group == g, 0.0, 1.0)
        total = total + times(stack2(keep * gws_ref[g]), tile(feat_src(skg_ref[:, g * T : (g + 1) * T]), ft_own))
    vv = stack2(gain((n - 1) * T) * total)
    fs = feat_src(own)
    own_ref[...] = peer_ref[0] + gain(T) * times(vv, tile(fs, feat_tgt(skb_ref[...])))
    sib_ref[...] = peer_ref[1] + gain(T) * times(vv, tile(fs, feat_tgt(sibling(id_ref[2], left_ref, right_ref))))


def down_kernel(id_ref, own_ref, both_ref, skb_ref, skl_ref, mid_ref, near_ref, out_ref):
    field = own_ref[...] + both_ref[1 - id_ref[2]]
    vv = stack2(field)
    fs_block = feat_src(skb_ref[...])
    for q in range(LEAVES_DEV):
        col = slice(q * T, (q + 1) * T)
        lf = gain(T) * times(vv, tile(fs_block, feat_tgt(skl_ref[:, col])))
        far = times(stack2(lf), tile(feat_src(skl_ref[:, col]), feat_tgt(mid_ref[VEC : VEC + 3, col])))
        out_ref[:, col] = near_ref[:, col] + gain(T) * far


VM = pl.BlockSpec(memory_space=pltpu.VMEM)
SM = pl.BlockSpec(memory_space=pltpu.SMEM)


def shape(*dims):
    return jax.ShapeDtypeStruct(dims, f32)


def kernel(fn, name, out, scalars, arrays):
    return pl.pallas_call(
        fn,
        out_shape=out,
        in_specs=[SM] * scalars + [VM] * arrays,
        out_specs=jax.tree.map(lambda _: VM, out),
        compiler_params=pltpu.CompilerParams(vmem_limit_bytes=24 << 20),
        name=name,
    )


def body(points, charges, morton, neighbours, counts, skel_leaf, skel_block, skel_group):
    n_groups = lax.axis_size("grp")
    n_z = lax.axis_size("z")
    n = points.shape[1]
    group_id = lax.axis_index("grp")
    z_id = lax.axis_index("z")
    core_id = lax.axis_index("core")
    block_id = (group_id * n_z + z_id) * 2 + core_id
    ids = jnp.stack([group_id, z_id, core_id, block_id * LEAVES_DEV]).astype(jnp.int32)
    inputs = (points, charges, morton.reshape(1, n), skel_leaf, skel_block)
    srt, packed = pl.pallas_call(
        up_kernel,
        out_shape=(shape(ROWS, n), shape(n_z, PACK, HALF)),
        in_specs=[pl.BlockSpec(memory_space=pltpu.HBM)] * 5,
        out_specs=(VM, VM),
        scratch_shapes=[pltpu.VMEM(x.shape, x.dtype) for x in inputs] + [pltpu.SemaphoreType.DMA((5,))],
        compiler_params=pltpu.CompilerParams(vmem_limit_bytes=60 << 20),
        name="up",
    )(*inputs)
    all_z = lax.all_to_all(packed, "z", 0, 0, tiled=False)
    whole = n_groups * n_z * 2
    axes = ("grp", "z", "core")
    left = lax.ppermute(srt, axes, [(i, i + 1) for i in range(whole - 1)])
    right = lax.ppermute(srt, axes, [(i + 1, i) for i in range(whole - 1)])
    near = kernel(near_kernel, "near", shape(VEC, n), 3, 3)(ids, neighbours, counts, left, srt, right)
    all_z, near = lax.optimization_barrier((all_z, near))
    gw = kernel(group_kernel, "group", shape(n_groups, VEC, T), 1, 2)(ids, all_z, skel_group)
    gws = lax.all_to_all(gw, "grp", 0, 0, tiled=False)
    peer = kernel(peer_kernel, "peer", shape(2, VEC, T), 1, 4)(ids, all_z, skel_block, left, right)
    own, sib = kernel(field_kernel, "field", (shape(VEC, T), shape(VEC, T)), 1, 6)(
        ids, gws, skel_group, peer, skel_block, left, right
    )
    both = lax.all_gather(sib, "core", axis=0, tiled=False)
    return kernel(down_kernel, "down", shape(VEC, n), 1, 6)(ids, own, both, skel_block, skel_leaf, srt, near)


def solution(mesh):
    fine = Mesh(mesh.devices.reshape(mesh.shape["grp"], mesh.shape["dev"] // 2, 2), ("grp", "z", "core"))
    all_axes = ("grp", "z", "core")
    return jax.shard_map(
        body,
        mesh=fine,
        in_specs=(
            P(None, all_axes),
            P(None, all_axes),
            P(all_axes),
            P(all_axes, None),
            P(all_axes),
            P(None, all_axes),
            P(None, all_axes),
            P(),
        ),
        out_specs=P(None, all_axes),
        check_vma=False,
    )
```

```python
import math

import jax
import jax.numpy as jnp
from jax import lax
from jax.experimental import pallas as pl
from jax.experimental.pallas import tpu as pltpu
from jax.sharding import Mesh, PartitionSpec as P

f32 = jnp.float32
bf16 = jnp.bfloat16
width_sq = 0.1
gain_factor = 5.0
coord_scale = math.sqrt(math.log2(math.e) / width_sq)
VEC = 16
ROWS = 24
T = 256
LEAVES_DEV = 4
PACK = 40
HALF = 128


def dg(a, b, ca, cb):
    return lax.dot_general(a, b, (((ca,), (cb,)), ((), ())), preferred_element_type=f32)


def split2(v):
    h = v.astype(bf16)
    return h, (v - h.astype(f32)).astype(bf16)


def split3(v):
    a = v.astype(bf16).astype(f32)
    r = v - a
    b = r.astype(bf16).astype(f32)
    return a, b, r - b


def centred(x3):
    x = (x3 - 1.0) * coord_scale
    n = jnp.sum(x * x, axis=0, keepdims=True)
    return x, n, jnp.ones_like(n), jnp.zeros((3,) + n.shape[1:], f32)


def feat_src(x3):
    x, n, o, z = centred(x3)
    a, b, c = split3(jnp.concatenate([x, n, o, z], axis=0))
    return jnp.concatenate([a, a, a, b, b, c], axis=0).astype(bf16)


def feat_tgt(x3):
    x, n, o, z = centred(x3)
    a, b, c = split3(jnp.concatenate([2.0 * x, -o, -n, z], axis=0))
    return jnp.concatenate([a, b, c, a, b, a], axis=0).astype(bf16)


def tile(fs, ft):
    return split2(jnp.exp2(dg(fs, ft, 0, 0)))


def stack2(v):
    h, l = split2(v)
    return jnp.concatenate([h, l], axis=0)


def times(vv, kt):
    kh, kl = kt
    r = dg(vv, kh, 1, 0)
    return r[:VEC] + r[VEC:] + dg(vv[:VEC], kl, 1, 0)


def gain(count):
    return gain_factor / math.sqrt(count)


def pack(w, skel):
    z = jnp.zeros((1, HALF), f32)
    return jnp.concatenate([w[:, :HALF], w[:, HALF:], skel[:, :HALF], z, skel[:, HALF:], z], axis=0)


def unpack(p):
    w = jnp.concatenate([p[:VEC], p[VEC : 2 * VEC]], axis=1)
    skel = jnp.concatenate([p[2 * VEC : 2 * VEC + 3], p[2 * VEC + 4 : 2 * VEC + 7]], axis=1)
    return w, skel


def up_kernel(pts_hbm, chg_hbm, mor_hbm, skl_hbm, skb_hbm, srt_ref, pack_ref, *scratch):
    pts_ref, chg_ref, mor_ref, skl_ref, skb_ref, sems = scratch
    copies = [
        pltpu.make_async_copy(src, dst, sems.at[i])
        for i, (src, dst) in enumerate(
            ((pts_hbm, pts_ref), (chg_hbm, chg_ref), (mor_hbm, mor_ref), (skl_hbm, skl_ref), (skb_hbm, skb_ref))
        )
    ]
    for c in copies:
        c.start()
    for c in copies:
        c.wait()
    n = chg_ref.shape[1]
    rows = jnp.concatenate([chg_ref[...], pts_ref[...], jnp.zeros((5, n), f32)], axis=0)
    a, b, c = split3(rows)
    parts = jnp.concatenate([a, b, c], axis=0).astype(bf16)
    for i in range(n // T):
        col = slice(i * T, (i + 1) * T)
        hot = (lax.broadcasted_iota(jnp.int32, (n, T), 0) == mor_ref[:, col]).astype(f32).astype(bf16)
        s = dg(parts, hot, 1, 0)
        srt_ref[:, col] = s[:ROWS] + s[ROWS : 2 * ROWS] + s[2 * ROWS :]
    srt_ref[VEC + 3 : VEC + 6, :T] = skb_ref[...]
    ft_block = feat_tgt(skb_ref[...])
    total = jnp.zeros((VEC, T), f32)
    for q in range(LEAVES_DEV):
        col = slice(q * T, (q + 1) * T)
        skel = skl_ref[:, col]
        lw = times(stack2(srt_ref[:VEC, col]), tile(feat_src(srt_ref[VEC : VEC + 3, col]), feat_tgt(skel)))
        total = total + times(stack2(gain(T) * lw), tile(feat_src(skel), ft_block))
    packed = pack(gain(LEAVES_DEV * T) * total, skb_ref[...])
    for z in range(pack_ref.shape[0]):
        pack_ref[z] = packed


def own_group(id_ref, skg_ref):
    return skg_ref[:, pl.ds(pl.multiple_of(id_ref[0] * T, T), T)]


def raised(id_ref, packs_ref, skg_ref):
    ft = feat_tgt(own_group(id_ref, skg_ref))
    total = jnp.zeros((VEC, T), f32)
    for c in range(packs_ref.shape[0]):
        w, skel = unpack(packs_ref[c])
        total = total + times(stack2(w), tile(feat_src(skel), ft))
    return total


def half_kernel(id_ref, part_ref, skg_ref, half_ref):
    half_ref[...] = raised(id_ref, part_ref, skg_ref)


def group_kernel(id_ref, part_ref, skg_ref, half_ref, gw_ref):
    total = half_ref[...] + raised(id_ref, part_ref, skg_ref)
    total = gain(4 * part_ref.shape[0] * T) * total
    for g in range(gw_ref.shape[0]):
        gw_ref[g] = total


def pre_kernel(skb_ref, skl_ref, mid_ref, mh_ref, ml_ref):
    fs_block = feat_src(skb_ref[...])
    for q in range(LEAVES_DEV):
        col = slice(q * T, (q + 1) * T)
        ah, al = tile(fs_block, feat_tgt(skl_ref[:, col]))
        bh, bl = tile(feat_src(skl_ref[:, col]), feat_tgt(mid_ref[VEC : VEC + 3, col]))
        both = dg(ah, bh, 1, 0) + dg(al, bh, 1, 0) + dg(ah, bl, 1, 0)
        mh_ref[:, col], ml_ref[:, col] = split2(gain(T) * gain(T) * both)


def near_kernel(id_ref, nbr_ref, cnt_ref, left_ref, mid_ref, right_ref, near_ref):
    first = id_ref[3]
    fts = [feat_tgt(mid_ref[VEC : VEC + 3, q * T : (q + 1) * T]) for q in range(LEAVES_DEV)]
    acc = [jnp.zeros((VEC, T), f32) for _ in range(LEAVES_DEV)]
    for s in range(-LEAVES_DEV, 2 * LEAVES_DEV):
        ref = (left_ref, mid_ref, right_ref)[s // LEAVES_DEV + 1]
        j = s % LEAVES_DEV
        v = ref[:VEC, j * T : (j + 1) * T]
        fs = feat_src(ref[VEC : VEC + 3, j * T : (j + 1) * T])
        for q in range(LEAVES_DEV):
            if abs(s - q) > LEAVES_DEV:
                continue
            uses = jnp.int32(1 if s == q else 0)
            for k in range(nbr_ref.shape[1]):
                hit = jnp.logical_and(nbr_ref[q, k] == first + s, cnt_ref[q] > k)
                uses = uses + hit.astype(jnp.int32)
            acc[q] = acc[q] + times(stack2(uses.astype(f32) * v), tile(fs, fts[q]))
    for q in range(LEAVES_DEV):
        near_ref[:, q * T : (q + 1) * T] = gain(T) * acc[q]


def sibling(core, left_ref, right_ref):
    rows = slice(VEC + 3, VEC + 6)
    return jnp.where(core == 0, right_ref[rows, :T], left_ref[rows, :T])


def peer_kernel(id_ref, part_ref, other_ref, skb_ref, left_ref, right_ref, skg_ref, peer_ref, bh_ref, bl_ref):
    n = part_ref.shape[0]
    ft_own = feat_tgt(skb_ref[...])
    ft_sib = feat_tgt(sibling(id_ref[2], left_ref, right_ref))
    own = jnp.zeros((VEC, T), f32)
    sib = jnp.zeros((VEC, T), f32)
    for c in range(2 * n):
        w, skel = unpack((part_ref if c < n else other_ref)[c % n])
        fs = feat_src(skel)
        if c < n:
            vv = stack2(jnp.where(id_ref[1] == c, 0.0, 1.0) * w)
            own = own + times(vv, tile(fs, ft_own))
            sib = sib + times(stack2(w), tile(fs, ft_sib))
        else:
            vv = stack2(w)
            own = own + times(vv, tile(fs, ft_own))
            sib = sib + times(vv, tile(fs, ft_sib))
    peer_ref[0] = gain((4 * n - 1) * T) * own
    peer_ref[1] = gain((4 * n - 1) * T) * sib
    fs = feat_src(own_group(id_ref, skg_ref))
    bh_ref[:, :T], bl_ref[:, :T] = tile(fs, ft_own)
    bh_ref[:, T:], bl_ref[:, T:] = tile(fs, ft_sib)


def field_kernel(id_ref, gws_ref, skg_ref, bh_ref, bl_ref, peer_ref, own_ref, sib_ref):
    n = gws_ref.shape[0]
    ft_own = feat_tgt(own_group(id_ref, skg_ref))
    total = jnp.zeros((VEC, T), f32)
    for g in range(n):
        keep = jnp.where(id_ref[0] == g, 0.0, 1.0)
        col = slice(g * T, (g + 1) * T)
        total = total + times(stack2(keep * gws_ref[g]), tile(feat_src(skg_ref[:, col]), ft_own))
    lowered = gain(T) * times(stack2(gain((n - 1) * T) * total), (bh_ref[...], bl_ref[...]))
    own_ref[...] = peer_ref[0] + lowered[:, :T]
    sib_ref[...] = peer_ref[1] + lowered[:, T:]


def down_kernel(id_ref, own_ref, both_ref, mh_ref, ml_ref, near_ref, out_ref):
    field = own_ref[...] + both_ref[1 - id_ref[2]]
    out_ref[...] = near_ref[...] + times(stack2(field), (mh_ref[...], ml_ref[...]))


VM = pl.BlockSpec(memory_space=pltpu.VMEM)
SM = pl.BlockSpec(memory_space=pltpu.SMEM)


def shape(*dims, dtype=f32):
    return jax.ShapeDtypeStruct(dims, dtype)


def kernel(fn, name, out, scalars, arrays):
    return pl.pallas_call(
        fn,
        out_shape=out,
        in_specs=[SM] * scalars + [VM] * arrays,
        out_specs=jax.tree.map(lambda _: VM, out),
        compiler_params=pltpu.CompilerParams(vmem_limit_bytes=24 << 20),
        name=name,
    )


def body(points, charges, morton, neighbours, counts, skel_leaf, skel_block, skel_group):
    n_groups = lax.axis_size("grp")
    n_z8 = lax.axis_size("z8")
    n = points.shape[1]
    axes = ("grp", "z8", "zp", "core")
    group_id = lax.axis_index("grp")
    z8_id = lax.axis_index("z8")
    core_id = lax.axis_index("core")
    block_id = ((group_id * n_z8 + z8_id) * 2 + lax.axis_index("zp")) * 2 + core_id
    ids = jnp.stack([group_id, z8_id, core_id, block_id * LEAVES_DEV]).astype(jnp.int32)
    inputs = (points, charges, morton.reshape(1, n), skel_leaf, skel_block)
    srt, packed = pl.pallas_call(
        up_kernel,
        out_shape=(shape(ROWS, n), shape(n_z8, PACK, HALF)),
        in_specs=[pl.BlockSpec(memory_space=pltpu.HBM)] * 5,
        out_specs=(VM, VM),
        scratch_shapes=[pltpu.VMEM(x.shape, x.dtype) for x in inputs] + [pltpu.SemaphoreType.DMA((5,))],
        compiler_params=pltpu.CompilerParams(vmem_limit_bytes=60 << 20),
        name="up",
    )(*inputs)
    part = lax.all_to_all(packed, "z8", 0, 0, tiled=False)
    whole = n_groups * n_z8 * 4
    left = lax.ppermute(srt, axes, [(i, i + 1) for i in range(whole - 1)])
    right = lax.ppermute(srt, axes, [(i + 1, i) for i in range(whole - 1)])
    half_shape = shape(T, n, dtype=bf16)
    mh, ml = kernel(pre_kernel, "pre", (half_shape, half_shape), 0, 3)(skel_block, skel_leaf, srt)
    near = kernel(near_kernel, "near", shape(VEC, n), 3, 3)(ids, neighbours, counts, left, srt, right)
    part, near, mh, ml = lax.optimization_barrier((part, near, mh, ml))
    other = lax.ppermute(part, "zp", [(0, 1), (1, 0)])
    half = kernel(half_kernel, "half", shape(VEC, T), 1, 2)(ids, part, skel_group)
    gw = kernel(group_kernel, "group", shape(n_groups, VEC, T), 1, 3)(ids, other, skel_group, half)
    gws = lax.all_to_all(gw, "grp", 0, 0, tiled=False)
    peer, bh, bl = kernel(
        peer_kernel, "peer", (shape(2, VEC, T), shape(T, 2 * T, dtype=bf16), shape(T, 2 * T, dtype=bf16)), 1, 6
    )(ids, part, other, skel_block, left, right, skel_group)
    own, sib = kernel(field_kernel, "field", (shape(VEC, T), shape(VEC, T)), 1, 5)(ids, gws, skel_group, bh, bl, peer)
    both = lax.all_gather(sib, "core", axis=0, tiled=False)
    return kernel(down_kernel, "down", shape(VEC, n), 1, 5)(ids, own, both, mh, ml, near)


def solution(mesh):
    fine = Mesh(mesh.devices.reshape(mesh.shape["grp"], mesh.shape["dev"] // 4, 2, 2), ("grp", "z8", "zp", "core"))
    all_axes = ("grp", "z8", "zp", "core")
    return jax.shard_map(
        body,
        mesh=fine,
        in_specs=(
            P(None, all_axes),
            P(None, all_axes),
            P(all_axes),
            P(all_axes, None),
            P(all_axes),
            P(None, all_axes),
            P(None, all_axes),
            P(),
        ),
        out_specs=P(None, all_axes),
        check_vma=False,
    )
```

```python
import math

import jax
import jax.numpy as jnp
from jax import lax
from jax.experimental import pallas as pl
from jax.experimental.pallas import tpu as pltpu
from jax.sharding import Mesh, PartitionSpec as P

f32 = jnp.float32
bf16 = jnp.bfloat16
width_sq = 0.1
gain_factor = 5.0
coord_scale = math.sqrt(math.log2(math.e) / width_sq)
VEC = 16
ROWS = 24
T = 256
LEAVES_DEV = 4
PACK = 40
HALF = 128


def dg(a, b, ca, cb):
    return lax.dot_general(a, b, (((ca,), (cb,)), ((), ())), preferred_element_type=f32)


def split2(v):
    h = v.astype(bf16)
    return h, (v - h.astype(f32)).astype(bf16)


def split3(v):
    a = v.astype(bf16).astype(f32)
    r = v - a
    b = r.astype(bf16).astype(f32)
    return a, b, r - b


def centred(x3):
    x = (x3 - 1.0) * coord_scale
    n = jnp.sum(x * x, axis=0, keepdims=True)
    return x, n, jnp.ones_like(n), jnp.zeros((3,) + n.shape[1:], f32)


def feat_src(x3):
    x, n, o, z = centred(x3)
    a, b, c = split3(jnp.concatenate([x, n, o, z], axis=0))
    return jnp.concatenate([a, a, a, b, b, c], axis=0).astype(bf16)


def feat_tgt(x3):
    x, n, o, z = centred(x3)
    a, b, c = split3(jnp.concatenate([2.0 * x, -o, -n, z], axis=0))
    return jnp.concatenate([a, b, c, a, b, a], axis=0).astype(bf16)


def tile(fs, ft):
    return split2(jnp.exp2(dg(fs, ft, 0, 0)))


def stack2(v):
    h, l = split2(v)
    return jnp.concatenate([h, l], axis=0)


def times(vv, kt):
    kh, kl = kt
    r = dg(vv, kh, 1, 0)
    return r[:VEC] + r[VEC:] + dg(vv[:VEC], kl, 1, 0)


def gain(count):
    return gain_factor / math.sqrt(count)


def pack(w, skel):
    z = jnp.zeros((1, HALF), f32)
    return jnp.concatenate([w[:, :HALF], w[:, HALF:], skel[:, :HALF], z, skel[:, HALF:], z], axis=0)


def unpack(p):
    w = jnp.concatenate([p[:VEC], p[VEC : 2 * VEC]], axis=1)
    skel = jnp.concatenate([p[2 * VEC : 2 * VEC + 3], p[2 * VEC + 4 : 2 * VEC + 7]], axis=1)
    return w, skel


def up_kernel(pts_hbm, chg_hbm, mor_hbm, skl_hbm, skb_hbm, srt_ref, pack_ref, *scratch):
    pts_ref, chg_ref, mor_ref, skl_ref, skb_ref, sems = scratch
    copies = [
        pltpu.make_async_copy(src, dst, sems.at[i])
        for i, (src, dst) in enumerate(
            ((pts_hbm, pts_ref), (chg_hbm, chg_ref), (mor_hbm, mor_ref), (skl_hbm, skl_ref), (skb_hbm, skb_ref))
        )
    ]
    for c in copies:
        c.start()
    for c in copies:
        c.wait()
    n = chg_ref.shape[1]
    rows = jnp.concatenate([chg_ref[...], pts_ref[...], jnp.zeros((5, n), f32)], axis=0)
    a, b, c = split3(rows)
    parts = jnp.concatenate([a, b, c], axis=0).astype(bf16)
    for i in range(n // T):
        col = slice(i * T, (i + 1) * T)
        hot = (lax.broadcasted_iota(jnp.int32, (n, T), 0) == mor_ref[:, col]).astype(f32).astype(bf16)
        s = dg(parts, hot, 1, 0)
        srt_ref[:, col] = s[:ROWS] + s[ROWS : 2 * ROWS] + s[2 * ROWS :]
    srt_ref[VEC + 3 : VEC + 6, :T] = skb_ref[...]
    ft_block = feat_tgt(skb_ref[...])
    total = jnp.zeros((VEC, T), f32)
    for q in range(LEAVES_DEV):
        col = slice(q * T, (q + 1) * T)
        skel = skl_ref[:, col]
        lw = times(stack2(srt_ref[:VEC, col]), tile(feat_src(srt_ref[VEC : VEC + 3, col]), feat_tgt(skel)))
        total = total + times(stack2(gain(T) * lw), tile(feat_src(skel), ft_block))
    packed = pack(gain(LEAVES_DEV * T) * total, skb_ref[...])
    for z in range(pack_ref.shape[0]):
        pack_ref[z] = packed


def own_group(id_ref, skg_ref):
    return skg_ref[:, pl.ds(pl.multiple_of(id_ref[0] * T, T), T)]


def raised(id_ref, packs_ref, skg_ref):
    ft = feat_tgt(own_group(id_ref, skg_ref))
    total = jnp.zeros((VEC, T), f32)
    for c in range(packs_ref.shape[0]):
        w, skel = unpack(packs_ref[c])
        total = total + times(stack2(w), tile(feat_src(skel), ft))
    return total


def group_kernel(id_ref, part_ref, skg_ref, gw_ref):
    total = gain(4 * part_ref.shape[0] * T) * raised(id_ref, part_ref, skg_ref)
    for g in range(gw_ref.shape[0]):
        gw_ref[g] = total


def pre_kernel(skb_ref, skl_ref, mid_ref, mh_ref, ml_ref):
    fs_block = feat_src(skb_ref[...])
    for q in range(LEAVES_DEV):
        col = slice(q * T, (q + 1) * T)
        ah, al = tile(fs_block, feat_tgt(skl_ref[:, col]))
        bh, bl = tile(feat_src(skl_ref[:, col]), feat_tgt(mid_ref[VEC : VEC + 3, col]))
        both = dg(ah, bh, 1, 0) + dg(al, bh, 1, 0) + dg(ah, bl, 1, 0)
        mh_ref[:, col], ml_ref[:, col] = split2(gain(T) * gain(T) * both)


def near_kernel(id_ref, nbr_ref, cnt_ref, sib_ref, adj_ref, mid_ref, near_ref, left_ref, right_ref):
    first = id_ref[3]
    on_left = id_ref[2] == 1
    left_ref[...] = jnp.where(on_left, sib_ref[...], adj_ref[...])
    right_ref[...] = jnp.where(on_left, adj_ref[...], sib_ref[...])
    fts = [feat_tgt(mid_ref[VEC : VEC + 3, q * T : (q + 1) * T]) for q in range(LEAVES_DEV)]
    acc = [jnp.zeros((VEC, T), f32) for _ in range(LEAVES_DEV)]
    for s in range(-LEAVES_DEV, 2 * LEAVES_DEV):
        ref = (left_ref, mid_ref, right_ref)[s // LEAVES_DEV + 1]
        j = s % LEAVES_DEV
        v = ref[:VEC, j * T : (j + 1) * T]
        fs = feat_src(ref[VEC : VEC + 3, j * T : (j + 1) * T])
        for q in range(LEAVES_DEV):
            if abs(s - q) > LEAVES_DEV:
                continue
            uses = jnp.int32(1 if s == q else 0)
            for k in range(nbr_ref.shape[1]):
                hit = jnp.logical_and(nbr_ref[q, k] == first + s, cnt_ref[q] > k)
                uses = uses + hit.astype(jnp.int32)
            acc[q] = acc[q] + times(stack2(uses.astype(f32) * v), tile(fs, fts[q]))
    for q in range(LEAVES_DEV):
        near_ref[:, q * T : (q + 1) * T] = gain(T) * acc[q]


def peer_kernel(id_ref, part_ref, other_ref, skb_ref, sibling_ref, skg_ref, peer_ref, bh_ref, bl_ref):
    n = part_ref.shape[0]
    ft_own = feat_tgt(skb_ref[...])
    ft_sib = feat_tgt(sibling_ref[VEC + 3 : VEC + 6, :T])
    own = jnp.zeros((VEC, T), f32)
    sib = jnp.zeros((VEC, T), f32)
    for c in range(2 * n):
        w, skel = unpack((part_ref if c < n else other_ref)[c % n])
        fs = feat_src(skel)
        vv = stack2(w)
        sib = sib + times(vv, tile(fs, ft_sib))
        if c < n:
            vv = stack2(jnp.where(id_ref[1] == c, 0.0, 1.0) * w)
        own = own + times(vv, tile(fs, ft_own))
    peer_ref[0] = gain((4 * n - 1) * T) * own
    peer_ref[1] = gain((4 * n - 1) * T) * sib
    kh, kl = tile(feat_src(own_group(id_ref, skg_ref)), ft_own)
    bh_ref[...] = kh
    bl_ref[...] = kl


def field_kernel(id_ref, gws_ref, skg_ref, peer_ref, part_ref):
    n = gws_ref.shape[0]
    ft_own = feat_tgt(own_group(id_ref, skg_ref))
    total = jnp.zeros((VEC, T), f32)
    for g in range(n):
        keep = jnp.where(id_ref[0] == g, 0.0, 1.0)
        col = slice(g * T, (g + 1) * T)
        total = total + times(stack2(keep * gws_ref[g]), tile(feat_src(skg_ref[:, col]), ft_own))
    part_ref[:VEC, :] = gain((n - 1) * T) * total
    part_ref[VEC:, :] = peer_ref[1]


def down_kernel(id_ref, cell_ref, peer_ref, bh_ref, bl_ref, mh_ref, ml_ref, near_ref, out_ref):
    group = jnp.sum(cell_ref[:, :VEC, :], axis=0)
    field = gain(T) * times(stack2(group), (bh_ref[...], bl_ref[...]))
    field = field + peer_ref[0] + cell_ref[id_ref[4], VEC:, :]
    out_ref[...] = near_ref[...] + times(stack2(field), (mh_ref[...], ml_ref[...]))


VM = pl.BlockSpec(memory_space=pltpu.VMEM)
SM = pl.BlockSpec(memory_space=pltpu.SMEM)


def shape(*dims, dtype=f32):
    return jax.ShapeDtypeStruct(dims, dtype)


def cost(tiles):
    return pl.CostEstimate(flops=tiles * 10**8, bytes_accessed=tiles * 2**18, transcendentals=tiles * T * T)


def kernel(fn, name, out, scalars, arrays, scratch=(), tiles=1):
    return pl.pallas_call(
        fn,
        out_shape=out,
        in_specs=[SM] * scalars + [VM] * arrays,
        out_specs=jax.tree.map(lambda _: VM, out),
        scratch_shapes=scratch,
        cost_estimate=cost(tiles),
        compiler_params=pltpu.CompilerParams(vmem_limit_bytes=24 << 20),
        name=name,
    )


def body(points, charges, morton, neighbours, counts, skel_leaf, skel_block, skel_group):
    n_groups = lax.axis_size("grp")
    n_z8 = lax.axis_size("z8")
    n = points.shape[1]
    axes = ("grp", "z8", "zp", "core")
    group_id = lax.axis_index("grp")
    z8_id = lax.axis_index("z8")
    zp_id = lax.axis_index("zp")
    core_id = lax.axis_index("core")
    block_id = ((group_id * n_z8 + z8_id) * 2 + zp_id) * 2 + core_id
    ids = [group_id, z8_id, core_id, block_id * LEAVES_DEV, zp_id * 2 + 1 - core_id]
    ids = jnp.stack(ids).astype(jnp.int32)
    inputs = (points, charges, morton.reshape(1, n), skel_leaf, skel_block)
    srt, packed = pl.pallas_call(
        up_kernel,
        out_shape=(shape(ROWS, n), shape(n_z8, PACK, HALF)),
        in_specs=[pl.BlockSpec(memory_space=pltpu.HBM)] * 5,
        out_specs=(VM, VM),
        scratch_shapes=[pltpu.VMEM(x.shape, x.dtype) for x in inputs] + [pltpu.SemaphoreType.DMA((5,))],
        compiler_params=pltpu.CompilerParams(vmem_limit_bytes=60 << 20),
        name="up",
    )(*inputs)
    part = lax.all_to_all(packed, "z8", 0, 0, tiled=False)
    whole = n_groups * n_z8 * 4
    swap = [(0, 1), (1, 0)]
    sib = lax.ppermute(srt, "core", swap)
    odd = range(1, whole - 1, 2)
    adj = lax.ppermute(srt, axes, [(i, i + 1) for i in odd] + [(i + 1, i) for i in odd])
    half_shape = shape(T, n, dtype=bf16)
    mh, ml = kernel(pre_kernel, "pre", (half_shape, half_shape), 0, 3, tiles=12)(skel_block, skel_leaf, srt)
    block = pltpu.VMEM((ROWS, n), f32)
    near = kernel(near_kernel, "near", shape(VEC, n), 3, 3, (block, block), 40)(ids, neighbours, counts, sib, adj, srt)
    part, near, mh, ml = lax.optimization_barrier((part, near, mh, ml))
    other = lax.ppermute(part, "zp", swap)
    gw = kernel(group_kernel, "group", shape(n_groups, VEC, T), 1, 2, tiles=30)(ids, part, skel_group)
    gws = lax.all_to_all(gw, "grp", 0, 0, tiled=False)
    square = shape(T, T, dtype=bf16)
    peer, bh, bl = kernel(peer_kernel, "peer", (shape(2, VEC, T), square, square), 1, 5, tiles=33)(
        ids, part, other, skel_block, sib, skel_group
    )
    mine = kernel(field_kernel, "field", shape(2 * VEC, T), 1, 3, tiles=20)(ids, gws, skel_group, peer)
    cell = lax.all_gather(mine, ("zp", "core"), axis=0, tiled=False)
    return kernel(down_kernel, "down", shape(VEC, n), 1, 7)(ids, cell, peer, bh, bl, mh, ml, near)


def solution(mesh):
    fine = Mesh(mesh.devices.reshape(mesh.shape["grp"], mesh.shape["dev"] // 4, 2, 2), ("grp", "z8", "zp", "core"))
    all_axes = ("grp", "z8", "zp", "core")
    return jax.shard_map(
        body,
        mesh=fine,
        in_specs=(
            P(None, all_axes),
            P(None, all_axes),
            P(all_axes),
            P(all_axes, None),
            P(all_axes),
            P(None, all_axes),
            P(None, all_axes),
            P(),
        ),
        out_specs=P(None, all_axes),
        check_vma=False,
    )
```

```python
import math

import jax
import jax.numpy as jnp
from jax import lax
from jax.experimental import pallas as pl
from jax.experimental.pallas import tpu as pltpu
from jax.sharding import Mesh, PartitionSpec as P

f32 = jnp.float32
bf16 = jnp.bfloat16
width_sq = 0.1
gain_factor = 5.0
coord_scale = math.sqrt(math.log2(math.e) / width_sq)
VEC = 16
ROWS = 24
T = 256
LEAVES_DEV = 4
PACK = 40
HALF = 128


def dg(a, b, ca, cb):
    return lax.dot_general(a, b, (((ca,), (cb,)), ((), ())), preferred_element_type=f32)


def split2(v):
    h = v.astype(bf16)
    return h, (v - h.astype(f32)).astype(bf16)


def split3(v):
    a = v.astype(bf16).astype(f32)
    r = v - a
    b = r.astype(bf16).astype(f32)
    return a, b, r - b


def centred(x3):
    x = (x3 - 1.0) * coord_scale
    n = jnp.sum(x * x, axis=0, keepdims=True)
    return x, n, jnp.ones_like(n), jnp.zeros((3,) + n.shape[1:], f32)


def feat_src(x3):
    x, n, o, z = centred(x3)
    a, b, c = split3(jnp.concatenate([x, n, o, z], axis=0))
    return jnp.concatenate([a, a, a, b, b, c], axis=0).astype(bf16)


def feat_tgt(x3):
    x, n, o, z = centred(x3)
    a, b, c = split3(jnp.concatenate([2.0 * x, -o, -n, z], axis=0))
    return jnp.concatenate([a, b, c, a, b, a], axis=0).astype(bf16)


def tile(fs, ft):
    return split2(jnp.exp2(dg(fs, ft, 0, 0)))


def stack2(v):
    h, l = split2(v)
    return jnp.concatenate([h, l], axis=0)


def times(vv, kt):
    kh, kl = kt
    r = dg(vv, kh, 1, 0)
    return r[:VEC] + r[VEC:] + dg(vv[:VEC], kl, 1, 0)


def gain(count):
    return gain_factor / math.sqrt(count)


def pack(w, skel):
    z = jnp.zeros((1, HALF), f32)
    return jnp.concatenate([w[:, :HALF], w[:, HALF:], skel[:, :HALF], z, skel[:, HALF:], z], axis=0)


def unpack(p):
    w = jnp.concatenate([p[:VEC], p[VEC : 2 * VEC]], axis=1)
    skel = jnp.concatenate([p[2 * VEC : 2 * VEC + 3], p[2 * VEC + 4 : 2 * VEC + 7]], axis=1)
    return w, skel


def up_kernel(pts_hbm, chg_hbm, mor_hbm, skl_hbm, skb_hbm, srt_ref, pack_ref, *scratch):
    pts_ref, chg_ref, mor_ref, skl_ref, skb_ref, sems = scratch
    copies = [
        pltpu.make_async_copy(src, dst, sems.at[i])
        for i, (src, dst) in enumerate(
            ((skl_hbm, skl_ref), (skb_hbm, skb_ref), (pts_hbm, pts_ref), (mor_hbm, mor_ref), (chg_hbm, chg_ref))
        )
    ]
    for c in copies:
        c.start()
    for c in copies:
        c.wait()
    n = chg_ref.shape[1]
    rows = jnp.concatenate([chg_ref[...], pts_ref[...], jnp.zeros((5, n), f32)], axis=0)
    a, b, c = split3(rows)
    parts = jnp.concatenate([a, b, c], axis=0).astype(bf16)
    row = lax.broadcasted_iota(jnp.int32, (n, T), 0)
    ft_block = feat_tgt(skb_ref[...])
    total = jnp.zeros((VEC, T), f32)
    for q in range(LEAVES_DEV):
        col = slice(q * T, (q + 1) * T)
        skel = skl_ref[:, col]
        hot = (row == mor_ref[:, col]).astype(f32).astype(bf16)
        s = dg(parts, hot, 1, 0)
        srt = s[:ROWS] + s[ROWS : 2 * ROWS] + s[2 * ROWS :]
        srt_ref[:, col] = srt
        vv = jnp.concatenate([s[:VEC], s[ROWS : ROWS + VEC] + s[2 * ROWS : 2 * ROWS + VEC]], axis=0).astype(bf16)
        lw = times(vv, tile(feat_src(srt[VEC : VEC + 3]), feat_tgt(skel)))
        total = total + times(stack2(gain(T) * lw), tile(feat_src(skel), ft_block))
    srt_ref[VEC + 3 : VEC + 6, :T] = skb_ref[...]
    packed = pack(gain(LEAVES_DEV * T) * total, skb_ref[...])
    for z in range(pack_ref.shape[0]):
        pack_ref[z] = packed


def own_group(skg_ref):
    return skg_ref[:, pl.ds(pl.multiple_of(lax.axis_index("grp") * T, T), T)]


def raised(packs_ref, skg_ref):
    ft = feat_tgt(own_group(skg_ref))
    total = jnp.zeros((VEC, T), f32)
    for c in range(packs_ref.shape[0]):
        w, skel = unpack(packs_ref[c])
        total = total + times(stack2(w), tile(feat_src(skel), ft))
    return total


def group_kernel(part_ref, skg_ref, gw_ref):
    total = gain(4 * part_ref.shape[0] * T) * raised(part_ref, skg_ref)
    for g in range(gw_ref.shape[0]):
        gw_ref[g] = total


def pre_kernel(skb_ref, skl_ref, mid_ref, mh_ref, ml_ref):
    fs_block = feat_src(skb_ref[...])
    for q in range(LEAVES_DEV):
        col = slice(q * T, (q + 1) * T)
        ah, al = tile(fs_block, feat_tgt(skl_ref[:, col]))
        bh, bl = tile(feat_src(skl_ref[:, col]), feat_tgt(mid_ref[VEC : VEC + 3, col]))
        both = dg(ah, bh, 1, 0) + dg(al, bh, 1, 0) + dg(ah, bl, 1, 0)
        mh_ref[:, col], ml_ref[:, col] = split2(gain(T) * gain(T) * both)


def near_kernel(nbr_ref, cnt_ref, sib_ref, adj_ref, mid_ref, near_ref, left_ref, right_ref):
    core = lax.axis_index("core")
    pair = (lax.axis_index("grp") * lax.axis_size("z8") + lax.axis_index("z8")) * 2 + lax.axis_index("zp")
    first = (pair * 2 + core) * LEAVES_DEV
    on_left = core == 1
    left_ref[...] = jnp.where(on_left, sib_ref[...], adj_ref[...])
    right_ref[...] = jnp.where(on_left, adj_ref[...], sib_ref[...])
    fts = [feat_tgt(mid_ref[VEC : VEC + 3, q * T : (q + 1) * T]) for q in range(LEAVES_DEV)]
    acc = [jnp.zeros((VEC, T), f32) for _ in range(LEAVES_DEV)]
    for s in range(-LEAVES_DEV, 2 * LEAVES_DEV):
        ref = (left_ref, mid_ref, right_ref)[s // LEAVES_DEV + 1]
        j = s % LEAVES_DEV
        v = ref[:VEC, j * T : (j + 1) * T]
        fs = feat_src(ref[VEC : VEC + 3, j * T : (j + 1) * T])
        for q in range(LEAVES_DEV):
            if abs(s - q) > LEAVES_DEV:
                continue
            uses = jnp.int32(1 if s == q else 0)
            for k in range(nbr_ref.shape[1]):
                hit = jnp.logical_and(nbr_ref[q, k] == first + s, cnt_ref[q] > k)
                uses = uses + hit.astype(jnp.int32)
            acc[q] = acc[q] + times(stack2(uses.astype(f32) * v), tile(fs, fts[q]))
    for q in range(LEAVES_DEV):
        near_ref[:, q * T : (q + 1) * T] = gain(T) * acc[q]


def peer_kernel(part_ref, other_ref, skb_ref, sibling_ref, skg_ref, peer_ref, bh_ref, bl_ref):
    n = part_ref.shape[0]
    ft_own = feat_tgt(skb_ref[...])
    ft_sib = feat_tgt(sibling_ref[VEC + 3 : VEC + 6, :T])
    own = jnp.zeros((VEC, T), f32)
    sib = jnp.zeros((VEC, T), f32)
    for c in range(2 * n):
        w, skel = unpack((part_ref if c < n else other_ref)[c % n])
        fs = feat_src(skel)
        vv = stack2(w)
        sib = sib + times(vv, tile(fs, ft_sib))
        if c < n:
            vv = stack2(jnp.where(lax.axis_index("z8") == c, 0.0, 1.0) * w)
        own = own + times(vv, tile(fs, ft_own))
    peer_ref[0] = gain((4 * n - 1) * T) * own
    peer_ref[1] = gain((4 * n - 1) * T) * sib
    kh, kl = tile(feat_src(own_group(skg_ref)), ft_own)
    bh_ref[...] = kh
    bl_ref[...] = kl


def field_kernel(gws_ref, skg_ref, peer_ref, part_ref):
    n = gws_ref.shape[0]
    ft_own = feat_tgt(own_group(skg_ref))
    total = jnp.zeros((VEC, T), f32)
    for g in range(n):
        keep = jnp.where(lax.axis_index("grp") == g, 0.0, 1.0)
        col = slice(g * T, (g + 1) * T)
        total = total + times(stack2(keep * gws_ref[g]), tile(feat_src(skg_ref[:, col]), ft_own))
    part_ref[:VEC, :] = gain((n - 1) * T) * total
    part_ref[VEC:, :] = peer_ref[1]


def down_kernel(cell_ref, peer_ref, bh_ref, bl_ref, mh_ref, ml_ref, near_ref, out_ref):
    group = jnp.sum(cell_ref[:, :VEC, :], axis=0)
    field = gain(T) * times(stack2(group), (bh_ref[...], bl_ref[...]))
    field = field + peer_ref[0] + cell_ref[lax.axis_index("zp") * 2 + 1 - lax.axis_index("core"), VEC:, :]
    out_ref[...] = near_ref[...] + times(stack2(field), (mh_ref[...], ml_ref[...]))


VM = pl.BlockSpec(memory_space=pltpu.VMEM)
SM = pl.BlockSpec(memory_space=pltpu.SMEM)


def shape(*dims, dtype=f32):
    return jax.ShapeDtypeStruct(dims, dtype)


def cost(tiles):
    return pl.CostEstimate(flops=tiles * 10**8, bytes_accessed=tiles * 2**18, transcendentals=tiles * T * T)


def kernel(fn, name, out, scalars, arrays, scratch=(), tiles=1):
    return pl.pallas_call(
        fn,
        out_shape=out,
        in_specs=[SM] * scalars + [VM] * arrays,
        out_specs=jax.tree.map(lambda _: VM, out),
        scratch_shapes=scratch,
        cost_estimate=cost(tiles),
        compiler_params=pltpu.CompilerParams(vmem_limit_bytes=24 << 20),
        name=name,
    )


def body(points, charges, morton, neighbours, counts, skel_leaf, skel_block, skel_group):
    n_groups = lax.axis_size("grp")
    n_z8 = lax.axis_size("z8")
    n = points.shape[1]
    axes = ("grp", "z8", "zp", "core")
    inputs = (points, charges, morton.reshape(1, n), skel_leaf, skel_block)
    srt, packed = pl.pallas_call(
        up_kernel,
        out_shape=(shape(ROWS, n), shape(n_z8, PACK, HALF)),
        in_specs=[pl.BlockSpec(memory_space=pltpu.HBM)] * 5,
        out_specs=(VM, VM),
        scratch_shapes=[pltpu.VMEM(x.shape, x.dtype) for x in inputs] + [pltpu.SemaphoreType.DMA((5,))],
        compiler_params=pltpu.CompilerParams(vmem_limit_bytes=60 << 20),
        name="up",
    )(*inputs)
    part = lax.all_to_all(packed, "z8", 0, 0, tiled=False)
    whole = n_groups * n_z8 * 4
    swap = [(0, 1), (1, 0)]
    sib = lax.ppermute(srt, "core", swap)
    odd = range(1, whole - 1, 2)
    adj = lax.ppermute(srt, axes, [(i, i + 1) for i in odd] + [(i + 1, i) for i in odd])
    half_shape = shape(T, n, dtype=bf16)
    mh, ml = kernel(pre_kernel, "pre", (half_shape, half_shape), 0, 3, tiles=12)(skel_block, skel_leaf, srt)
    block = pltpu.VMEM((ROWS, n), f32)
    near = kernel(near_kernel, "near", shape(VEC, n), 2, 3, (block, block), 40)(neighbours, counts, sib, adj, srt)
    part, near, mh, ml = lax.optimization_barrier((part, near, mh, ml))
    other = lax.ppermute(part, "zp", swap)
    gw = kernel(group_kernel, "group", shape(n_groups, VEC, T), 0, 2, tiles=30)(part, skel_group)
    gws = lax.all_to_all(gw, "grp", 0, 0, tiled=False)
    square = shape(T, T, dtype=bf16)
    peer, bh, bl = kernel(peer_kernel, "peer", (shape(2, VEC, T), square, square), 0, 5, tiles=33)(
        part, other, skel_block, sib, skel_group
    )
    mine = kernel(field_kernel, "field", shape(2 * VEC, T), 0, 3, tiles=20)(gws, skel_group, peer)
    cell = lax.all_gather(mine, ("zp", "core"), axis=0, tiled=False)
    return kernel(down_kernel, "down", shape(VEC, n), 0, 7)(cell, peer, bh, bl, mh, ml, near)


def solution(mesh):
    fine = Mesh(mesh.devices.reshape(mesh.shape["grp"], mesh.shape["dev"] // 4, 2, 2), ("grp", "z8", "zp", "core"))
    all_axes = ("grp", "z8", "zp", "core")
    return jax.shard_map(
        body,
        mesh=fine,
        in_specs=(
            P(None, all_axes),
            P(None, all_axes),
            P(all_axes),
            P(all_axes, None),
            P(all_axes),
            P(None, all_axes),
            P(None, all_axes),
            P(),
        ),
        out_specs=P(None, all_axes),
        check_vma=False,
    )
```

```python
import math

import jax
import jax.numpy as jnp
from jax import lax
from jax.experimental import pallas as pl
from jax.experimental.pallas import tpu as pltpu
from jax.sharding import Mesh, PartitionSpec as P

f32 = jnp.float32
bf16 = jnp.bfloat16
width_sq = 0.1
gain_factor = 5.0
coord_scale = math.sqrt(math.log2(math.e) / width_sq)
VEC = 16
ROWS = 24
T = 256
LEAVES_DEV = 4
PACK = 40
HALF = 128


def dg(a, b, ca, cb):
    return lax.dot_general(a, b, (((ca,), (cb,)), ((), ())), preferred_element_type=f32)


def split2(v):
    h = v.astype(bf16)
    return h, (v - h.astype(f32)).astype(bf16)


def split3(v):
    a = v.astype(bf16).astype(f32)
    r = v - a
    b = r.astype(bf16).astype(f32)
    return a, b, r - b


def centred(x3):
    x = (x3 - 1.0) * coord_scale
    n = jnp.sum(x * x, axis=0, keepdims=True)
    return x, n, jnp.ones_like(n), jnp.zeros((3,) + n.shape[1:], f32)


def feat_src(x3):
    x, n, o, z = centred(x3)
    a, b, c = split3(jnp.concatenate([x, n, o, z], axis=0))
    return jnp.concatenate([a, a, a, b, b, c], axis=0).astype(bf16)


def feat_tgt(x3):
    x, n, o, z = centred(x3)
    a, b, c = split3(jnp.concatenate([2.0 * x, -o, -n, z], axis=0))
    return jnp.concatenate([a, b, c, a, b, a], axis=0).astype(bf16)


def tile(fs, ft):
    return split2(jnp.exp2(dg(fs, ft, 0, 0)))


def stack2(v):
    h, l = split2(v)
    return jnp.concatenate([h, l], axis=0)


def times(vv, kt):
    kh, kl = kt
    r = dg(vv, kh, 1, 0)
    return r[:VEC] + r[VEC:] + dg(vv[:VEC], kl, 1, 0)


def gain(count):
    return gain_factor / math.sqrt(count)


def pack(w, skel):
    z = jnp.zeros((1, HALF), f32)
    return jnp.concatenate([w[:, :HALF], w[:, HALF:], skel[:, :HALF], z, skel[:, HALF:], z], axis=0)


def unpack(p):
    w = jnp.concatenate([p[:VEC], p[VEC : 2 * VEC]], axis=1)
    skel = jnp.concatenate([p[2 * VEC : 2 * VEC + 3], p[2 * VEC + 4 : 2 * VEC + 7]], axis=1)
    return w, skel


def up_kernel(pts_hbm, chg_hbm, mor_hbm, skl_hbm, skb_hbm, srt_ref, pack_ref, *scratch):
    pts_ref, chg_ref, mor_ref, skl_ref, skb_ref, sems = scratch
    copies = [
        pltpu.make_async_copy(src, dst, sems.at[i])
        for i, (src, dst) in enumerate(
            ((skl_hbm, skl_ref), (skb_hbm, skb_ref), (pts_hbm, pts_ref), (mor_hbm, mor_ref), (chg_hbm, chg_ref))
        )
    ]
    for c in copies:
        c.start()
    for c in copies:
        c.wait()
    n = chg_ref.shape[1]
    rows = jnp.concatenate([chg_ref[...], pts_ref[...], jnp.zeros((5, n), f32)], axis=0)
    a, b, c = split3(rows)
    parts = jnp.concatenate([a, b, c], axis=0).astype(bf16)
    row = lax.broadcasted_iota(jnp.int32, (n, T), 0)
    ft_block = feat_tgt(skb_ref[...])
    total = jnp.zeros((VEC, T), f32)
    for q in range(LEAVES_DEV):
        col = slice(q * T, (q + 1) * T)
        skel = skl_ref[:, col]
        hot = (row == mor_ref[:, col]).astype(f32).astype(bf16)
        s = dg(parts, hot, 1, 0)
        srt = s[:ROWS] + s[ROWS : 2 * ROWS] + s[2 * ROWS :]
        srt_ref[:, col] = srt
        vv = jnp.concatenate([s[:VEC], s[ROWS : ROWS + VEC] + s[2 * ROWS : 2 * ROWS + VEC]], axis=0).astype(bf16)
        lw = times(vv, tile(feat_src(srt[VEC : VEC + 3]), feat_tgt(skel)))
        total = total + times(stack2(gain(T) * lw), tile(feat_src(skel), ft_block))
    srt_ref[VEC + 3 : VEC + 6, :T] = skb_ref[...]
    packed = pack(gain(LEAVES_DEV * T) * total, skb_ref[...])
    for z in range(pack_ref.shape[0]):
        pack_ref[z] = packed


def own_group(skg_ref):
    return skg_ref[:, pl.ds(pl.multiple_of(lax.axis_index("grp") * T, T), T)]


def raised(packs_ref, skg_ref):
    ft = feat_tgt(own_group(skg_ref))
    total = jnp.zeros((VEC, T), f32)
    for c in range(packs_ref.shape[0]):
        w, skel = unpack(packs_ref[c])
        total = total + times(stack2(w), tile(feat_src(skel), ft))
    return total


def group_kernel(part_ref, skg_ref, gw_ref):
    total = gain(4 * part_ref.shape[0] * T) * raised(part_ref, skg_ref)
    for g in range(gw_ref.shape[0]):
        gw_ref[g] = total


def pre_kernel(skb_ref, skl_ref, mid_ref, mh_ref, ml_ref):
    fs_block = feat_src(skb_ref[...])
    for q in range(LEAVES_DEV):
        col = slice(q * T, (q + 1) * T)
        ah, al = tile(fs_block, feat_tgt(skl_ref[:, col]))
        bh, bl = tile(feat_src(skl_ref[:, col]), feat_tgt(mid_ref[VEC : VEC + 3, col]))
        both = dg(ah, bh, 1, 0) + dg(al, bh, 1, 0) + dg(ah, bl, 1, 0)
        mh_ref[:, col], ml_ref[:, col] = split2(gain(T) * gain(T) * both)


def first_leaf():
    pair = (lax.axis_index("grp") * lax.axis_size("z8") + lax.axis_index("z8")) * 2 + lax.axis_index("zp")
    return (pair * 2 + lax.axis_index("core")) * LEAVES_DEV


def leaf(ref, j):
    col = slice(j * T, (j + 1) * T)
    return ref[:VEC, col], ref[VEC : VEC + 3, col]


def uses(nbr_ref, cnt_ref, q, source):
    count = jnp.int32(0)
    for k in range(nbr_ref.shape[1]):
        hit = jnp.logical_and(nbr_ref[q, k] == source, cnt_ref[q] > k)
        count = count + hit.astype(jnp.int32)
    return count


def side_near(nbr_ref, cnt_ref, blk_ref, on_right, fts, acc):
    first = first_leaf() + jnp.where(on_right, LEAVES_DEV, -LEAVES_DEV)
    for d in range(LEAVES_DEV):
        (v0, x0), (v1, x1) = leaf(blk_ref, d), leaf(blk_ref, LEAVES_DEV - 1 - d)
        v = jnp.where(on_right, v0, v1)
        fs = feat_src(jnp.where(on_right, x0, x1))
        source = first + jnp.where(on_right, d, LEAVES_DEV - 1 - d)
        for e in range(d, LEAVES_DEV):
            q0, q1 = e, LEAVES_DEV - 1 - e
            m = jnp.where(on_right, uses(nbr_ref, cnt_ref, q0, source), uses(nbr_ref, cnt_ref, q1, source))
            r = times(stack2(m.astype(f32) * v), tile(fs, jnp.where(on_right, fts[q0], fts[q1])))
            acc[q0] = acc[q0] + jnp.where(on_right, r, 0.0)
            acc[q1] = acc[q1] + jnp.where(on_right, 0.0, r)


def near_kernel(nbr_ref, cnt_ref, sib_ref, mid_ref, near_ref):
    on_right = lax.axis_index("core") == 0
    first = first_leaf()
    fts = [feat_tgt(leaf(mid_ref, q)[1]) for q in range(LEAVES_DEV)]
    acc = [jnp.zeros((VEC, T), f32) for _ in range(LEAVES_DEV)]
    for j in range(LEAVES_DEV):
        v, x = leaf(mid_ref, j)
        fs = feat_src(x)
        for q in range(LEAVES_DEV):
            m = 1 if j == q else uses(nbr_ref, cnt_ref, q, first + j)
            vv = stack2(v if j == q else m.astype(f32) * v)
            acc[q] = acc[q] + times(vv, tile(fs, fts[q]))
    side_near(nbr_ref, cnt_ref, sib_ref, on_right, fts, acc)
    for q in range(LEAVES_DEV):
        near_ref[:, q * T : (q + 1) * T] = gain(T) * acc[q]


def peer_kernel(
    nbr_ref, cnt_ref, part_ref, other_ref, skb_ref, sibling_ref, skg_ref, adj_ref, mid_ref, near_ref, peer_ref, bh_ref, bl_ref, all_ref
):
    n = part_ref.shape[0]
    ft_own = feat_tgt(skb_ref[...])
    ft_sib = feat_tgt(sibling_ref[VEC + 3 : VEC + 6, :T])
    own = jnp.zeros((VEC, T), f32)
    sib = jnp.zeros((VEC, T), f32)
    for c in range(2 * n):
        w, skel = unpack((part_ref if c < n else other_ref)[c % n])
        fs = feat_src(skel)
        vv = stack2(w)
        sib = sib + times(vv, tile(fs, ft_sib))
        if c < n:
            vv = stack2(jnp.where(lax.axis_index("z8") == c, 0.0, 1.0) * w)
        own = own + times(vv, tile(fs, ft_own))
    peer_ref[0] = gain((4 * n - 1) * T) * own
    peer_ref[1] = gain((4 * n - 1) * T) * sib
    kh, kl = tile(feat_src(own_group(skg_ref)), ft_own)
    bh_ref[...] = kh
    bl_ref[...] = kl
    fts = [feat_tgt(leaf(mid_ref, q)[1]) for q in range(LEAVES_DEV)]
    acc = [jnp.zeros((VEC, T), f32) for _ in range(LEAVES_DEV)]
    side_near(nbr_ref, cnt_ref, adj_ref, lax.axis_index("core") == 1, fts, acc)
    for q in range(LEAVES_DEV):
        col = slice(q * T, (q + 1) * T)
        all_ref[:, col] = near_ref[:, col] + gain(T) * acc[q]


def field_kernel(gws_ref, skg_ref, peer_ref, part_ref):
    n = gws_ref.shape[0]
    ft_own = feat_tgt(own_group(skg_ref))
    total = jnp.zeros((VEC, T), f32)
    for g in range(n):
        keep = jnp.where(lax.axis_index("grp") == g, 0.0, 1.0)
        col = slice(g * T, (g + 1) * T)
        total = total + times(stack2(keep * gws_ref[g]), tile(feat_src(skg_ref[:, col]), ft_own))
    part_ref[:VEC, :] = gain((n - 1) * T) * total
    part_ref[VEC:, :] = peer_ref[1]


def down_kernel(cell_ref, peer_ref, bh_ref, bl_ref, mh_ref, ml_ref, near_ref, out_ref):
    group = jnp.sum(cell_ref[:, :VEC, :], axis=0)
    field = gain(T) * times(stack2(group), (bh_ref[...], bl_ref[...]))
    field = field + peer_ref[0] + cell_ref[lax.axis_index("zp") * 2 + 1 - lax.axis_index("core"), VEC:, :]
    out_ref[...] = near_ref[...] + times(stack2(field), (mh_ref[...], ml_ref[...]))


VM = pl.BlockSpec(memory_space=pltpu.VMEM)
SM = pl.BlockSpec(memory_space=pltpu.SMEM)


def shape(*dims, dtype=f32):
    return jax.ShapeDtypeStruct(dims, dtype)


def cost(tiles):
    return pl.CostEstimate(flops=tiles * 10**8, bytes_accessed=tiles * 2**18, transcendentals=tiles * T * T)


def kernel(fn, name, out, scalars, arrays, scratch=(), tiles=1):
    return pl.pallas_call(
        fn,
        out_shape=out,
        in_specs=[SM] * scalars + [VM] * arrays,
        out_specs=jax.tree.map(lambda _: VM, out),
        scratch_shapes=scratch,
        cost_estimate=cost(tiles),
        compiler_params=pltpu.CompilerParams(vmem_limit_bytes=24 << 20),
        name=name,
    )


def body(points, charges, morton, neighbours, counts, skel_leaf, skel_block, skel_group):
    n_groups = lax.axis_size("grp")
    n_z8 = lax.axis_size("z8")
    n = points.shape[1]
    axes = ("grp", "z8", "zp", "core")
    inputs = (points, charges, morton.reshape(1, n), skel_leaf, skel_block)
    srt, packed = pl.pallas_call(
        up_kernel,
        out_shape=(shape(ROWS, n), shape(n_z8, PACK, HALF)),
        in_specs=[pl.BlockSpec(memory_space=pltpu.HBM)] * 5,
        out_specs=(VM, VM),
        scratch_shapes=[pltpu.VMEM(x.shape, x.dtype) for x in inputs] + [pltpu.SemaphoreType.DMA((5,))],
        compiler_params=pltpu.CompilerParams(vmem_limit_bytes=60 << 20),
        name="up",
    )(*inputs)
    part = lax.all_to_all(packed, "z8", 0, 0, tiled=False)
    whole = n_groups * n_z8 * 4
    swap = [(0, 1), (1, 0)]
    sib = lax.ppermute(srt, "core", swap)
    half_shape = shape(T, n, dtype=bf16)
    mh, ml = kernel(pre_kernel, "pre", (half_shape, half_shape), 0, 3, tiles=12)(skel_block, skel_leaf, srt)
    near = kernel(near_kernel, "near", shape(VEC, n), 2, 2, tiles=26)(neighbours, counts, sib, srt)
    srt, near, mh, ml = lax.optimization_barrier((srt, near, mh, ml))
    odd = range(1, whole - 1, 2)
    adj = lax.ppermute(srt, axes, [(i, i + 1) for i in odd] + [(i + 1, i) for i in odd])
    part, near, mh, ml = lax.optimization_barrier((part, near, mh, ml))
    other = lax.ppermute(part, "zp", swap)
    gw = kernel(group_kernel, "group", shape(n_groups, VEC, T), 0, 2, tiles=30)(part, skel_group)
    gws = lax.all_to_all(gw, "grp", 0, 0, tiled=False)
    square = shape(T, T, dtype=bf16)
    peer, bh, bl, near = kernel(peer_kernel, "peer", (shape(2, VEC, T), square, square, shape(VEC, n)), 2, 8, tiles=43)(
        neighbours, counts, part, other, skel_block, sib, skel_group, adj, srt, near
    )
    mine = kernel(field_kernel, "field", shape(2 * VEC, T), 0, 3, tiles=20)(gws, skel_group, peer)
    cell = lax.all_gather(mine, ("zp", "core"), axis=0, tiled=False)
    return kernel(down_kernel, "down", shape(VEC, n), 0, 7)(cell, peer, bh, bl, mh, ml, near)


def solution(mesh):
    fine = Mesh(mesh.devices.reshape(mesh.shape["grp"], mesh.shape["dev"] // 4, 2, 2), ("grp", "z8", "zp", "core"))
    all_axes = ("grp", "z8", "zp", "core")
    return jax.shard_map(
        body,
        mesh=fine,
        in_specs=(
            P(None, all_axes),
            P(None, all_axes),
            P(all_axes),
            P(all_axes, None),
            P(all_axes),
            P(None, all_axes),
            P(None, all_axes),
            P(),
        ),
        out_specs=P(None, all_axes),
        check_vma=False,
    )
```

```python
import math

import jax
import jax.numpy as jnp
from jax import lax
from jax.experimental import pallas as pl
from jax.experimental.pallas import tpu as pltpu
from jax.sharding import Mesh, PartitionSpec as P

f32 = jnp.float32
bf16 = jnp.bfloat16
width_sq = 0.1
gain_factor = 5.0
coord_scale = math.sqrt(math.log2(math.e) / width_sq)
VEC = 16
ROWS = 24
T = 256
LEAVES_DEV = 4
PACK = 40
HALF = 128


def dg(a, b, ca, cb):
    return lax.dot_general(a, b, (((ca,), (cb,)), ((), ())), preferred_element_type=f32)


def split2(v):
    h = v.astype(bf16)
    return h, (v - h.astype(f32)).astype(bf16)


def split3(v):
    a = v.astype(bf16).astype(f32)
    r = v - a
    b = r.astype(bf16).astype(f32)
    return a, b, r - b


def centred(x3):
    x = (x3 - 1.0) * coord_scale
    n = jnp.sum(x * x, axis=0, keepdims=True)
    return x, n, jnp.ones_like(n), jnp.zeros((3,) + n.shape[1:], f32)


def feat_src(x3):
    x, n, o, z = centred(x3)
    a, b, c = split3(jnp.concatenate([x, n, o, z], axis=0))
    return jnp.concatenate([a, a, a, b, b, c], axis=0).astype(bf16)


def feat_tgt(x3):
    x, n, o, z = centred(x3)
    a, b, c = split3(jnp.concatenate([2.0 * x, -o, -n, z], axis=0))
    return jnp.concatenate([a, b, c, a, b, a], axis=0).astype(bf16)


def tile(fs, ft):
    return split2(jnp.exp2(dg(fs, ft, 0, 0)))


def stack2(v):
    h, l = split2(v)
    return jnp.concatenate([h, l], axis=0)


def times(vv, kt):
    kh, kl = kt
    r = dg(vv, kh, 1, 0)
    return r[:VEC] + r[VEC:] + dg(vv[:VEC], kl, 1, 0)


def gain(count):
    return gain_factor / math.sqrt(count)


def pack(w, skel):
    z = jnp.zeros((1, HALF), f32)
    return jnp.concatenate([w[:, :HALF], w[:, HALF:], skel[:, :HALF], z, skel[:, HALF:], z], axis=0)


def unpack(p):
    w = jnp.concatenate([p[:VEC], p[VEC : 2 * VEC]], axis=1)
    skel = jnp.concatenate([p[2 * VEC : 2 * VEC + 3], p[2 * VEC + 4 : 2 * VEC + 7]], axis=1)
    return w, skel


def up_kernel(pts_hbm, chg_hbm, mor_hbm, skl_hbm, skb_hbm, srt_ref, pack_ref, *scratch):
    pts_ref, chg_ref, mor_ref, skl_ref, skb_ref, kh_ref, kl_ref, sems = scratch
    pairs = ((skl_hbm, skl_ref), (skb_hbm, skb_ref), (mor_hbm, mor_ref), (pts_hbm, pts_ref), (chg_hbm, chg_ref))
    copies = [pltpu.make_async_copy(src, dst, sems.at[i]) for i, (src, dst) in enumerate(pairs)]
    for c in copies:
        c.start()
    copies[0].wait()
    copies[1].wait()
    ft_block = feat_tgt(skb_ref[...])
    for q in range(LEAVES_DEV):
        col = slice(q * T, (q + 1) * T)
        kh, kl = tile(feat_src(skl_ref[:, col]), ft_block)
        kh_ref[col, :] = kh
        kl_ref[col, :] = kl
    for c in copies[2:]:
        c.wait()
    n = chg_ref.shape[1]
    rows = jnp.concatenate([chg_ref[...], pts_ref[...], jnp.zeros((5, n), f32)], axis=0)
    a, b, c = split3(rows)
    parts = jnp.concatenate([a, b, c], axis=0).astype(bf16)
    row = lax.broadcasted_iota(jnp.int32, (n, T), 0)
    sorts = []
    for q in range(LEAVES_DEV):
        col = slice(q * T, (q + 1) * T)
        hot = (row == mor_ref[:, col]).astype(f32).astype(bf16)
        s = dg(parts, hot, 1, 0)
        srt = s[:ROWS] + s[ROWS : 2 * ROWS] + s[2 * ROWS :]
        if q == 0:
            srt = jnp.concatenate([srt[: VEC + 3], skb_ref[...], srt[VEC + 6 :]], axis=0)
        srt_ref[:, col] = srt
        sorts.append(s)
    total = jnp.zeros((VEC, T), f32)
    for q in range(LEAVES_DEV):
        col = slice(q * T, (q + 1) * T)
        s = sorts[q]
        vv = jnp.concatenate([s[:VEC], s[ROWS : ROWS + VEC] + s[2 * ROWS : 2 * ROWS + VEC]], axis=0).astype(bf16)
        lw = times(vv, tile(feat_src(srt_ref[VEC : VEC + 3, col]), feat_tgt(skl_ref[:, col])))
        total = total + times(stack2(gain(T) * lw), (kh_ref[col, :], kl_ref[col, :]))
    packed = pack(gain(LEAVES_DEV * T) * total, skb_ref[...])
    for z in range(pack_ref.shape[0]):
        pack_ref[z] = packed


def own_group(skg_ref):
    return skg_ref[:, pl.ds(pl.multiple_of(lax.axis_index("grp") * T, T), T)]


def raised(packs_ref, skg_ref):
    ft = feat_tgt(own_group(skg_ref))
    total = jnp.zeros((VEC, T), f32)
    for c in range(packs_ref.shape[0]):
        w, skel = unpack(packs_ref[c])
        total = total + times(stack2(w), tile(feat_src(skel), ft))
    return total


def group_kernel(part_ref, skg_ref, gw_ref):
    total = gain(4 * part_ref.shape[0] * T) * raised(part_ref, skg_ref)
    for g in range(gw_ref.shape[0]):
        gw_ref[g] = total


def pre_kernel(skb_ref, skl_ref, mid_ref, mh_ref, ml_ref):
    fs_block = feat_src(skb_ref[...])
    for q in range(LEAVES_DEV):
        col = slice(q * T, (q + 1) * T)
        ah, al = tile(fs_block, feat_tgt(skl_ref[:, col]))
        bh, bl = tile(feat_src(skl_ref[:, col]), feat_tgt(mid_ref[VEC : VEC + 3, col]))
        both = dg(ah, bh, 1, 0) + dg(al, bh, 1, 0) + dg(ah, bl, 1, 0)
        mh_ref[:, col], ml_ref[:, col] = split2(gain(T) * gain(T) * both)


def first_leaf():
    pair = (lax.axis_index("grp") * lax.axis_size("z8") + lax.axis_index("z8")) * 2 + lax.axis_index("zp")
    return (pair * 2 + lax.axis_index("core")) * LEAVES_DEV


def leaf(ref, j):
    col = slice(j * T, (j + 1) * T)
    return ref[:VEC, col], ref[VEC : VEC + 3, col]


def slots(nbr_ref, cnt_ref):
    shape = nbr_ref.shape
    leaves = (shape[0], shape[0])
    diagonal = lax.broadcasted_iota(jnp.int32, leaves, 0) == lax.broadcasted_iota(jnp.int32, leaves, 1)
    count = jnp.sum(jnp.where(diagonal, cnt_ref[...].astype(f32), 0.0), axis=1, keepdims=True)
    used = lax.broadcasted_iota(jnp.int32, shape, 1).astype(f32) < count
    return jnp.where(used, nbr_ref[...], -(1 << 24))


def uses(table, source):
    return jnp.sum(jnp.where(table == source, 1.0, 0.0), axis=1, keepdims=True)


def side_near(table, blk_ref, on_right, fts, acc):
    first = first_leaf() + jnp.where(on_right, LEAVES_DEV, -LEAVES_DEV)
    for d in range(LEAVES_DEV):
        (v0, x0), (v1, x1) = leaf(blk_ref, d), leaf(blk_ref, LEAVES_DEV - 1 - d)
        v = jnp.where(on_right, v0, v1)
        fs = feat_src(jnp.where(on_right, x0, x1))
        source = first + jnp.where(on_right, d, LEAVES_DEV - 1 - d)
        m = uses(table, source)
        for e in range(d, LEAVES_DEV):
            q0, q1 = e, LEAVES_DEV - 1 - e
            times_used = jnp.where(on_right, m[q0 : q0 + 1], m[q1 : q1 + 1])
            r = times(stack2(times_used * v), tile(fs, jnp.where(on_right, fts[q0], fts[q1])))
            acc[q0] = acc[q0] + jnp.where(on_right, r, 0.0)
            acc[q1] = acc[q1] + jnp.where(on_right, 0.0, r)


def near_kernel(nbr_ref, cnt_ref, sib_ref, mid_ref, near_ref):
    on_right = lax.axis_index("core") == 0
    first = first_leaf()
    table = slots(nbr_ref, cnt_ref)
    fts = [feat_tgt(leaf(mid_ref, q)[1]) for q in range(LEAVES_DEV)]
    acc = [jnp.zeros((VEC, T), f32) for _ in range(LEAVES_DEV)]
    for j in range(LEAVES_DEV):
        v, x = leaf(mid_ref, j)
        fs = feat_src(x)
        m = uses(table, first + j)
        for q in range(LEAVES_DEV):
            vv = stack2(v if j == q else m[q : q + 1] * v)
            acc[q] = acc[q] + times(vv, tile(fs, fts[q]))
    side_near(table, sib_ref, on_right, fts, acc)
    for q in range(LEAVES_DEV):
        near_ref[:, q * T : (q + 1) * T] = gain(T) * acc[q]


def peer_kernel(
    nbr_ref, cnt_ref, part_ref, other_ref, skb_ref, sibling_ref, skg_ref, adj_ref, mid_ref, near_ref, peer_ref, bh_ref, bl_ref, all_ref
):
    n = part_ref.shape[0]
    ft_own = feat_tgt(skb_ref[...])
    ft_sib = feat_tgt(sibling_ref[VEC + 3 : VEC + 6, :T])
    own = jnp.zeros((VEC, T), f32)
    sib = jnp.zeros((VEC, T), f32)
    for c in range(2 * n):
        w, skel = unpack((part_ref if c < n else other_ref)[c % n])
        fs = feat_src(skel)
        vv = stack2(w)
        sib = sib + times(vv, tile(fs, ft_sib))
        if c < n:
            vv = stack2(jnp.where(lax.axis_index("z8") == c, 0.0, 1.0) * w)
        own = own + times(vv, tile(fs, ft_own))
    peer_ref[0] = gain((4 * n - 1) * T) * own
    peer_ref[1] = gain((4 * n - 1) * T) * sib
    kh, kl = tile(feat_src(own_group(skg_ref)), ft_own)
    bh_ref[...] = kh
    bl_ref[...] = kl
    fts = [feat_tgt(leaf(mid_ref, q)[1]) for q in range(LEAVES_DEV)]
    acc = [jnp.zeros((VEC, T), f32) for _ in range(LEAVES_DEV)]
    side_near(slots(nbr_ref, cnt_ref), adj_ref, lax.axis_index("core") == 1, fts, acc)
    for q in range(LEAVES_DEV):
        col = slice(q * T, (q + 1) * T)
        all_ref[:, col] = near_ref[:, col] + gain(T) * acc[q]


def field_kernel(gws_ref, skg_ref, peer_ref, part_ref):
    n = gws_ref.shape[0]
    ft_own = feat_tgt(own_group(skg_ref))
    total = jnp.zeros((VEC, T), f32)
    for g in range(n):
        keep = jnp.where(lax.axis_index("grp") == g, 0.0, 1.0)
        col = slice(g * T, (g + 1) * T)
        total = total + times(stack2(keep * gws_ref[g]), tile(feat_src(skg_ref[:, col]), ft_own))
    part_ref[:VEC, :] = gain((n - 1) * T) * total
    part_ref[VEC:, :] = peer_ref[1]


def down_kernel(cell_ref, peer_ref, bh_ref, bl_ref, mh_ref, ml_ref, near_ref, out_ref):
    group = jnp.sum(cell_ref[:, :VEC, :], axis=0)
    field = gain(T) * times(stack2(group), (bh_ref[...], bl_ref[...]))
    field = field + peer_ref[0] + cell_ref[lax.axis_index("zp") * 2 + 1 - lax.axis_index("core"), VEC:, :]
    out_ref[...] = near_ref[...] + times(stack2(field), (mh_ref[...], ml_ref[...]))


VM = pl.BlockSpec(memory_space=pltpu.VMEM)
SM = pl.BlockSpec(memory_space=pltpu.SMEM)


def shape(*dims, dtype=f32):
    return jax.ShapeDtypeStruct(dims, dtype)


def cost(tiles):
    return pl.CostEstimate(flops=tiles * 10**8, bytes_accessed=tiles * 2**18, transcendentals=tiles * T * T)


def kernel(fn, name, out, scalars, arrays, scratch=(), tiles=1):
    return pl.pallas_call(
        fn,
        out_shape=out,
        in_specs=[SM] * scalars + [VM] * arrays,
        out_specs=jax.tree.map(lambda _: VM, out),
        scratch_shapes=scratch,
        cost_estimate=cost(tiles),
        compiler_params=pltpu.CompilerParams(vmem_limit_bytes=24 << 20),
        name=name,
    )


def body(points, charges, morton, neighbours, counts, skel_leaf, skel_block, skel_group):
    n_groups = lax.axis_size("grp")
    n_z8 = lax.axis_size("z8")
    n = points.shape[1]
    axes = ("grp", "z8", "zp", "core")
    counts = counts.reshape(1, LEAVES_DEV)
    inputs = (points, charges, morton.reshape(1, n), skel_leaf, skel_block)
    srt, packed = pl.pallas_call(
        up_kernel,
        out_shape=(shape(ROWS, n), shape(n_z8, PACK, HALF)),
        in_specs=[pl.BlockSpec(memory_space=pltpu.HBM)] * 5,
        out_specs=(VM, VM),
        scratch_shapes=[pltpu.VMEM(x.shape, x.dtype) for x in inputs]
        + [pltpu.VMEM((n, T), bf16), pltpu.VMEM((n, T), bf16), pltpu.SemaphoreType.DMA((5,))],
        compiler_params=pltpu.CompilerParams(vmem_limit_bytes=60 << 20),
        name="up",
    )(*inputs)
    part = lax.all_to_all(packed, "z8", 0, 0, tiled=False)
    whole = n_groups * n_z8 * 4
    swap = [(0, 1), (1, 0)]
    sib = lax.ppermute(srt, "core", swap)
    half_shape = shape(T, n, dtype=bf16)
    mh, ml = kernel(pre_kernel, "pre", (half_shape, half_shape), 0, 3, tiles=12)(skel_block, skel_leaf, srt)
    near = kernel(near_kernel, "near", shape(VEC, n), 0, 4, tiles=26)(neighbours, counts, sib, srt)
    srt, near, mh, ml = lax.optimization_barrier((srt, near, mh, ml))
    odd = range(1, whole - 1, 2)
    adj = lax.ppermute(srt, axes, [(i, i + 1) for i in odd] + [(i + 1, i) for i in odd])
    part, near, mh, ml = lax.optimization_barrier((part, near, mh, ml))
    other = lax.ppermute(part, "zp", swap)
    gw = kernel(group_kernel, "group", shape(n_groups, VEC, T), 0, 2, tiles=30)(part, skel_group)
    gws = lax.all_to_all(gw, "grp", 0, 0, tiled=False)
    square = shape(T, T, dtype=bf16)
    peer, bh, bl, near = kernel(peer_kernel, "peer", (shape(2, VEC, T), square, square, shape(VEC, n)), 0, 10, tiles=43)(
        neighbours, counts, part, other, skel_block, sib, skel_group, adj, srt, near
    )
    mine = kernel(field_kernel, "field", shape(2 * VEC, T), 0, 3, tiles=20)(gws, skel_group, peer)
    cell = lax.all_gather(mine, ("zp", "core"), axis=0, tiled=False)
    return kernel(down_kernel, "down", shape(VEC, n), 0, 7)(cell, peer, bh, bl, mh, ml, near)


def solution(mesh):
    fine = Mesh(mesh.devices.reshape(mesh.shape["grp"], mesh.shape["dev"] // 4, 2, 2), ("grp", "z8", "zp", "core"))
    all_axes = ("grp", "z8", "zp", "core")
    return jax.shard_map(
        body,
        mesh=fine,
        in_specs=(
            P(None, all_axes),
            P(None, all_axes),
            P(all_axes),
            P(all_axes, None),
            P(all_axes),
            P(None, all_axes),
            P(None, all_axes),
            P(),
        ),
        out_specs=P(None, all_axes),
        check_vma=False,
    )
```

```python
import math

import jax
import jax.numpy as jnp
from jax import lax
from jax.experimental import pallas as pl
from jax.experimental.pallas import tpu as pltpu
from jax.sharding import Mesh, PartitionSpec as P

f32 = jnp.float32
bf16 = jnp.bfloat16
width_sq = 0.1
gain_factor = 5.0
coord_scale = math.sqrt(math.log2(math.e) / width_sq)
VEC = 16
ROWS = 24
T = 256
LEAVES_DEV = 4
PACK = 40
HALF = 128


def dg(a, b, ca, cb):
    return lax.dot_general(a, b, (((ca,), (cb,)), ((), ())), preferred_element_type=f32)


def split2(v):
    h = v.astype(bf16)
    return h, (v - h.astype(f32)).astype(bf16)


def split3(v):
    a = v.astype(bf16).astype(f32)
    r = v - a
    b = r.astype(bf16).astype(f32)
    return a, b, r - b


def centred(x3):
    x = (x3 - 1.0) * coord_scale
    n = jnp.sum(x * x, axis=0, keepdims=True)
    return x, n, jnp.ones_like(n), jnp.zeros((3,) + n.shape[1:], f32)


def feat_src(x3):
    x, n, o, z = centred(x3)
    a, b, c = split3(jnp.concatenate([x, n, o, z], axis=0))
    return jnp.concatenate([a, a, a, b, b, c], axis=0).astype(bf16)


def feat_tgt(x3):
    x, n, o, z = centred(x3)
    a, b, c = split3(jnp.concatenate([2.0 * x, -o, -n, z], axis=0))
    return jnp.concatenate([a, b, c, a, b, a], axis=0).astype(bf16)


def tile(fs, ft):
    return split2(jnp.exp2(dg(fs, ft, 0, 0)))


def stack2(v):
    h, l = split2(v)
    return jnp.concatenate([h, l], axis=0)


def times(vv, kt):
    kh, kl = kt
    r = dg(vv, kh, 1, 0)
    return r[:VEC] + r[VEC:] + dg(vv[:VEC], kl, 1, 0)


def gain(count):
    return gain_factor / math.sqrt(count)


def pack(w, skel):
    z = jnp.zeros((1, HALF), f32)
    return jnp.concatenate([w[:, :HALF], w[:, HALF:], skel[:, :HALF], z, skel[:, HALF:], z], axis=0)


def unpack(p):
    w = jnp.concatenate([p[:VEC], p[VEC : 2 * VEC]], axis=1)
    skel = jnp.concatenate([p[2 * VEC : 2 * VEC + 3], p[2 * VEC + 4 : 2 * VEC + 7]], axis=1)
    return w, skel


def up_kernel(pts_hbm, chg_hbm, mor_hbm, skl_hbm, skb_hbm, srt_ref, pack_ref, *scratch):
    pts_ref, chg_ref, mor_ref, skl_ref, skb_ref, kh_ref, kl_ref, sems = scratch
    pairs = ((skl_hbm, skl_ref), (skb_hbm, skb_ref), (mor_hbm, mor_ref), (pts_hbm, pts_ref), (chg_hbm, chg_ref))
    copies = [pltpu.make_async_copy(src, dst, sems.at[i]) for i, (src, dst) in enumerate(pairs)]
    for c in copies:
        c.start()
    copies[0].wait()
    copies[1].wait()
    ft_block = feat_tgt(skb_ref[...])
    for q in range(LEAVES_DEV):
        col = slice(q * T, (q + 1) * T)
        kh, kl = tile(feat_src(skl_ref[:, col]), ft_block)
        kh_ref[col, :] = kh
        kl_ref[col, :] = kl
    for c in copies[2:]:
        c.wait()
    n = chg_ref.shape[1]
    rows = jnp.concatenate([chg_ref[...], pts_ref[...], jnp.zeros((5, n), f32)], axis=0)
    a, b, c = split3(rows)
    parts = jnp.concatenate([a, b, c], axis=0).astype(bf16)
    row = lax.broadcasted_iota(jnp.int32, (n, T), 0)
    sorts = []
    for q in range(LEAVES_DEV):
        col = slice(q * T, (q + 1) * T)
        hot = (row == mor_ref[:, col]).astype(f32).astype(bf16)
        s = dg(parts, hot, 1, 0)
        srt = s[:ROWS] + s[ROWS : 2 * ROWS] + s[2 * ROWS :]
        if q == 0:
            srt = jnp.concatenate([srt[: VEC + 3], skb_ref[...], srt[VEC + 6 :]], axis=0)
        srt_ref[:, col] = srt
        sorts.append(s)
    total = jnp.zeros((VEC, T), f32)
    for q in range(LEAVES_DEV):
        col = slice(q * T, (q + 1) * T)
        s = sorts[q]
        vv = jnp.concatenate([s[:VEC], s[ROWS : ROWS + VEC] + s[2 * ROWS : 2 * ROWS + VEC]], axis=0).astype(bf16)
        lw = times(vv, tile(feat_src(srt_ref[VEC : VEC + 3, col]), feat_tgt(skl_ref[:, col])))
        total = total + times(stack2(gain(T) * lw), (kh_ref[col, :], kl_ref[col, :]))
    packed = pack(gain(LEAVES_DEV * T) * total, skb_ref[...])
    for z in range(pack_ref.shape[0]):
        pack_ref[z] = packed


def own_group(skg_ref):
    return skg_ref[:, pl.ds(pl.multiple_of(lax.axis_index("grp") * T, T), T)]


def raised(packs_ref, skg_ref):
    ft = feat_tgt(own_group(skg_ref))
    total = jnp.zeros((VEC, T), f32)
    for c in range(packs_ref.shape[0]):
        w, skel = unpack(packs_ref[c])
        total = total + times(stack2(w), tile(feat_src(skel), ft))
    return total


def group_kernel(part_ref, skg_ref, gw_ref):
    total = gain(4 * part_ref.shape[0] * T) * raised(part_ref, skg_ref)
    for g in range(gw_ref.shape[0]):
        gw_ref[g] = total


def first_leaf():
    pair = (lax.axis_index("grp") * lax.axis_size("z8") + lax.axis_index("z8")) * 2 + lax.axis_index("zp")
    return (pair * 2 + lax.axis_index("core")) * LEAVES_DEV


def leaf(ref, j):
    col = slice(j * T, (j + 1) * T)
    return ref[:VEC, col], ref[VEC : VEC + 3, col]


def slots(nbr_ref, cnt_ref):
    shape = nbr_ref.shape
    leaves = (shape[0], shape[0])
    diagonal = lax.broadcasted_iota(jnp.int32, leaves, 0) == lax.broadcasted_iota(jnp.int32, leaves, 1)
    count = jnp.sum(jnp.where(diagonal, cnt_ref[...].astype(f32), 0.0), axis=1, keepdims=True)
    used = lax.broadcasted_iota(jnp.int32, shape, 1).astype(f32) < count
    return jnp.where(used, nbr_ref[...], -(1 << 24))


def uses(table, source):
    return jnp.sum(jnp.where(table == source, 1.0, 0.0), axis=1, keepdims=True)


def side_near(table, blk_ref, on_right, fts, acc):
    first = first_leaf() + jnp.where(on_right, LEAVES_DEV, -LEAVES_DEV)
    for d in range(LEAVES_DEV):
        (v0, x0), (v1, x1) = leaf(blk_ref, d), leaf(blk_ref, LEAVES_DEV - 1 - d)
        v = jnp.where(on_right, v0, v1)
        fs = feat_src(jnp.where(on_right, x0, x1))
        source = first + jnp.where(on_right, d, LEAVES_DEV - 1 - d)
        m = uses(table, source)
        for e in range(d, LEAVES_DEV):
            q0, q1 = e, LEAVES_DEV - 1 - e
            times_used = jnp.where(on_right, m[q0 : q0 + 1], m[q1 : q1 + 1])
            r = times(stack2(times_used * v), tile(fs, jnp.where(on_right, fts[q0], fts[q1])))
            acc[q0] = acc[q0] + jnp.where(on_right, r, 0.0)
            acc[q1] = acc[q1] + jnp.where(on_right, 0.0, r)


def near_kernel(nbr_ref, cnt_ref, mid_ref, skb_ref, skl_ref, near_ref, mh_ref, ml_ref):
    first = first_leaf()
    table = slots(nbr_ref, cnt_ref)
    fts = [feat_tgt(leaf(mid_ref, q)[1]) for q in range(LEAVES_DEV)]
    fs_block = feat_src(skb_ref[...])
    for q in range(LEAVES_DEV):
        col = slice(q * T, (q + 1) * T)
        ah, al = tile(fs_block, feat_tgt(skl_ref[:, col]))
        bh, bl = tile(feat_src(skl_ref[:, col]), fts[q])
        both = dg(ah, bh, 1, 0) + dg(al, bh, 1, 0) + dg(ah, bl, 1, 0)
        mh_ref[:, col], ml_ref[:, col] = split2(gain(T) * gain(T) * both)
    acc = [jnp.zeros((VEC, T), f32) for _ in range(LEAVES_DEV)]
    for j in range(LEAVES_DEV):
        v, x = leaf(mid_ref, j)
        fs = feat_src(x)
        m = uses(table, first + j)
        for q in range(LEAVES_DEV):
            vv = stack2(v if j == q else m[q : q + 1] * v)
            acc[q] = acc[q] + times(vv, tile(fs, fts[q]))
    for q in range(LEAVES_DEV):
        near_ref[:, q * T : (q + 1) * T] = gain(T) * acc[q]


def peer_kernel(
    nbr_ref, cnt_ref, part_ref, other_ref, skb_ref, sibling_ref, skg_ref, adj_ref, mid_ref, near_ref, peer_ref, bh_ref, bl_ref, all_ref
):
    n = part_ref.shape[0]
    ft_own = feat_tgt(skb_ref[...])
    ft_sib = feat_tgt(sibling_ref[VEC + 3 : VEC + 6, :T])
    own = jnp.zeros((VEC, T), f32)
    sib = jnp.zeros((VEC, T), f32)
    for c in range(2 * n):
        w, skel = unpack((part_ref if c < n else other_ref)[c % n])
        fs = feat_src(skel)
        vv = stack2(w)
        sib = sib + times(vv, tile(fs, ft_sib))
        if c < n:
            vv = stack2(jnp.where(lax.axis_index("z8") == c, 0.0, 1.0) * w)
        own = own + times(vv, tile(fs, ft_own))
    peer_ref[0] = gain((4 * n - 1) * T) * own
    peer_ref[1] = gain((4 * n - 1) * T) * sib
    kh, kl = tile(feat_src(own_group(skg_ref)), ft_own)
    bh_ref[...] = kh
    bl_ref[...] = kl
    fts = [feat_tgt(leaf(mid_ref, q)[1]) for q in range(LEAVES_DEV)]
    acc = [jnp.zeros((VEC, T), f32) for _ in range(LEAVES_DEV)]
    table = slots(nbr_ref, cnt_ref)
    side_near(table, sibling_ref, lax.axis_index("core") == 0, fts, acc)
    side_near(table, adj_ref, lax.axis_index("core") == 1, fts, acc)
    for q in range(LEAVES_DEV):
        col = slice(q * T, (q + 1) * T)
        all_ref[:, col] = near_ref[:, col] + gain(T) * acc[q]


def field_kernel(gws_ref, skg_ref, peer_ref, part_ref):
    n = gws_ref.shape[0]
    ft_own = feat_tgt(own_group(skg_ref))
    total = jnp.zeros((VEC, T), f32)
    for g in range(n):
        keep = jnp.where(lax.axis_index("grp") == g, 0.0, 1.0)
        col = slice(g * T, (g + 1) * T)
        total = total + times(stack2(keep * gws_ref[g]), tile(feat_src(skg_ref[:, col]), ft_own))
    part_ref[:VEC, :] = gain((n - 1) * T) * total
    part_ref[VEC:, :] = peer_ref[1]


def down_kernel(cell_ref, peer_ref, bh_ref, bl_ref, mh_ref, ml_ref, near_ref, out_ref):
    group = jnp.sum(cell_ref[:, :VEC, :], axis=0)
    field = gain(T) * times(stack2(group), (bh_ref[...], bl_ref[...]))
    field = field + peer_ref[0] + cell_ref[lax.axis_index("zp") * 2 + 1 - lax.axis_index("core"), VEC:, :]
    out_ref[...] = near_ref[...] + times(stack2(field), (mh_ref[...], ml_ref[...]))


VM = pl.BlockSpec(memory_space=pltpu.VMEM)
SM = pl.BlockSpec(memory_space=pltpu.SMEM)


def shape(*dims, dtype=f32):
    return jax.ShapeDtypeStruct(dims, dtype)


def cost(tiles):
    return pl.CostEstimate(flops=tiles * 10**8, bytes_accessed=tiles * 2**18, transcendentals=tiles * T * T)


def kernel(fn, name, out, scalars, arrays, scratch=(), tiles=1):
    return pl.pallas_call(
        fn,
        out_shape=out,
        in_specs=[SM] * scalars + [VM] * arrays,
        out_specs=jax.tree.map(lambda _: VM, out),
        scratch_shapes=scratch,
        cost_estimate=cost(tiles),
        compiler_params=pltpu.CompilerParams(vmem_limit_bytes=24 << 20),
        name=name,
    )


def body(points, charges, morton, neighbours, counts, skel_leaf, skel_block, skel_group):
    n_groups = lax.axis_size("grp")
    n_z8 = lax.axis_size("z8")
    n = points.shape[1]
    axes = ("grp", "z8", "zp", "core")
    counts = counts.reshape(1, LEAVES_DEV)
    inputs = (points, charges, morton.reshape(1, n), skel_leaf, skel_block)
    srt, packed = pl.pallas_call(
        up_kernel,
        out_shape=(shape(ROWS, n), shape(n_z8, PACK, HALF)),
        in_specs=[pl.BlockSpec(memory_space=pltpu.HBM)] * 5,
        out_specs=(VM, VM),
        scratch_shapes=[pltpu.VMEM(x.shape, x.dtype) for x in inputs]
        + [pltpu.VMEM((n, T), bf16), pltpu.VMEM((n, T), bf16), pltpu.SemaphoreType.DMA((5,))],
        compiler_params=pltpu.CompilerParams(vmem_limit_bytes=60 << 20),
        name="up",
    )(*inputs)
    part = lax.all_to_all(packed, "z8", 0, 0, tiled=False)
    whole = n_groups * n_z8 * 4
    swap = [(0, 1), (1, 0)]
    sib = lax.ppermute(srt, "core", swap)
    operator = shape(T, n, dtype=bf16)
    near, mh, ml = kernel(near_kernel, "near", (shape(VEC, n), operator, operator), 0, 5, tiles=28)(
        neighbours, counts, srt, skel_block, skel_leaf
    )
    srt, near, mh, ml = lax.optimization_barrier((srt, near, mh, ml))
    odd = range(1, whole - 1, 2)
    adj = lax.ppermute(srt, axes, [(i, i + 1) for i in odd] + [(i + 1, i) for i in odd])
    part, near, mh, ml = lax.optimization_barrier((part, near, mh, ml))
    other = lax.ppermute(part, "zp", swap)
    gw = kernel(group_kernel, "group", shape(n_groups, VEC, T), 0, 2, tiles=30)(part, skel_group)
    gws = lax.all_to_all(gw, "grp", 0, 0, tiled=False)
    square = shape(T, T, dtype=bf16)
    peer, bh, bl, near = kernel(peer_kernel, "peer", (shape(2, VEC, T), square, square, shape(VEC, n)), 0, 10, tiles=53)(
        neighbours, counts, part, other, skel_block, sib, skel_group, adj, srt, near
    )
    mine = kernel(field_kernel, "field", shape(2 * VEC, T), 0, 3, tiles=20)(gws, skel_group, peer)
    cell = lax.all_gather(mine, ("zp", "core"), axis=0, tiled=False)
    return kernel(down_kernel, "down", shape(VEC, n), 0, 7)(cell, peer, bh, bl, mh, ml, near)


def solution(mesh):
    fine = Mesh(mesh.devices.reshape(mesh.shape["grp"], mesh.shape["dev"] // 4, 2, 2), ("grp", "z8", "zp", "core"))
    all_axes = ("grp", "z8", "zp", "core")
    return jax.shard_map(
        body,
        mesh=fine,
        in_specs=(
            P(None, all_axes),
            P(None, all_axes),
            P(all_axes),
            P(all_axes, None),
            P(all_axes),
            P(None, all_axes),
            P(None, all_axes),
            P(),
        ),
        out_specs=P(None, all_axes),
        check_vma=False,
    )
```

```python
import math

import jax
import jax.numpy as jnp
from jax import lax
from jax.experimental import pallas as pl
from jax.experimental.pallas import tpu as pltpu
from jax.sharding import Mesh, PartitionSpec as P

f32 = jnp.float32
bf16 = jnp.bfloat16
width_sq = 0.1
gain_factor = 5.0
coord_scale = math.sqrt(math.log2(math.e) / width_sq)
VEC = 16
ROWS = 24
T = 256
LEAVES_DEV = 4
PACK = 40
HALF = 128


def dg(a, b, ca, cb):
    return lax.dot_general(a, b, (((ca,), (cb,)), ((), ())), preferred_element_type=f32)


def split2(v):
    h = v.astype(bf16)
    return h, (v - h.astype(f32)).astype(bf16)


def split3(v):
    a = v.astype(bf16).astype(f32)
    r = v - a
    b = r.astype(bf16).astype(f32)
    return a, b, r - b


def centred(x3):
    x = (x3 - 1.0) * coord_scale
    n = jnp.sum(x * x, axis=0, keepdims=True)
    return x, n, jnp.ones_like(n), jnp.zeros((3,) + n.shape[1:], f32)


def feat_src(x3):
    x, n, o, z = centred(x3)
    a, b, c = split3(jnp.concatenate([x, n, o, z], axis=0))
    return jnp.concatenate([a, a, a, b, b, c], axis=0).astype(bf16)


def feat_tgt(x3):
    x, n, o, z = centred(x3)
    a, b, c = split3(jnp.concatenate([2.0 * x, -o, -n, z], axis=0))
    return jnp.concatenate([a, b, c, a, b, a], axis=0).astype(bf16)


def tile(fs, ft):
    return split2(jnp.exp2(dg(fs, ft, 0, 0)))


def stack2(v):
    h, l = split2(v)
    return jnp.concatenate([h, l], axis=0)


def times(vv, kt):
    kh, kl = kt
    r = dg(vv, kh, 1, 0)
    return r[:VEC] + r[VEC:] + dg(vv[:VEC], kl, 1, 0)


def gain(count):
    return gain_factor / math.sqrt(count)


def pack(w, skel):
    z = jnp.zeros((1, HALF), f32)
    return jnp.concatenate([w[:, :HALF], w[:, HALF:], skel[:, :HALF], z, skel[:, HALF:], z], axis=0)


def unpack(p):
    w = jnp.concatenate([p[:VEC], p[VEC : 2 * VEC]], axis=1)
    skel = jnp.concatenate([p[2 * VEC : 2 * VEC + 3], p[2 * VEC + 4 : 2 * VEC + 7]], axis=1)
    return w, skel


def up_kernel(pts_hbm, chg_hbm, mor_hbm, skl_hbm, skb_hbm, srt_ref, pack_ref, *scratch):
    pts_ref, chg_ref, mor_ref, skl_ref, skb_ref, kh_ref, kl_ref, sems = scratch
    pairs = ((skl_hbm, skl_ref), (skb_hbm, skb_ref), (mor_hbm, mor_ref), (pts_hbm, pts_ref), (chg_hbm, chg_ref))
    copies = [pltpu.make_async_copy(src, dst, sems.at[i]) for i, (src, dst) in enumerate(pairs)]
    for c in copies:
        c.start()
    copies[0].wait()
    copies[1].wait()
    ft_block = feat_tgt(skb_ref[...])
    for q in range(LEAVES_DEV):
        col = slice(q * T, (q + 1) * T)
        kh, kl = tile(feat_src(skl_ref[:, col]), ft_block)
        kh_ref[col, :] = kh
        kl_ref[col, :] = kl
    for c in copies[2:]:
        c.wait()
    n = chg_ref.shape[1]
    rows = jnp.concatenate([chg_ref[...], pts_ref[...], jnp.zeros((5, n), f32)], axis=0)
    a, b, c = split3(rows)
    parts = jnp.concatenate([a, b, c], axis=0).astype(bf16)
    row = lax.broadcasted_iota(jnp.int32, (n, T), 0)
    sorts = []
    for q in range(LEAVES_DEV):
        col = slice(q * T, (q + 1) * T)
        hot = (row == mor_ref[:, col]).astype(f32).astype(bf16)
        s = dg(parts, hot, 1, 0)
        srt = s[:ROWS] + s[ROWS : 2 * ROWS] + s[2 * ROWS :]
        srt_ref[:, col] = srt
        sorts.append(s)
    total = jnp.zeros((VEC, T), f32)
    for q in range(LEAVES_DEV):
        col = slice(q * T, (q + 1) * T)
        s = sorts[q]
        vv = jnp.concatenate([s[:VEC], s[ROWS : ROWS + VEC] + s[2 * ROWS : 2 * ROWS + VEC]], axis=0).astype(bf16)
        lw = times(vv, tile(feat_src(srt_ref[VEC : VEC + 3, col]), feat_tgt(skl_ref[:, col])))
        total = total + times(stack2(gain(T) * lw), (kh_ref[col, :], kl_ref[col, :]))
    packed = pack(gain(LEAVES_DEV * T) * total, skb_ref[...])
    for z in range(pack_ref.shape[0]):
        pack_ref[z] = packed


def own_group(skg_ref):
    return skg_ref[:, pl.ds(pl.multiple_of(lax.axis_index("grp") * T, T), T)]


def raised(packs_ref, skg_ref):
    ft = feat_tgt(own_group(skg_ref))
    total = jnp.zeros((VEC, T), f32)
    for c in range(packs_ref.shape[0]):
        w, skel = unpack(packs_ref[c])
        total = total + times(stack2(w), tile(feat_src(skel), ft))
    return total


def group_kernel(part_ref, skg_ref, gw_ref):
    total = gain(4 * part_ref.shape[0] * T) * raised(part_ref, skg_ref)
    for g in range(gw_ref.shape[0]):
        gw_ref[g] = total


def first_leaf():
    pair = (lax.axis_index("grp") * lax.axis_size("z8") + lax.axis_index("z8")) * 2 + lax.axis_index("zp")
    return (pair * 2 + lax.axis_index("core")) * LEAVES_DEV


def leaf(ref, j):
    col = slice(j * T, (j + 1) * T)
    return ref[:VEC, col], ref[VEC : VEC + 3, col]


def slots(nbr_ref, cnt_ref):
    shape = nbr_ref.shape
    leaves = (shape[0], shape[0])
    diagonal = lax.broadcasted_iota(jnp.int32, leaves, 0) == lax.broadcasted_iota(jnp.int32, leaves, 1)
    count = jnp.sum(jnp.where(diagonal, cnt_ref[...].astype(f32), 0.0), axis=1, keepdims=True)
    used = lax.broadcasted_iota(jnp.int32, shape, 1).astype(f32) < count
    return jnp.where(used, nbr_ref[...], -(1 << 24))


def uses(table, source):
    return jnp.sum(jnp.where(table == source, 1.0, 0.0), axis=1, keepdims=True)


def side_near(table, blk_ref, on_right, fts, acc):
    first = first_leaf() + jnp.where(on_right, LEAVES_DEV, -LEAVES_DEV)
    for d in range(LEAVES_DEV):
        (v0, x0), (v1, x1) = leaf(blk_ref, d), leaf(blk_ref, LEAVES_DEV - 1 - d)
        v = jnp.where(on_right, v0, v1)
        fs = feat_src(jnp.where(on_right, x0, x1))
        source = first + jnp.where(on_right, d, LEAVES_DEV - 1 - d)
        m = uses(table, source)
        for e in range(d, LEAVES_DEV):
            q0, q1 = e, LEAVES_DEV - 1 - e
            times_used = jnp.where(on_right, m[q0 : q0 + 1], m[q1 : q1 + 1])
            r = times(stack2(times_used * v), tile(fs, jnp.where(on_right, fts[q0], fts[q1])))
            acc[q0] = acc[q0] + jnp.where(on_right, r, 0.0)
            acc[q1] = acc[q1] + jnp.where(on_right, 0.0, r)


def near_kernel(nbr_ref, cnt_ref, mid_ref, skb_ref, skl_ref, near_ref, mh_ref, ml_ref):
    first = first_leaf()
    table = slots(nbr_ref, cnt_ref)
    fts = [feat_tgt(leaf(mid_ref, q)[1]) for q in range(LEAVES_DEV)]
    fs_block = feat_src(skb_ref[...])
    for q in range(LEAVES_DEV):
        col = slice(q * T, (q + 1) * T)
        ah, al = tile(fs_block, feat_tgt(skl_ref[:, col]))
        bh, bl = tile(feat_src(skl_ref[:, col]), fts[q])
        both = dg(ah, bh, 1, 0) + dg(al, bh, 1, 0) + dg(ah, bl, 1, 0)
        mh_ref[:, col], ml_ref[:, col] = split2(gain(T) * gain(T) * both)
    acc = [jnp.zeros((VEC, T), f32) for _ in range(LEAVES_DEV)]
    for j in range(LEAVES_DEV):
        v, x = leaf(mid_ref, j)
        fs = feat_src(x)
        m = uses(table, first + j)
        for q in range(LEAVES_DEV):
            vv = stack2(v if j == q else m[q : q + 1] * v)
            acc[q] = acc[q] + times(vv, tile(fs, fts[q]))
    for q in range(LEAVES_DEV):
        near_ref[:, q * T : (q + 1) * T] = gain(T) * acc[q]


def peer_kernel(
    nbr_ref, cnt_ref, part_ref, other_ref, skb_ref, skp_ref, skg_ref, sib_ref, adj_ref, mid_ref, near_ref, *outs
):
    peer_ref, bh_ref, bl_ref, all_ref = outs
    n = part_ref.shape[0]
    ft_own = feat_tgt(skb_ref[...])
    ft_pair = feat_tgt(skp_ref[...])
    own = jnp.zeros((VEC, T), f32)
    pair = jnp.zeros((VEC, T), f32)
    for c in range(2 * n):
        w, skel = unpack((part_ref if c < n else other_ref)[c % n])
        fs = feat_src(skel)
        vv = stack2(w)
        pair = pair + times(vv, tile(fs, ft_pair))
        if c < n:
            vv = stack2(jnp.where(lax.axis_index("z8") == c, 0.0, 1.0) * w)
        own = own + times(vv, tile(fs, ft_own))
    peer_ref[0] = gain((4 * n - 1) * T) * own
    peer_ref[1] = gain((4 * n - 1) * T) * pair
    kh, kl = tile(feat_src(own_group(skg_ref)), ft_own)
    bh_ref[...] = kh
    bl_ref[...] = kl
    fts = [feat_tgt(leaf(mid_ref, q)[1]) for q in range(LEAVES_DEV)]
    acc = [jnp.zeros((VEC, T), f32) for _ in range(LEAVES_DEV)]
    table = slots(nbr_ref, cnt_ref)
    side_near(table, sib_ref, lax.axis_index("core") == 0, fts, acc)
    side_near(table, adj_ref, lax.axis_index("core") == 1, fts, acc)
    for q in range(LEAVES_DEV):
        col = slice(q * T, (q + 1) * T)
        all_ref[:, col] = near_ref[:, col] + gain(T) * acc[q]


def field_kernel(gws_ref, skg_ref, peer_ref, part_ref):
    n = gws_ref.shape[0]
    ft_own = feat_tgt(own_group(skg_ref))
    total = jnp.zeros((VEC, T), f32)
    for g in range(n):
        keep = jnp.where(lax.axis_index("grp") == g, 0.0, 1.0)
        col = slice(g * T, (g + 1) * T)
        total = total + times(stack2(keep * gws_ref[g]), tile(feat_src(skg_ref[:, col]), ft_own))
    part_ref[:VEC, :] = gain((n - 1) * T) * total
    part_ref[VEC:, :] = peer_ref[1]


def down_kernel(cell_ref, peer_ref, bh_ref, bl_ref, mh_ref, ml_ref, near_ref, out_ref):
    group = jnp.sum(cell_ref[:, :VEC, :], axis=0)
    field = gain(T) * times(stack2(group), (bh_ref[...], bl_ref[...]))
    field = field + peer_ref[0] + cell_ref[(1 - lax.axis_index("zp")) * 2 + lax.axis_index("core"), VEC:, :]
    out_ref[...] = near_ref[...] + times(stack2(field), (mh_ref[...], ml_ref[...]))


VM = pl.BlockSpec(memory_space=pltpu.VMEM)
SM = pl.BlockSpec(memory_space=pltpu.SMEM)


def shape(*dims, dtype=f32):
    return jax.ShapeDtypeStruct(dims, dtype)


def cost(tiles):
    return pl.CostEstimate(flops=tiles * 10**8, bytes_accessed=tiles * 2**18, transcendentals=tiles * T * T)


def kernel(fn, name, out, scalars, arrays, scratch=(), tiles=1):
    return pl.pallas_call(
        fn,
        out_shape=out,
        in_specs=[SM] * scalars + [VM] * arrays,
        out_specs=jax.tree.map(lambda _: VM, out),
        scratch_shapes=scratch,
        cost_estimate=cost(tiles),
        compiler_params=pltpu.CompilerParams(vmem_limit_bytes=24 << 20),
        name=name,
    )


def body(points, charges, morton, neighbours, counts, skel_leaf, skel_block, skel_group):
    n_groups = lax.axis_size("grp")
    n_z8 = lax.axis_size("z8")
    n = points.shape[1]
    axes = ("grp", "z8", "zp", "core")
    counts = counts.reshape(1, LEAVES_DEV)
    inputs = (points, charges, morton.reshape(1, n), skel_leaf, skel_block)
    srt, packed = pl.pallas_call(
        up_kernel,
        out_shape=(shape(ROWS, n), shape(n_z8, PACK, HALF)),
        in_specs=[pl.BlockSpec(memory_space=pltpu.HBM)] * 5,
        out_specs=(VM, VM),
        scratch_shapes=[pltpu.VMEM(x.shape, x.dtype) for x in inputs]
        + [pltpu.VMEM((n, T), bf16), pltpu.VMEM((n, T), bf16), pltpu.SemaphoreType.DMA((5,))],
        compiler_params=pltpu.CompilerParams(vmem_limit_bytes=60 << 20),
        name="up",
    )(*inputs)
    part = lax.all_to_all(packed, "z8", 0, 0, tiled=False)
    whole = n_groups * n_z8 * 4
    swap = [(0, 1), (1, 0)]
    sib = lax.ppermute(srt, "core", swap)
    operator = shape(T, n, dtype=bf16)
    near, mh, ml = kernel(near_kernel, "near", (shape(VEC, n), operator, operator), 0, 5, tiles=28)(
        neighbours, counts, srt, skel_block, skel_leaf
    )
    srt, near, mh, ml, skel = lax.optimization_barrier((srt, near, mh, ml, skel_block))
    pair_skel = lax.ppermute(skel, "zp", swap)
    odd = range(1, whole - 1, 2)
    adj = lax.ppermute(srt, axes, [(i, i + 1) for i in odd] + [(i + 1, i) for i in odd])
    part, near, mh, ml = lax.optimization_barrier((part, near, mh, ml))
    other = lax.ppermute(part, "core", swap)
    gw = kernel(group_kernel, "group", shape(n_groups, VEC, T), 0, 2, tiles=30)(part, skel_group)
    gws = lax.all_to_all(gw, "grp", 0, 0, tiled=False)
    square = shape(T, T, dtype=bf16)
    peer, bh, bl, near = kernel(peer_kernel, "peer", (shape(2, VEC, T), square, square, shape(VEC, n)), 0, 11, tiles=53)(
        neighbours, counts, part, other, skel_block, pair_skel, skel_group, sib, adj, srt, near
    )
    mine = kernel(field_kernel, "field", shape(2 * VEC, T), 0, 3, tiles=20)(gws, skel_group, peer)
    cell = lax.all_gather(mine, ("zp", "core"), axis=0, tiled=False)
    return kernel(down_kernel, "down", shape(VEC, n), 0, 7)(cell, peer, bh, bl, mh, ml, near)


def solution(mesh):
    fine = Mesh(mesh.devices.reshape(mesh.shape["grp"], mesh.shape["dev"] // 4, 2, 2), ("grp", "z8", "zp", "core"))
    all_axes = ("grp", "z8", "zp", "core")
    return jax.shard_map(
        body,
        mesh=fine,
        in_specs=(
            P(None, all_axes),
            P(None, all_axes),
            P(all_axes),
            P(all_axes, None),
            P(all_axes),
            P(None, all_axes),
            P(None, all_axes),
            P(),
        ),
        out_specs=P(None, all_axes),
        check_vma=False,
    )
```

```python
import math

import jax
import jax.numpy as jnp
from jax import lax
from jax.experimental import pallas as pl
from jax.experimental.pallas import tpu as pltpu
from jax.sharding import Mesh, PartitionSpec as P

f32 = jnp.float32
bf16 = jnp.bfloat16
width_sq = 0.1
gain_factor = 5.0
coord_scale = math.sqrt(math.log2(math.e) / width_sq)
VEC = 16
ROWS = 24
T = 256
LEAVES_DEV = 4
PACK = 40
HALF = 128


def dg(a, b, ca, cb):
    return lax.dot_general(a, b, (((ca,), (cb,)), ((), ())), preferred_element_type=f32)


def split2(v):
    h = v.astype(bf16)
    return h, (v - h.astype(f32)).astype(bf16)


def split3(v):
    a = v.astype(bf16).astype(f32)
    r = v - a
    b = r.astype(bf16).astype(f32)
    return a, b, r - b


def centred(x3):
    x = (x3 - 1.0) * coord_scale
    n = jnp.sum(x * x, axis=0, keepdims=True)
    return x, n, jnp.ones_like(n), jnp.zeros((3,) + n.shape[1:], f32)


def feat_src(x3):
    x, n, o, z = centred(x3)
    a, b, c = split3(jnp.concatenate([x, n, o, z], axis=0))
    return jnp.concatenate([a, a, a, b, b, c], axis=0).astype(bf16)


def feat_tgt(x3):
    x, n, o, z = centred(x3)
    a, b, c = split3(jnp.concatenate([2.0 * x, -o, -n, z], axis=0))
    return jnp.concatenate([a, b, c, a, b, a], axis=0).astype(bf16)


def tile(fs, ft):
    return split2(jnp.exp2(dg(fs, ft, 0, 0)))


def stack2(v):
    h, l = split2(v)
    return jnp.concatenate([h, l], axis=0)


def times(vv, kt):
    kh, kl = kt
    r = dg(vv, kh, 1, 0)
    return r[:VEC] + r[VEC:] + dg(vv[:VEC], kl, 1, 0)


def gain(count):
    return gain_factor / math.sqrt(count)


def pack(w, skel):
    z = jnp.zeros((1, HALF), f32)
    return jnp.concatenate([w[:, :HALF], w[:, HALF:], skel[:, :HALF], z, skel[:, HALF:], z], axis=0)


def unpack(p):
    w = jnp.concatenate([p[:VEC], p[VEC : 2 * VEC]], axis=1)
    skel = jnp.concatenate([p[2 * VEC : 2 * VEC + 3], p[2 * VEC + 4 : 2 * VEC + 7]], axis=1)
    return w, skel


def up_kernel(pts_hbm, chg_hbm, mor_hbm, skl_hbm, skb_hbm, srt_ref, pack_ref, *scratch):
    pts_ref, chg_ref, mor_ref, skl_ref, skb_ref, kh_ref, kl_ref, sems = scratch
    pairs = ((skl_hbm, skl_ref), (skb_hbm, skb_ref), (mor_hbm, mor_ref), (pts_hbm, pts_ref), (chg_hbm, chg_ref))
    copies = [pltpu.make_async_copy(src, dst, sems.at[i]) for i, (src, dst) in enumerate(pairs)]
    for c in copies:
        c.start()
    copies[0].wait()
    copies[1].wait()
    ft_block = feat_tgt(skb_ref[...])
    for q in range(LEAVES_DEV):
        col = slice(q * T, (q + 1) * T)
        kh, kl = tile(feat_src(skl_ref[:, col]), ft_block)
        kh_ref[col, :] = kh
        kl_ref[col, :] = kl
    for c in copies[2:]:
        c.wait()
    n = chg_ref.shape[1]
    rows = jnp.concatenate([chg_ref[...], pts_ref[...], jnp.zeros((5, n), f32)], axis=0)
    a, b, c = split3(rows)
    parts = jnp.concatenate([a, b, c], axis=0).astype(bf16)
    row = lax.broadcasted_iota(jnp.int16, (n, T), 0)
    cols = [slice(q * T, (q + 1) * T) for q in range(LEAVES_DEV)]
    hots = [jnp.where(row == mor_ref[:, col].astype(jnp.int16), bf16(1), bf16(0)) for col in cols]
    sums = [dg(parts, hot, 1, 0) for hot in hots]
    srts = [s[:ROWS] + s[ROWS : 2 * ROWS] + s[2 * ROWS :] for s in sums]
    srts[0] = jnp.concatenate([srts[0][: VEC + 3], skb_ref[...], srts[0][VEC + 6 :]], axis=0)
    for col, srt in zip(cols, srts):
        srt_ref[:, col] = srt
    sources = [feat_src(srt[VEC : VEC + 3]) for srt in srts]
    targets = [feat_tgt(skl_ref[:, col]) for col in cols]
    exponents = [dg(fs, ft, 0, 0) for fs, ft in zip(sources, targets)]
    tiles = [split2(jnp.exp2(e)) for e in exponents]
    splits = [(s[:VEC], s[ROWS : ROWS + VEC] + s[2 * ROWS : 2 * ROWS + VEC]) for s in sums]
    weights = [times(jnp.concatenate(hl, axis=0).astype(bf16), kt) for hl, kt in zip(splits, tiles)]
    total = jnp.zeros((VEC, T), f32)
    for col, lw in zip(cols, weights):
        total = total + times(stack2(gain(T) * lw), (kh_ref[col, :], kl_ref[col, :]))
    packed = pack(gain(LEAVES_DEV * T) * total, skb_ref[...])
    for z in range(pack_ref.shape[0]):
        pack_ref[z] = packed


def own_group(skg_ref):
    return skg_ref[:, pl.ds(pl.multiple_of(lax.axis_index("grp") * T, T), T)]


def raised(packs_ref, skg_ref):
    ft = feat_tgt(own_group(skg_ref))
    total = jnp.zeros((VEC, T), f32)
    for c in range(packs_ref.shape[0]):
        w, skel = unpack(packs_ref[c])
        total = total + times(stack2(w), tile(feat_src(skel), ft))
    return total


def group_kernel(part_ref, skg_ref, gw_ref):
    total = gain(4 * part_ref.shape[0] * T) * raised(part_ref, skg_ref)
    for g in range(gw_ref.shape[0]):
        gw_ref[g] = total


def first_leaf():
    pair = (lax.axis_index("grp") * lax.axis_size("z8") + lax.axis_index("z8")) * 2 + lax.axis_index("zp")
    return (pair * 2 + lax.axis_index("core")) * LEAVES_DEV


def leaf(ref, j):
    col = slice(j * T, (j + 1) * T)
    return ref[:VEC, col], ref[VEC : VEC + 3, col]


def slots(nbr_ref, cnt_ref):
    shape = nbr_ref.shape
    leaves = (shape[0], shape[0])
    diagonal = lax.broadcasted_iota(jnp.int32, leaves, 0) == lax.broadcasted_iota(jnp.int32, leaves, 1)
    count = jnp.sum(jnp.where(diagonal, cnt_ref[...].astype(f32), 0.0), axis=1, keepdims=True)
    used = lax.broadcasted_iota(jnp.int32, shape, 1).astype(f32) < count
    return jnp.where(used, nbr_ref[...], -(1 << 24))


def uses(table, source):
    return jnp.sum(jnp.where(table == source, 1.0, 0.0), axis=1, keepdims=True)


def side_near(table, blk_ref, on_right, fts, acc):
    first = first_leaf() + jnp.where(on_right, LEAVES_DEV, -LEAVES_DEV)
    for d in range(LEAVES_DEV):
        (v0, x0), (v1, x1) = leaf(blk_ref, d), leaf(blk_ref, LEAVES_DEV - 1 - d)
        v = jnp.where(on_right, v0, v1)
        fs = feat_src(jnp.where(on_right, x0, x1))
        source = first + jnp.where(on_right, d, LEAVES_DEV - 1 - d)
        m = uses(table, source)
        for e in range(d, LEAVES_DEV):
            q0, q1 = e, LEAVES_DEV - 1 - e
            times_used = jnp.where(on_right, m[q0 : q0 + 1], m[q1 : q1 + 1])
            r = times(stack2(times_used * v), tile(fs, jnp.where(on_right, fts[q0], fts[q1])))
            acc[q0] = acc[q0] + jnp.where(on_right, r, 0.0)
            acc[q1] = acc[q1] + jnp.where(on_right, 0.0, r)


def near_kernel(nbr_ref, cnt_ref, mid_ref, skb_ref, skl_ref, near_ref, mh_ref, ml_ref):
    first = first_leaf()
    table = slots(nbr_ref, cnt_ref)
    fts = [feat_tgt(leaf(mid_ref, q)[1]) for q in range(LEAVES_DEV)]
    fs_block = feat_src(skb_ref[...])
    for q in range(LEAVES_DEV):
        col = slice(q * T, (q + 1) * T)
        ah, al = tile(fs_block, feat_tgt(skl_ref[:, col]))
        bh, bl = tile(feat_src(skl_ref[:, col]), fts[q])
        both = dg(ah, bh, 1, 0) + dg(al, bh, 1, 0) + dg(ah, bl, 1, 0)
        mh_ref[:, col], ml_ref[:, col] = split2(gain(T) * gain(T) * both)
    acc = [jnp.zeros((VEC, T), f32) for _ in range(LEAVES_DEV)]
    for j in range(LEAVES_DEV):
        v, x = leaf(mid_ref, j)
        fs = feat_src(x)
        m = uses(table, first + j)
        for q in range(LEAVES_DEV):
            vv = stack2(v if j == q else m[q : q + 1] * v)
            acc[q] = acc[q] + times(vv, tile(fs, fts[q]))
    for q in range(LEAVES_DEV):
        near_ref[:, q * T : (q + 1) * T] = gain(T) * acc[q]


def peer_kernel(
    nbr_ref, cnt_ref, part_ref, other_ref, skb_ref, sibling_ref, skg_ref, adj_ref, mid_ref, near_ref, peer_ref, bh_ref, bl_ref, all_ref
):
    n = part_ref.shape[0]
    ft_own = feat_tgt(skb_ref[...])
    ft_sib = feat_tgt(sibling_ref[VEC + 3 : VEC + 6, :T])
    own = jnp.zeros((VEC, T), f32)
    sib = jnp.zeros((VEC, T), f32)
    for c in range(2 * n):
        w, skel = unpack((part_ref if c < n else other_ref)[c % n])
        fs = feat_src(skel)
        vv = stack2(w)
        sib = sib + times(vv, tile(fs, ft_sib))
        if c < n:
            vv = stack2(jnp.where(lax.axis_index("z8") == c, 0.0, 1.0) * w)
        own = own + times(vv, tile(fs, ft_own))
    peer_ref[0] = gain((4 * n - 1) * T) * own
    peer_ref[1] = gain((4 * n - 1) * T) * sib
    kh, kl = tile(feat_src(own_group(skg_ref)), ft_own)
    bh_ref[...] = kh
    bl_ref[...] = kl
    fts = [feat_tgt(leaf(mid_ref, q)[1]) for q in range(LEAVES_DEV)]
    acc = [jnp.zeros((VEC, T), f32) for _ in range(LEAVES_DEV)]
    table = slots(nbr_ref, cnt_ref)
    side_near(table, sibling_ref, lax.axis_index("core") == 0, fts, acc)
    side_near(table, adj_ref, lax.axis_index("core") == 1, fts, acc)
    for q in range(LEAVES_DEV):
        col = slice(q * T, (q + 1) * T)
        all_ref[:, col] = near_ref[:, col] + gain(T) * acc[q]


def field_kernel(gws_ref, skg_ref, peer_ref, part_ref):
    n = gws_ref.shape[0]
    ft_own = feat_tgt(own_group(skg_ref))
    total = jnp.zeros((VEC, T), f32)
    for g in range(n):
        keep = jnp.where(lax.axis_index("grp") == g, 0.0, 1.0)
        col = slice(g * T, (g + 1) * T)
        total = total + times(stack2(keep * gws_ref[g]), tile(feat_src(skg_ref[:, col]), ft_own))
    part_ref[:VEC, :] = gain((n - 1) * T) * total
    part_ref[VEC:, :] = peer_ref[1]


def down_kernel(cell_ref, peer_ref, bh_ref, bl_ref, mh_ref, ml_ref, near_ref, out_ref):
    group = jnp.sum(cell_ref[:, :VEC, :], axis=0)
    field = gain(T) * times(stack2(group), (bh_ref[...], bl_ref[...]))
    field = field + peer_ref[0] + cell_ref[lax.axis_index("zp") * 2 + 1 - lax.axis_index("core"), VEC:, :]
    out_ref[...] = near_ref[...] + times(stack2(field), (mh_ref[...], ml_ref[...]))


VM = pl.BlockSpec(memory_space=pltpu.VMEM)
SM = pl.BlockSpec(memory_space=pltpu.SMEM)


def shape(*dims, dtype=f32):
    return jax.ShapeDtypeStruct(dims, dtype)


def cost(tiles):
    return pl.CostEstimate(flops=tiles * 10**8, bytes_accessed=tiles * 2**18, transcendentals=tiles * T * T)


def kernel(fn, name, out, scalars, arrays, scratch=(), tiles=1):
    return pl.pallas_call(
        fn,
        out_shape=out,
        in_specs=[SM] * scalars + [VM] * arrays,
        out_specs=jax.tree.map(lambda _: VM, out),
        scratch_shapes=scratch,
        cost_estimate=cost(tiles),
        compiler_params=pltpu.CompilerParams(vmem_limit_bytes=24 << 20),
        name=name,
    )


def body(points, charges, morton, neighbours, counts, skel_leaf, skel_block, skel_group):
    n_groups = lax.axis_size("grp")
    n_z8 = lax.axis_size("z8")
    n = points.shape[1]
    axes = ("grp", "z8", "zp", "core")
    counts = counts.reshape(1, LEAVES_DEV)
    inputs = (points, charges, morton.reshape(1, n), skel_leaf, skel_block)
    srt, packed = pl.pallas_call(
        up_kernel,
        out_shape=(shape(ROWS, n), shape(n_z8, PACK, HALF)),
        in_specs=[pl.BlockSpec(memory_space=pltpu.HBM)] * 5,
        out_specs=(VM, VM),
        scratch_shapes=[pltpu.VMEM(x.shape, x.dtype) for x in inputs]
        + [pltpu.VMEM((n, T), bf16), pltpu.VMEM((n, T), bf16), pltpu.SemaphoreType.DMA((5,))],
        compiler_params=pltpu.CompilerParams(vmem_limit_bytes=60 << 20),
        name="up",
    )(*inputs)
    part = lax.all_to_all(packed, "z8", 0, 0, tiled=False)
    whole = n_groups * n_z8 * 4
    swap = [(0, 1), (1, 0)]
    sib = lax.ppermute(srt, "core", swap)
    operator = shape(T, n, dtype=bf16)
    near, mh, ml = kernel(near_kernel, "near", (shape(VEC, n), operator, operator), 0, 5, tiles=28)(
        neighbours, counts, srt, skel_block, skel_leaf
    )
    srt, near, mh, ml = lax.optimization_barrier((srt, near, mh, ml))
    odd = range(1, whole - 1, 2)
    adj = lax.ppermute(srt, axes, [(i, i + 1) for i in odd] + [(i + 1, i) for i in odd])
    part, near, mh, ml = lax.optimization_barrier((part, near, mh, ml))
    other = lax.ppermute(part, "zp", swap)
    gw = kernel(group_kernel, "group", shape(n_groups, VEC, T), 0, 2, tiles=30)(part, skel_group)
    gws = lax.all_to_all(gw, "grp", 0, 0, tiled=False)
    square = shape(T, T, dtype=bf16)
    peer, bh, bl, near = kernel(peer_kernel, "peer", (shape(2, VEC, T), square, square, shape(VEC, n)), 0, 10, tiles=53)(
        neighbours, counts, part, other, skel_block, sib, skel_group, adj, srt, near
    )
    mine = kernel(field_kernel, "field", shape(2 * VEC, T), 0, 3, tiles=20)(gws, skel_group, peer)
    cell = lax.all_gather(mine, ("zp", "core"), axis=0, tiled=False)
    return kernel(down_kernel, "down", shape(VEC, n), 0, 7)(cell, peer, bh, bl, mh, ml, near)


def solution(mesh):
    fine = Mesh(mesh.devices.reshape(mesh.shape["grp"], mesh.shape["dev"] // 4, 2, 2), ("grp", "z8", "zp", "core"))
    all_axes = ("grp", "z8", "zp", "core")
    return jax.shard_map(
        body,
        mesh=fine,
        in_specs=(
            P(None, all_axes),
            P(None, all_axes),
            P(all_axes),
            P(all_axes, None),
            P(all_axes),
            P(None, all_axes),
            P(None, all_axes),
            P(),
        ),
        out_specs=P(None, all_axes),
        check_vma=False,
    )
```

```python
import math

import jax
import jax.numpy as jnp
from jax import lax
from jax.experimental import pallas as pl
from jax.experimental.pallas import tpu as pltpu
from jax.sharding import Mesh, PartitionSpec as P

f32 = jnp.float32
bf16 = jnp.bfloat16
width_sq = 0.1
gain_factor = 5.0
coord_scale = math.sqrt(math.log2(math.e) / width_sq)
VEC = 16
ROWS = 24
T = 256
LEAVES_DEV = 4
PACK = 40
HALF = 128


def dg(a, b, ca, cb):
    return lax.dot_general(a, b, (((ca,), (cb,)), ((), ())), preferred_element_type=f32)


def split2(v):
    h = v.astype(bf16)
    return h, (v - h.astype(f32)).astype(bf16)


def split3(v):
    a = v.astype(bf16).astype(f32)
    r = v - a
    b = r.astype(bf16).astype(f32)
    return a, b, r - b


def centred(x3):
    x = (x3 - 1.0) * coord_scale
    n = jnp.sum(x * x, axis=0, keepdims=True)
    return x, n, jnp.ones_like(n), jnp.zeros((3,) + n.shape[1:], f32)


def feat_src(x3):
    x, n, o, z = centred(x3)
    a, b, c = split3(jnp.concatenate([x, n, o, z], axis=0))
    return jnp.concatenate([a, a, a, b, b, c], axis=0).astype(bf16)


def feat_tgt(x3):
    x, n, o, z = centred(x3)
    a, b, c = split3(jnp.concatenate([2.0 * x, -o, -n, z], axis=0))
    return jnp.concatenate([a, b, c, a, b, a], axis=0).astype(bf16)


def tile(fs, ft):
    return split2(jnp.exp2(dg(fs, ft, 0, 0)))


def stack2(v):
    h, l = split2(v)
    return jnp.concatenate([h, l], axis=0)


def times(vv, kt):
    kh, kl = kt
    r = dg(vv, kh, 1, 0)
    return r[:VEC] + r[VEC:] + dg(vv[:VEC], kl, 1, 0)


def gain(count):
    return gain_factor / math.sqrt(count)


def pack(w, skel):
    z = jnp.zeros((1, HALF), f32)
    return jnp.concatenate([w[:, :HALF], w[:, HALF:], skel[:, :HALF], z, skel[:, HALF:], z], axis=0)


def unpack(p):
    w = jnp.concatenate([p[:VEC], p[VEC : 2 * VEC]], axis=1)
    skel = jnp.concatenate([p[2 * VEC : 2 * VEC + 3], p[2 * VEC + 4 : 2 * VEC + 7]], axis=1)
    return w, skel


def up_kernel(pts_hbm, chg_hbm, mor_hbm, skl_hbm, skb_hbm, srt_ref, pack_ref, *scratch):
    pts_ref, chg_ref, mor_ref, skl_ref, skb_ref, kh_ref, kl_ref, sems = scratch
    pairs = ((skl_hbm, skl_ref), (skb_hbm, skb_ref), (mor_hbm, mor_ref), (pts_hbm, pts_ref), (chg_hbm, chg_ref))
    copies = [pltpu.make_async_copy(src, dst, sems.at[i]) for i, (src, dst) in enumerate(pairs)]
    for c in copies:
        c.start()
    copies[0].wait()
    copies[1].wait()
    ft_block = feat_tgt(skb_ref[...])
    for q in range(LEAVES_DEV):
        col = slice(q * T, (q + 1) * T)
        kh, kl = tile(feat_src(skl_ref[:, col]), ft_block)
        kh_ref[col, :] = kh
        kl_ref[col, :] = kl
    for c in copies[2:]:
        c.wait()
    n = chg_ref.shape[1]
    rows = jnp.concatenate([chg_ref[...], pts_ref[...], jnp.zeros((5, n), f32)], axis=0)
    a, b, c = split3(rows)
    parts = jnp.concatenate([a, b, c], axis=0).astype(bf16)
    row = lax.broadcasted_iota(jnp.int16, (n, T), 0)
    cols = [slice(q * T, (q + 1) * T) for q in range(LEAVES_DEV)]
    hots = [jnp.where(row == mor_ref[:, col].astype(jnp.int16), bf16(1), bf16(0)) for col in cols]
    sums = [dg(parts, hot, 1, 0) for hot in hots]
    srts = [s[:ROWS] + s[ROWS : 2 * ROWS] + s[2 * ROWS :] for s in sums]
    srts[0] = jnp.concatenate([srts[0][: VEC + 3], skb_ref[...], srts[0][VEC + 6 :]], axis=0)
    for col, srt in zip(cols, srts):
        srt_ref[:, col] = srt
    sources = [feat_src(srt[VEC : VEC + 3]) for srt in srts]
    targets = [feat_tgt(skl_ref[:, col]) for col in cols]
    exponents = [dg(fs, ft, 0, 0) for fs, ft in zip(sources, targets)]
    tiles = [split2(jnp.exp2(e)) for e in exponents]
    splits = [(s[:VEC], s[ROWS : ROWS + VEC] + s[2 * ROWS : 2 * ROWS + VEC]) for s in sums]
    weights = [times(jnp.concatenate(hl, axis=0).astype(bf16), kt) for hl, kt in zip(splits, tiles)]
    total = jnp.zeros((VEC, T), f32)
    for col, lw in zip(cols, weights):
        total = total + times(stack2(gain(T) * lw), (kh_ref[col, :], kl_ref[col, :]))
    packed = pack(gain(LEAVES_DEV * T) * total, skb_ref[...])
    for z in range(pack_ref.shape[0]):
        pack_ref[z] = packed


def own_group(skg_ref):
    return skg_ref[:, pl.ds(pl.multiple_of(lax.axis_index("grp") * T, T), T)]


def raised(packs_ref, skg_ref):
    ft = feat_tgt(own_group(skg_ref))
    total = jnp.zeros((VEC, T), f32)
    for c in range(packs_ref.shape[0]):
        w, skel = unpack(packs_ref[c])
        total = total + times(stack2(w), tile(feat_src(skel), ft))
    return total


def group_kernel(part_ref, skg_ref, gw_ref):
    total = gain(4 * part_ref.shape[0] * T) * raised(part_ref, skg_ref)
    for g in range(gw_ref.shape[0]):
        gw_ref[g] = total


def first_leaf():
    pair = (lax.axis_index("grp") * lax.axis_size("z8") + lax.axis_index("z8")) * 2 + lax.axis_index("zp")
    return (pair * 2 + lax.axis_index("core")) * LEAVES_DEV


def leaf(ref, j):
    col = slice(j * T, (j + 1) * T)
    return ref[:VEC, col], ref[VEC : VEC + 3, col]


def slots(nbr_ref, cnt_ref):
    shape = nbr_ref.shape
    leaves = (shape[0], shape[0])
    diagonal = lax.broadcasted_iota(jnp.int32, leaves, 0) == lax.broadcasted_iota(jnp.int32, leaves, 1)
    count = jnp.sum(jnp.where(diagonal, cnt_ref[...].astype(f32), 0.0), axis=1, keepdims=True)
    used = lax.broadcasted_iota(jnp.int32, shape, 1).astype(f32) < count
    return jnp.where(used, nbr_ref[...], -(1 << 24))


def uses(table, source):
    return jnp.sum(jnp.where(table == source, 1.0, 0.0), axis=1, keepdims=True)


def side_near(table, blk_ref, on_right, fts):
    first = first_leaf() + jnp.where(on_right, LEAVES_DEV, -LEAVES_DEV)
    targets = [jnp.where(on_right, fts[e], fts[LEAVES_DEV - 1 - e]) for e in range(LEAVES_DEV)]
    acc = [jnp.zeros((VEC, T), f32) for _ in range(LEAVES_DEV)]
    for d in range(LEAVES_DEV):
        (v0, x0), (v1, x1) = leaf(blk_ref, d), leaf(blk_ref, LEAVES_DEV - 1 - d)
        v = jnp.where(on_right, v0, v1)
        fs = feat_src(jnp.where(on_right, x0, x1))
        m = uses(table, first + jnp.where(on_right, d, LEAVES_DEV - 1 - d))
        for e in range(d, LEAVES_DEV):
            q0, q1 = e, LEAVES_DEV - 1 - e
            times_used = jnp.where(on_right, m[q0 : q0 + 1], m[q1 : q1 + 1])
            acc[e] = acc[e] + times(stack2(times_used * v), tile(fs, targets[e]))
    return acc


def near_kernel(nbr_ref, cnt_ref, mid_ref, skb_ref, skl_ref, near_ref, mh_ref, ml_ref):
    first = first_leaf()
    table = slots(nbr_ref, cnt_ref)
    leaves = range(LEAVES_DEV)
    cols = [slice(q * T, (q + 1) * T) for q in leaves]
    own = [leaf(mid_ref, q) for q in leaves]
    fts = [feat_tgt(x) for _, x in own]
    fss = [feat_src(x) for _, x in own]
    fs_block = feat_src(skb_ref[...])
    skl_t = [feat_tgt(skl_ref[:, col]) for col in cols]
    skl_s = [feat_src(skl_ref[:, col]) for col in cols]
    used = [uses(table, first + j) for j in leaves]
    lower = [tile(fs_block, ft) for ft in skl_t]
    spread = [tile(fs, ft) for fs, ft in zip(skl_s, fts)]
    operator = []
    for (ah, al), (bh, bl) in zip(lower, spread):
        both = dg(ah, bh, 1, 0) + dg(al, bh, 1, 0) + dg(ah, bl, 1, 0)
        operator.append(split2(gain(T) * gain(T) * both))
    acc = [jnp.zeros((VEC, T), f32) for _ in leaves]
    for j in leaves:
        v = own[j][0]
        tiles = [tile(fss[j], ft) for ft in fts]
        weighted = [stack2(v if j == q else used[j][q : q + 1] * v) for q in leaves]
        for q in leaves:
            acc[q] = acc[q] + times(weighted[q], tiles[q])
    for q, col in enumerate(cols):
        near_ref[:, col] = gain(T) * acc[q]
        mh_ref[:, col], ml_ref[:, col] = operator[q]


def peer_kernel(
    nbr_ref, cnt_ref, part_ref, other_ref, skb_ref, sibling_ref, skg_ref, adj_ref, mid_ref, near_ref, *outs
):
    peer_ref, bh_ref, bl_ref, all_ref = outs
    table = slots(nbr_ref, cnt_ref)
    fts = [feat_tgt(leaf(mid_ref, q)[1]) for q in range(LEAVES_DEV)]
    core0 = lax.axis_index("core") == 0
    sib_near = side_near(table, sibling_ref, core0, fts)
    adj_near = side_near(table, adj_ref, jnp.logical_not(core0), fts)
    for q in range(LEAVES_DEV):
        p = LEAVES_DEV - 1 - q
        total = jnp.where(core0, sib_near[q] + adj_near[p], sib_near[p] + adj_near[q])
        col = slice(q * T, (q + 1) * T)
        all_ref[:, col] = near_ref[:, col] + gain(T) * total
    n = part_ref.shape[0]
    ft_own = feat_tgt(skb_ref[...])
    ft_sib = feat_tgt(sibling_ref[VEC + 3 : VEC + 6, :T])
    own = jnp.zeros((VEC, T), f32)
    sib = jnp.zeros((VEC, T), f32)
    for c in range(2 * n):
        w, skel = unpack((part_ref if c < n else other_ref)[c % n])
        fs = feat_src(skel)
        vv = stack2(w)
        sib = sib + times(vv, tile(fs, ft_sib))
        if c < n:
            vv = stack2(jnp.where(lax.axis_index("z8") == c, 0.0, 1.0) * w)
        own = own + times(vv, tile(fs, ft_own))
    peer_ref[0] = gain((4 * n - 1) * T) * own
    peer_ref[1] = gain((4 * n - 1) * T) * sib
    kh, kl = tile(feat_src(own_group(skg_ref)), ft_own)
    bh_ref[...] = kh
    bl_ref[...] = kl


def field_kernel(gws_ref, skg_ref, peer_ref, part_ref):
    n = gws_ref.shape[0]
    ft_own = feat_tgt(own_group(skg_ref))
    total = jnp.zeros((VEC, T), f32)
    for g in range(n):
        keep = jnp.where(lax.axis_index("grp") == g, 0.0, 1.0)
        col = slice(g * T, (g + 1) * T)
        total = total + times(stack2(keep * gws_ref[g]), tile(feat_src(skg_ref[:, col]), ft_own))
    part_ref[:VEC, :] = gain((n - 1) * T) * total
    part_ref[VEC:, :] = peer_ref[1]


def down_kernel(cell_ref, peer_ref, bh_ref, bl_ref, mh_ref, ml_ref, near_ref, out_ref):
    group = jnp.sum(cell_ref[:, :VEC, :], axis=0)
    field = gain(T) * times(stack2(group), (bh_ref[...], bl_ref[...]))
    field = field + peer_ref[0] + cell_ref[lax.axis_index("zp") * 2 + 1 - lax.axis_index("core"), VEC:, :]
    out_ref[...] = near_ref[...] + times(stack2(field), (mh_ref[...], ml_ref[...]))


VM = pl.BlockSpec(memory_space=pltpu.VMEM)
SM = pl.BlockSpec(memory_space=pltpu.SMEM)


def shape(*dims, dtype=f32):
    return jax.ShapeDtypeStruct(dims, dtype)


def cost(tiles):
    return pl.CostEstimate(flops=tiles * 10**8, bytes_accessed=tiles * 2**18, transcendentals=tiles * T * T)


def kernel(fn, name, out, scalars, arrays, scratch=(), tiles=1):
    return pl.pallas_call(
        fn,
        out_shape=out,
        in_specs=[SM] * scalars + [VM] * arrays,
        out_specs=jax.tree.map(lambda _: VM, out),
        scratch_shapes=scratch,
        cost_estimate=cost(tiles),
        compiler_params=pltpu.CompilerParams(vmem_limit_bytes=24 << 20),
        name=name,
    )


def body(points, charges, morton, neighbours, counts, skel_leaf, skel_block, skel_group):
    n_groups = lax.axis_size("grp")
    n_z8 = lax.axis_size("z8")
    n = points.shape[1]
    axes = ("grp", "z8", "zp", "core")
    counts = counts.reshape(1, LEAVES_DEV)
    inputs = (points, charges, morton.reshape(1, n), skel_leaf, skel_block)
    srt, packed = pl.pallas_call(
        up_kernel,
        out_shape=(shape(ROWS, n), shape(n_z8, PACK, HALF)),
        in_specs=[pl.BlockSpec(memory_space=pltpu.HBM)] * 5,
        out_specs=(VM, VM),
        scratch_shapes=[pltpu.VMEM(x.shape, x.dtype) for x in inputs]
        + [pltpu.VMEM((n, T), bf16), pltpu.VMEM((n, T), bf16), pltpu.SemaphoreType.DMA((5,))],
        compiler_params=pltpu.CompilerParams(vmem_limit_bytes=60 << 20),
        name="up",
    )(*inputs)
    part = lax.all_to_all(packed, "z8", 0, 0, tiled=False)
    whole = n_groups * n_z8 * 4
    swap = [(0, 1), (1, 0)]
    sib = lax.ppermute(srt, "core", swap)
    operator = shape(T, n, dtype=bf16)
    near, mh, ml = kernel(near_kernel, "near", (shape(VEC, n), operator, operator), 0, 5, tiles=28)(
        neighbours, counts, srt, skel_block, skel_leaf
    )
    srt, near, mh, ml = lax.optimization_barrier((srt, near, mh, ml))
    odd = range(1, whole - 1, 2)
    adj = lax.ppermute(srt, axes, [(i, i + 1) for i in odd] + [(i + 1, i) for i in odd])
    part, near, mh, ml = lax.optimization_barrier((part, near, mh, ml))
    other = lax.ppermute(part, "zp", swap)
    gw = kernel(group_kernel, "group", shape(n_groups, VEC, T), 0, 2, tiles=30)(part, skel_group)
    gws = lax.all_to_all(gw, "grp", 0, 0, tiled=False)
    square = shape(T, T, dtype=bf16)
    peer, bh, bl, near = kernel(peer_kernel, "peer", (shape(2, VEC, T), square, square, shape(VEC, n)), 0, 10, tiles=53)(
        neighbours, counts, part, other, skel_block, sib, skel_group, adj, srt, near
    )
    mine = kernel(field_kernel, "field", shape(2 * VEC, T), 0, 3, tiles=20)(gws, skel_group, peer)
    cell = lax.all_gather(mine, ("zp", "core"), axis=0, tiled=False)
    return kernel(down_kernel, "down", shape(VEC, n), 0, 7)(cell, peer, bh, bl, mh, ml, near)


def solution(mesh):
    fine = Mesh(mesh.devices.reshape(mesh.shape["grp"], mesh.shape["dev"] // 4, 2, 2), ("grp", "z8", "zp", "core"))
    all_axes = ("grp", "z8", "zp", "core")
    return jax.shard_map(
        body,
        mesh=fine,
        in_specs=(
            P(None, all_axes),
            P(None, all_axes),
            P(all_axes),
            P(all_axes, None),
            P(all_axes),
            P(None, all_axes),
            P(None, all_axes),
            P(),
        ),
        out_specs=P(None, all_axes),
        check_vma=False,
    )
```

```python
import math

import jax
import jax.numpy as jnp
from jax import lax
from jax.experimental import pallas as pl
from jax.experimental.pallas import tpu as pltpu
from jax.sharding import Mesh, PartitionSpec as P

f32 = jnp.float32
bf16 = jnp.bfloat16
width_sq = 0.1
gain_factor = 5.0
coord_scale = math.sqrt(math.log2(math.e) / width_sq)
VEC = 16
ROWS = 24
T = 256
LEAVES_DEV = 4
PACK = 40
HALF = 128


def dg(a, b, ca, cb):
    return lax.dot_general(a, b, (((ca,), (cb,)), ((), ())), preferred_element_type=f32)


def split2(v):
    h = v.astype(bf16)
    return h, (v - h.astype(f32)).astype(bf16)


def split3(v):
    a = v.astype(bf16).astype(f32)
    r = v - a
    b = r.astype(bf16).astype(f32)
    return a, b, r - b


def centred(x3):
    x = (x3 - 1.0) * coord_scale
    n = jnp.sum(x * x, axis=0, keepdims=True)
    return x, n, jnp.ones_like(n), jnp.zeros((3,) + n.shape[1:], f32)


def feat_src(x3):
    x, n, o, z = centred(x3)
    a, b, c = split3(jnp.concatenate([x, n, o, z], axis=0))
    return jnp.concatenate([a, a, a, b, b, c], axis=0).astype(bf16)


def feat_tgt(x3):
    x, n, o, z = centred(x3)
    a, b, c = split3(jnp.concatenate([2.0 * x, -o, -n, z], axis=0))
    return jnp.concatenate([a, b, c, a, b, a], axis=0).astype(bf16)


def tile(fs, ft):
    return split2(jnp.exp2(dg(fs, ft, 0, 0)))


def stack2(v):
    h, l = split2(v)
    return jnp.concatenate([h, l], axis=0)


def times(vv, kt):
    kh, kl = kt
    r = dg(vv, kh, 1, 0)
    return r[:VEC] + r[VEC:] + dg(vv[:VEC], kl, 1, 0)


def gain(count):
    return gain_factor / math.sqrt(count)


def pack(w, skel):
    z = jnp.zeros((1, HALF), f32)
    return jnp.concatenate([w[:, :HALF], w[:, HALF:], skel[:, :HALF], z, skel[:, HALF:], z], axis=0)


def unpack(p):
    w = jnp.concatenate([p[:VEC], p[VEC : 2 * VEC]], axis=1)
    skel = jnp.concatenate([p[2 * VEC : 2 * VEC + 3], p[2 * VEC + 4 : 2 * VEC + 7]], axis=1)
    return w, skel


def up_kernel(pts_hbm, chg_hbm, mor_hbm, skl_hbm, skb_hbm, srt_ref, pack_ref, *scratch):
    pts_ref, chg_ref, mor_ref, skl_ref, skb_ref, kh_ref, kl_ref, sems = scratch
    pairs = ((skl_hbm, skl_ref), (skb_hbm, skb_ref), (mor_hbm, mor_ref), (pts_hbm, pts_ref), (chg_hbm, chg_ref))
    copies = [pltpu.make_async_copy(src, dst, sems.at[i]) for i, (src, dst) in enumerate(pairs)]
    for c in copies:
        c.start()
    copies[0].wait()
    copies[1].wait()
    ft_block = feat_tgt(skb_ref[...])
    for q in range(LEAVES_DEV):
        col = slice(q * T, (q + 1) * T)
        kh, kl = tile(feat_src(skl_ref[:, col]), ft_block)
        kh_ref[col, :] = kh
        kl_ref[col, :] = kl
    for c in copies[2:]:
        c.wait()
    n = chg_ref.shape[1]
    rows = jnp.concatenate([chg_ref[...], pts_ref[...], jnp.zeros((5, n), f32)], axis=0)
    a, b, c = split3(rows)
    parts = jnp.concatenate([a, b, c], axis=0).astype(bf16)
    row = lax.broadcasted_iota(jnp.int16, (n, T), 0)
    cols = [slice(q * T, (q + 1) * T) for q in range(LEAVES_DEV)]
    hots = [jnp.where(row == mor_ref[:, col].astype(jnp.int16), bf16(1), bf16(0)) for col in cols]
    sums = [dg(parts, hot, 1, 0) for hot in hots]
    srts = [s[:ROWS] + s[ROWS : 2 * ROWS] + s[2 * ROWS :] for s in sums]
    for c in range(2):
        low, high = srts[c], srts[2 + c]
        last = skb_ref[2:3, :] if c == 0 else jnp.zeros((1, T), f32)
        srt_ref[:VEC, cols[c]] = low[:VEC]
        srt_ref[VEC : 2 * VEC, cols[c]] = high[:VEC]
        rest = [low[VEC : VEC + 3], skb_ref[c : c + 1, :], high[VEC : VEC + 3], last]
        srt_ref[2 * VEC :, cols[c]] = jnp.concatenate(rest, axis=0)
    sources = [feat_src(srt[VEC : VEC + 3]) for srt in srts]
    targets = [feat_tgt(skl_ref[:, col]) for col in cols]
    exponents = [dg(fs, ft, 0, 0) for fs, ft in zip(sources, targets)]
    tiles = [split2(jnp.exp2(e)) for e in exponents]
    splits = [(s[:VEC], s[ROWS : ROWS + VEC] + s[2 * ROWS : 2 * ROWS + VEC]) for s in sums]
    weights = [times(jnp.concatenate(hl, axis=0).astype(bf16), kt) for hl, kt in zip(splits, tiles)]
    total = jnp.zeros((VEC, T), f32)
    for col, lw in zip(cols, weights):
        total = total + times(stack2(gain(T) * lw), (kh_ref[col, :], kl_ref[col, :]))
    packed = pack(gain(LEAVES_DEV * T) * total, skb_ref[...])
    for z in range(pack_ref.shape[0]):
        pack_ref[z] = packed


def own_group(skg_ref):
    return skg_ref[:, pl.ds(pl.multiple_of(lax.axis_index("grp") * T, T), T)]


def raised(packs_ref, skg_ref):
    ft = feat_tgt(own_group(skg_ref))
    total = jnp.zeros((VEC, T), f32)
    for c in range(packs_ref.shape[0]):
        w, skel = unpack(packs_ref[c])
        total = total + times(stack2(w), tile(feat_src(skel), ft))
    return total


def group_kernel(part_ref, skg_ref, gw_ref):
    total = gain(4 * part_ref.shape[0] * T) * raised(part_ref, skg_ref)
    for g in range(gw_ref.shape[0]):
        gw_ref[g] = total


def first_leaf():
    pair = (lax.axis_index("grp") * lax.axis_size("z8") + lax.axis_index("z8")) * 2 + lax.axis_index("zp")
    return (pair * 2 + lax.axis_index("core")) * LEAVES_DEV


def leaf(ref, j):
    half, side = j // 2, j % 2
    col = slice(side * T, (side + 1) * T)
    point = 2 * VEC + 4 * half
    return ref[half * VEC : (half + 1) * VEC, col], ref[point : point + 3, col]


def slots(nbr_ref, cnt_ref):
    shape = nbr_ref.shape
    leaves = (shape[0], shape[0])
    diagonal = lax.broadcasted_iota(jnp.int32, leaves, 0) == lax.broadcasted_iota(jnp.int32, leaves, 1)
    count = jnp.sum(jnp.where(diagonal, cnt_ref[...].astype(f32), 0.0), axis=1, keepdims=True)
    used = lax.broadcasted_iota(jnp.int32, shape, 1).astype(f32) < count
    return jnp.where(used, nbr_ref[...], -(1 << 24))


def uses(table, source):
    return jnp.sum(jnp.where(table == source, 1.0, 0.0), axis=1, keepdims=True)


def side_near(table, blk_ref, on_right, fts, acc):
    first = first_leaf() + jnp.where(on_right, LEAVES_DEV, -LEAVES_DEV)
    for d in range(LEAVES_DEV):
        (v0, x0), (v1, x1) = leaf(blk_ref, d), leaf(blk_ref, LEAVES_DEV - 1 - d)
        v = jnp.where(on_right, v0, v1)
        fs = feat_src(jnp.where(on_right, x0, x1))
        source = first + jnp.where(on_right, d, LEAVES_DEV - 1 - d)
        m = uses(table, source)
        for e in range(d, LEAVES_DEV):
            q0, q1 = e, LEAVES_DEV - 1 - e
            times_used = jnp.where(on_right, m[q0 : q0 + 1], m[q1 : q1 + 1])
            r = times(stack2(times_used * v), tile(fs, jnp.where(on_right, fts[q0], fts[q1])))
            acc[q0] = acc[q0] + jnp.where(on_right, r, 0.0)
            acc[q1] = acc[q1] + jnp.where(on_right, 0.0, r)


def near_kernel(nbr_ref, cnt_ref, mid_ref, skb_ref, skl_ref, near_ref, mh_ref, ml_ref):
    first = first_leaf()
    table = slots(nbr_ref, cnt_ref)
    fts = [feat_tgt(leaf(mid_ref, q)[1]) for q in range(LEAVES_DEV)]
    fs_block = feat_src(skb_ref[...])
    for q in range(LEAVES_DEV):
        col = slice(q * T, (q + 1) * T)
        ah, al = tile(fs_block, feat_tgt(skl_ref[:, col]))
        bh, bl = tile(feat_src(skl_ref[:, col]), fts[q])
        both = dg(ah, bh, 1, 0) + dg(al, bh, 1, 0) + dg(ah, bl, 1, 0)
        mh_ref[:, col], ml_ref[:, col] = split2(gain(T) * gain(T) * both)
    acc = [jnp.zeros((VEC, T), f32) for _ in range(LEAVES_DEV)]
    for j in range(LEAVES_DEV):
        v, x = leaf(mid_ref, j)
        fs = feat_src(x)
        m = uses(table, first + j)
        for q in range(LEAVES_DEV):
            vv = stack2(v if j == q else m[q : q + 1] * v)
            acc[q] = acc[q] + times(vv, tile(fs, fts[q]))
    for q in range(LEAVES_DEV):
        near_ref[:, q * T : (q + 1) * T] = gain(T) * acc[q]


def peer_kernel(
    nbr_ref, cnt_ref, part_ref, other_ref, skb_ref, sibling_ref, skg_ref, adj_ref, mid_ref, near_ref, peer_ref, bh_ref, bl_ref, all_ref
):
    n = part_ref.shape[0]
    ft_own = feat_tgt(skb_ref[...])
    x, y, z = sibling_ref[35:36, :T], sibling_ref[35:36, T:], sibling_ref[39:40, :T]
    ft_sib = feat_tgt(jnp.concatenate([x, y, z], axis=0))
    own = jnp.zeros((VEC, T), f32)
    sib = jnp.zeros((VEC, T), f32)
    for c in range(2 * n):
        w, skel = unpack((part_ref if c < n else other_ref)[c % n])
        fs = feat_src(skel)
        vv = stack2(w)
        sib = sib + times(vv, tile(fs, ft_sib))
        if c < n:
            vv = stack2(jnp.where(lax.axis_index("z8") == c, 0.0, 1.0) * w)
        own = own + times(vv, tile(fs, ft_own))
    peer_ref[0] = gain((4 * n - 1) * T) * own
    peer_ref[1] = gain((4 * n - 1) * T) * sib
    kh, kl = tile(feat_src(own_group(skg_ref)), ft_own)
    bh_ref[...] = kh
    bl_ref[...] = kl
    fts = [feat_tgt(leaf(mid_ref, q)[1]) for q in range(LEAVES_DEV)]
    acc = [jnp.zeros((VEC, T), f32) for _ in range(LEAVES_DEV)]
    table = slots(nbr_ref, cnt_ref)
    side_near(table, sibling_ref, lax.axis_index("core") == 0, fts, acc)
    side_near(table, adj_ref, lax.axis_index("core") == 1, fts, acc)
    for q in range(LEAVES_DEV):
        col = slice(q * T, (q + 1) * T)
        all_ref[:, col] = near_ref[:, col] + gain(T) * acc[q]


def field_kernel(gws_ref, skg_ref, peer_ref, part_ref):
    n = gws_ref.shape[0]
    ft_own = feat_tgt(own_group(skg_ref))
    total = jnp.zeros((VEC, T), f32)
    for g in range(n):
        keep = jnp.where(lax.axis_index("grp") == g, 0.0, 1.0)
        col = slice(g * T, (g + 1) * T)
        total = total + times(stack2(keep * gws_ref[g]), tile(feat_src(skg_ref[:, col]), ft_own))
    part_ref[:VEC, :] = gain((n - 1) * T) * total
    part_ref[VEC:, :] = peer_ref[1]


def down_kernel(cell_ref, peer_ref, bh_ref, bl_ref, mh_ref, ml_ref, near_ref, out_ref):
    group = jnp.sum(cell_ref[:, :VEC, :], axis=0)
    field = gain(T) * times(stack2(group), (bh_ref[...], bl_ref[...]))
    field = field + peer_ref[0] + cell_ref[lax.axis_index("zp") * 2 + 1 - lax.axis_index("core"), VEC:, :]
    out_ref[...] = near_ref[...] + times(stack2(field), (mh_ref[...], ml_ref[...]))


VM = pl.BlockSpec(memory_space=pltpu.VMEM)
SM = pl.BlockSpec(memory_space=pltpu.SMEM)


def shape(*dims, dtype=f32):
    return jax.ShapeDtypeStruct(dims, dtype)


def cost(tiles):
    return pl.CostEstimate(flops=tiles * 10**8, bytes_accessed=tiles * 2**18, transcendentals=tiles * T * T)


def kernel(fn, name, out, scalars, arrays, scratch=(), tiles=1):
    return pl.pallas_call(
        fn,
        out_shape=out,
        in_specs=[SM] * scalars + [VM] * arrays,
        out_specs=jax.tree.map(lambda _: VM, out),
        scratch_shapes=scratch,
        cost_estimate=cost(tiles),
        compiler_params=pltpu.CompilerParams(vmem_limit_bytes=24 << 20),
        name=name,
    )


def body(points, charges, morton, neighbours, counts, skel_leaf, skel_block, skel_group):
    n_groups = lax.axis_size("grp")
    n_z8 = lax.axis_size("z8")
    n = points.shape[1]
    axes = ("grp", "z8", "zp", "core")
    counts = counts.reshape(1, LEAVES_DEV)
    inputs = (points, charges, morton.reshape(1, n), skel_leaf, skel_block)
    srt, packed = pl.pallas_call(
        up_kernel,
        out_shape=(shape(PACK, n // 2), shape(n_z8, PACK, HALF)),
        in_specs=[pl.BlockSpec(memory_space=pltpu.HBM)] * 5,
        out_specs=(VM, VM),
        scratch_shapes=[pltpu.VMEM(x.shape, x.dtype) for x in inputs]
        + [pltpu.VMEM((n, T), bf16), pltpu.VMEM((n, T), bf16), pltpu.SemaphoreType.DMA((5,))],
        compiler_params=pltpu.CompilerParams(vmem_limit_bytes=60 << 20),
        name="up",
    )(*inputs)
    part = lax.all_to_all(packed, "z8", 0, 0, tiled=False)
    whole = n_groups * n_z8 * 4
    swap = [(0, 1), (1, 0)]
    sib = lax.ppermute(srt, "core", swap)
    operator = shape(T, n, dtype=bf16)
    near, mh, ml = kernel(near_kernel, "near", (shape(VEC, n), operator, operator), 0, 5, tiles=28)(
        neighbours, counts, srt, skel_block, skel_leaf
    )
    srt, near, mh, ml = lax.optimization_barrier((srt, near, mh, ml))
    odd = range(1, whole - 1, 2)
    adj = lax.ppermute(srt, axes, [(i, i + 1) for i in odd] + [(i + 1, i) for i in odd])
    part, near, mh, ml = lax.optimization_barrier((part, near, mh, ml))
    other = lax.ppermute(part, "zp", swap)
    gw = kernel(group_kernel, "group", shape(n_groups, VEC, T), 0, 2, tiles=30)(part, skel_group)
    gws = lax.all_to_all(gw, "grp", 0, 0, tiled=False)
    square = shape(T, T, dtype=bf16)
    peer, bh, bl, near = kernel(peer_kernel, "peer", (shape(2, VEC, T), square, square, shape(VEC, n)), 0, 10, tiles=53)(
        neighbours, counts, part, other, skel_block, sib, skel_group, adj, srt, near
    )
    mine = kernel(field_kernel, "field", shape(2 * VEC, T), 0, 3, tiles=20)(gws, skel_group, peer)
    cell = lax.all_gather(mine, ("zp", "core"), axis=0, tiled=False)
    return kernel(down_kernel, "down", shape(VEC, n), 0, 7)(cell, peer, bh, bl, mh, ml, near)


def solution(mesh):
    fine = Mesh(mesh.devices.reshape(mesh.shape["grp"], mesh.shape["dev"] // 4, 2, 2), ("grp", "z8", "zp", "core"))
    all_axes = ("grp", "z8", "zp", "core")
    return jax.shard_map(
        body,
        mesh=fine,
        in_specs=(
            P(None, all_axes),
            P(None, all_axes),
            P(all_axes),
            P(all_axes, None),
            P(all_axes),
            P(None, all_axes),
            P(None, all_axes),
            P(),
        ),
        out_specs=P(None, all_axes),
        check_vma=False,
    )
```

```python
import math

import jax
import jax.numpy as jnp
from jax import lax
from jax.experimental import pallas as pl
from jax.experimental.pallas import tpu as pltpu
from jax.sharding import Mesh, PartitionSpec as P

f32 = jnp.float32
bf16 = jnp.bfloat16
width_sq = 0.1
gain_factor = 5.0
coord_scale = math.sqrt(math.log2(math.e) / width_sq)
VEC = 16
ROWS = 24
T = 256
LEAVES_DEV = 4
PACK = 40
HALF = 128


def dg(a, b, ca, cb):
    return lax.dot_general(a, b, (((ca,), (cb,)), ((), ())), preferred_element_type=f32)


def split2(v):
    h = v.astype(bf16)
    return h, (v - h.astype(f32)).astype(bf16)


def split3(v):
    a = v.astype(bf16).astype(f32)
    r = v - a
    b = r.astype(bf16).astype(f32)
    return a, b, r - b


def centred(x3):
    x = (x3 - 1.0) * coord_scale
    n = jnp.sum(x * x, axis=0, keepdims=True)
    return x, n, jnp.ones_like(n), jnp.zeros((3,) + n.shape[1:], f32)


def feat_src(x3):
    x, n, o, z = centred(x3)
    a, b, c = split3(jnp.concatenate([x, n, o, z], axis=0))
    return jnp.concatenate([a, a, a, b, b, c], axis=0).astype(bf16)


def feat_tgt(x3):
    x, n, o, z = centred(x3)
    a, b, c = split3(jnp.concatenate([2.0 * x, -o, -n, z], axis=0))
    return jnp.concatenate([a, b, c, a, b, a], axis=0).astype(bf16)


def tile(fs, ft):
    return split2(jnp.exp2(dg(fs, ft, 0, 0)))


def stack2(v):
    h, l = split2(v)
    return jnp.concatenate([h, l], axis=0)


def times(vv, kt):
    kh, kl = kt
    r = dg(vv, kh, 1, 0)
    return r[:VEC] + r[VEC:] + dg(vv[:VEC], kl, 1, 0)


def gain(count):
    return gain_factor / math.sqrt(count)


def pack(w, skel):
    z = jnp.zeros((1, HALF), f32)
    return jnp.concatenate([w[:, :HALF], w[:, HALF:], skel[:, :HALF], z, skel[:, HALF:], z], axis=0)


def unpack(p):
    w = jnp.concatenate([p[:VEC], p[VEC : 2 * VEC]], axis=1)
    skel = jnp.concatenate([p[2 * VEC : 2 * VEC + 3], p[2 * VEC + 4 : 2 * VEC + 7]], axis=1)
    return w, skel


def up_kernel(pts_hbm, chg_hbm, mor_hbm, skl_hbm, skb_hbm, srt_ref, pack_ref, *scratch):
    pts_ref, chg_ref, mor_ref, skl_ref, skb_ref, kh_ref, kl_ref, sems = scratch
    pairs = ((skl_hbm, skl_ref), (skb_hbm, skb_ref), (mor_hbm, mor_ref), (pts_hbm, pts_ref), (chg_hbm, chg_ref))
    copies = [pltpu.make_async_copy(src, dst, sems.at[i]) for i, (src, dst) in enumerate(pairs)]
    for c in copies:
        c.start()
    copies[0].wait()
    copies[1].wait()
    ft_block = feat_tgt(skb_ref[...])
    for q in range(LEAVES_DEV):
        col = slice(q * T, (q + 1) * T)
        kh, kl = tile(feat_src(skl_ref[:, col]), ft_block)
        kh_ref[col, :] = kh
        kl_ref[col, :] = kl
    for c in copies[2:]:
        c.wait()
    n = chg_ref.shape[1]
    rows = jnp.concatenate([chg_ref[...], pts_ref[...], jnp.zeros((5, n), f32)], axis=0)
    a, b, c = split3(rows)
    parts = jnp.concatenate([a, b, c], axis=0).astype(bf16)
    row = lax.broadcasted_iota(jnp.int16, (n, T), 0)
    cols = [slice(q * T, (q + 1) * T) for q in range(LEAVES_DEV)]
    hots = [jnp.where(row == mor_ref[:, col].astype(jnp.int16), bf16(1), bf16(0)) for col in cols]
    sums = [dg(parts, hot, 1, 0) for hot in hots]
    srts = [s[:ROWS] + s[ROWS : 2 * ROWS] + s[2 * ROWS :] for s in sums]
    srts[0] = jnp.concatenate([srts[0][: VEC + 3], skb_ref[...], srts[0][VEC + 6 :]], axis=0)
    for col, srt in zip(cols, srts):
        srt_ref[:, col] = srt
    sources = [feat_src(srt[VEC : VEC + 3]) for srt in srts]
    targets = [feat_tgt(skl_ref[:, col]) for col in cols]
    exponents = [dg(fs, ft, 0, 0) for fs, ft in zip(sources, targets)]
    tiles = [split2(jnp.exp2(e)) for e in exponents]
    splits = [(s[:VEC], s[ROWS : ROWS + VEC] + s[2 * ROWS : 2 * ROWS + VEC]) for s in sums]
    weights = [times(jnp.concatenate(hl, axis=0).astype(bf16), kt) for hl, kt in zip(splits, tiles)]
    total = jnp.zeros((VEC, T), f32)
    for col, lw in zip(cols, weights):
        total = total + times(stack2(gain(T) * lw), (kh_ref[col, :], kl_ref[col, :]))
    packed = pack(gain(LEAVES_DEV * T) * total, skb_ref[...])
    for z in range(pack_ref.shape[0]):
        pack_ref[z] = packed


def own_group(skg_ref):
    return skg_ref[:, pl.ds(pl.multiple_of(lax.axis_index("grp") * T, T), T)]


def raised(packs_ref, skg_ref):
    ft = feat_tgt(own_group(skg_ref))
    total = jnp.zeros((VEC, T), f32)
    for c in range(packs_ref.shape[0]):
        w, skel = unpack(packs_ref[c])
        total = total + times(stack2(w), tile(feat_src(skel), ft))
    return total


def group_kernel(part_ref, skg_ref, gw_ref):
    total = gain(4 * part_ref.shape[0] * T) * raised(part_ref, skg_ref)
    for g in range(gw_ref.shape[0]):
        gw_ref[g] = total


def first_leaf():
    pair = (lax.axis_index("grp") * lax.axis_size("z8") + lax.axis_index("z8")) * 2 + lax.axis_index("zp")
    return (pair * 2 + lax.axis_index("core")) * LEAVES_DEV


def leaf(ref, j):
    col = slice(j * T, (j + 1) * T)
    return ref[:VEC, col], ref[VEC : VEC + 3, col]


def slots(nbr_ref, cnt_ref):
    shape = nbr_ref.shape
    leaves = (shape[0], shape[0])
    diagonal = lax.broadcasted_iota(jnp.int32, leaves, 0) == lax.broadcasted_iota(jnp.int32, leaves, 1)
    count = jnp.sum(jnp.where(diagonal, cnt_ref[...].astype(f32), 0.0), axis=1, keepdims=True)
    used = lax.broadcasted_iota(jnp.int32, shape, 1).astype(f32) < count
    return jnp.where(used, nbr_ref[...], -(1 << 24))


def uses(table, source):
    return jnp.sum(jnp.where(table == source, 1.0, 0.0), axis=1, keepdims=True)


def side_near(table, blk_ref, on_right, fts):
    first = first_leaf() + jnp.where(on_right, LEAVES_DEV, -LEAVES_DEV)
    targets = [jnp.where(on_right, fts[e], fts[LEAVES_DEV - 1 - e]) for e in range(LEAVES_DEV)]
    acc = [jnp.zeros((VEC, T), f32) for _ in range(LEAVES_DEV)]
    for d in range(LEAVES_DEV):
        (v0, x0), (v1, x1) = leaf(blk_ref, d), leaf(blk_ref, LEAVES_DEV - 1 - d)
        v = jnp.where(on_right, v0, v1)
        fs = feat_src(jnp.where(on_right, x0, x1))
        m = uses(table, first + jnp.where(on_right, d, LEAVES_DEV - 1 - d))
        for e in range(d, LEAVES_DEV):
            q0, q1 = e, LEAVES_DEV - 1 - e
            times_used = jnp.where(on_right, m[q0 : q0 + 1], m[q1 : q1 + 1])
            acc[e] = acc[e] + times(stack2(times_used * v), tile(fs, targets[e]))
    return acc


def near_kernel(nbr_ref, cnt_ref, mid_ref, skb_ref, skl_ref, near_ref, mh_ref, ml_ref):
    first = first_leaf()
    table = slots(nbr_ref, cnt_ref)
    fts = [feat_tgt(leaf(mid_ref, q)[1]) for q in range(LEAVES_DEV)]
    fs_block = feat_src(skb_ref[...])
    for q in range(LEAVES_DEV):
        col = slice(q * T, (q + 1) * T)
        ah, al = tile(fs_block, feat_tgt(skl_ref[:, col]))
        bh, bl = tile(feat_src(skl_ref[:, col]), fts[q])
        both = dg(ah, bh, 1, 0) + dg(al, bh, 1, 0) + dg(ah, bl, 1, 0)
        mh_ref[:, col], ml_ref[:, col] = split2(gain(T) * gain(T) * both)
    acc = [jnp.zeros((VEC, T), f32) for _ in range(LEAVES_DEV)]
    for j in range(LEAVES_DEV):
        v, x = leaf(mid_ref, j)
        fs = feat_src(x)
        m = uses(table, first + j)
        for q in range(LEAVES_DEV):
            vv = stack2(v if j == q else m[q : q + 1] * v)
            acc[q] = acc[q] + times(vv, tile(fs, fts[q]))
    for q in range(LEAVES_DEV):
        near_ref[:, q * T : (q + 1) * T] = gain(T) * acc[q]


def peer_kernel(
    nbr_ref, cnt_ref, part_ref, other_ref, skb_ref, sibling_ref, skg_ref, adj_ref, mid_ref, near_ref, *outs
):
    peer_ref, bh_ref, bl_ref, all_ref = outs
    table = slots(nbr_ref, cnt_ref)
    fts = [feat_tgt(leaf(mid_ref, q)[1]) for q in range(LEAVES_DEV)]
    core0 = lax.axis_index("core") == 0
    sib_near = side_near(table, sibling_ref, core0, fts)
    adj_near = side_near(table, adj_ref, jnp.logical_not(core0), fts)
    for q in range(LEAVES_DEV):
        p = LEAVES_DEV - 1 - q
        total = jnp.where(core0, sib_near[q] + adj_near[p], sib_near[p] + adj_near[q])
        col = slice(q * T, (q + 1) * T)
        all_ref[:, col] = near_ref[:, col] + gain(T) * total
    n = part_ref.shape[0]
    ft_own = feat_tgt(skb_ref[...])
    ft_sib = feat_tgt(sibling_ref[VEC + 3 : VEC + 6, :T])
    own = jnp.zeros((VEC, T), f32)
    sib = jnp.zeros((VEC, T), f32)
    for c in range(2 * n):
        w, skel = unpack((part_ref if c < n else other_ref)[c % n])
        fs = feat_src(skel)
        vv = stack2(w)
        sib = sib + times(vv, tile(fs, ft_sib))
        if c < n:
            vv = stack2(jnp.where(lax.axis_index("z8") == c, 0.0, 1.0) * w)
        own = own + times(vv, tile(fs, ft_own))
    peer_ref[0] = gain((4 * n - 1) * T) * own
    peer_ref[1] = gain((4 * n - 1) * T) * sib
    kh, kl = tile(feat_src(own_group(skg_ref)), ft_own)
    bh_ref[...] = kh
    bl_ref[...] = kl


def field_kernel(gws_ref, skg_ref, peer_ref, part_ref):
    n = gws_ref.shape[0]
    ft_own = feat_tgt(own_group(skg_ref))
    total = jnp.zeros((VEC, T), f32)
    for g in range(n):
        keep = jnp.where(lax.axis_index("grp") == g, 0.0, 1.0)
        col = slice(g * T, (g + 1) * T)
        total = total + times(stack2(keep * gws_ref[g]), tile(feat_src(skg_ref[:, col]), ft_own))
    part_ref[:VEC, :] = gain((n - 1) * T) * total
    part_ref[VEC:, :] = peer_ref[1]


def down_kernel(cell_ref, peer_ref, bh_ref, bl_ref, mh_ref, ml_ref, near_ref, out_ref):
    group = jnp.sum(cell_ref[:, :VEC, :], axis=0)
    field = gain(T) * times(stack2(group), (bh_ref[...], bl_ref[...]))
    field = field + peer_ref[0] + cell_ref[lax.axis_index("zp") * 2 + 1 - lax.axis_index("core"), VEC:, :]
    out_ref[...] = near_ref[...] + times(stack2(field), (mh_ref[...], ml_ref[...]))


VM = pl.BlockSpec(memory_space=pltpu.VMEM)
SM = pl.BlockSpec(memory_space=pltpu.SMEM)


def shape(*dims, dtype=f32):
    return jax.ShapeDtypeStruct(dims, dtype)


def cost(tiles):
    return pl.CostEstimate(flops=tiles * 10**8, bytes_accessed=tiles * 2**18, transcendentals=tiles * T * T)


def kernel(fn, name, out, scalars, arrays, scratch=(), tiles=1):
    return pl.pallas_call(
        fn,
        out_shape=out,
        in_specs=[SM] * scalars + [VM] * arrays,
        out_specs=jax.tree.map(lambda _: VM, out),
        scratch_shapes=scratch,
        cost_estimate=cost(tiles),
        compiler_params=pltpu.CompilerParams(vmem_limit_bytes=24 << 20),
        name=name,
    )


def body(points, charges, morton, neighbours, counts, skel_leaf, skel_block, skel_group):
    n_groups = lax.axis_size("grp")
    n_z8 = lax.axis_size("z8")
    n = points.shape[1]
    axes = ("grp", "z8", "zp", "core")
    counts = counts.reshape(1, LEAVES_DEV)
    inputs = (points, charges, morton.reshape(1, n), skel_leaf, skel_block)
    srt, packed = pl.pallas_call(
        up_kernel,
        out_shape=(shape(ROWS, n), shape(n_z8, PACK, HALF)),
        in_specs=[pl.BlockSpec(memory_space=pltpu.HBM)] * 5,
        out_specs=(VM, VM),
        scratch_shapes=[pltpu.VMEM(x.shape, x.dtype) for x in inputs]
        + [pltpu.VMEM((n, T), bf16), pltpu.VMEM((n, T), bf16), pltpu.SemaphoreType.DMA((5,))],
        compiler_params=pltpu.CompilerParams(vmem_limit_bytes=60 << 20),
        name="up",
    )(*inputs)
    part = lax.all_to_all(packed, "z8", 0, 0, tiled=False)
    whole = n_groups * n_z8 * 4
    swap = [(0, 1), (1, 0)]
    sib = lax.ppermute(srt, "core", swap)
    operator = shape(T, n, dtype=bf16)
    near, mh, ml = kernel(near_kernel, "near", (shape(VEC, n), operator, operator), 0, 5, tiles=28)(
        neighbours, counts, srt, skel_block, skel_leaf
    )
    srt, near, mh, ml = lax.optimization_barrier((srt, near, mh, ml))
    odd = range(1, whole - 1, 2)
    adj = lax.ppermute(srt, axes, [(i, i + 1) for i in odd] + [(i + 1, i) for i in odd])
    part, near, mh, ml = lax.optimization_barrier((part, near, mh, ml))
    other = lax.ppermute(part, "zp", swap)
    gw = kernel(group_kernel, "group", shape(n_groups, VEC, T), 0, 2, tiles=30)(part, skel_group)
    gws = lax.all_to_all(gw, "grp", 0, 0, tiled=False)
    square = shape(T, T, dtype=bf16)
    peer, bh, bl, near = kernel(peer_kernel, "peer", (shape(2, VEC, T), square, square, shape(VEC, n)), 0, 10, tiles=53)(
        neighbours, counts, part, other, skel_block, sib, skel_group, adj, srt, near
    )
    mine = kernel(field_kernel, "field", shape(2 * VEC, T), 0, 3, tiles=20)(gws, skel_group, peer)
    cell = lax.all_gather(mine, ("zp", "core"), axis=0, tiled=False)
    return kernel(down_kernel, "down", shape(VEC, n), 0, 7)(cell, peer, bh, bl, mh, ml, near)


def solution(mesh):
    fine = Mesh(mesh.devices.reshape(mesh.shape["grp"], mesh.shape["dev"] // 4, 2, 2), ("grp", "z8", "zp", "core"))
    all_axes = ("grp", "z8", "zp", "core")
    return jax.shard_map(
        body,
        mesh=fine,
        in_specs=(
            P(None, all_axes),
            P(None, all_axes),
            P(all_axes),
            P(all_axes, None),
            P(all_axes),
            P(None, all_axes),
            P(None, all_axes),
            P(),
        ),
        out_specs=P(None, all_axes),
        check_vma=False,
    )
```
